32 devices in a mesh: row: 4 (over z), col: 8 (over y, x, core).
Axes of the slice: x: 2, y: 2, z: 4, core: 2. Of those that a mesh axis runs over, the one named last changes fastest.
Arguments:
- gaussian_sketch: bfloat16 [16384, 256], P(('col', 'row')), may hold values from -6 to 6
- block_values: bfloat16 [8192, 128, 128], P(('row', 'col')), may hold values from -6 to 6
- block_rows: int32 [8192], P(('row', 'col')), may hold values from 0 to 127, as said below
- block_columns: int32 [8192], P(('row', 'col')), may hold values from 0 to 127, as said below
Outputs:
- range_basis: float32 [16384, 256], P(('row', 'col'))
- upper_factor: float32 [256, 256], replicated
The draws below stay inside these ranges and needn't reach their ends.
Inputs may be any that keep to these rules, and one draw needn't show every extreme that they name: `block_rows`: entry k * 256 + m, k = i * 8 + j, names a block row in [i * 32, (i + 1) * 32); no (row, column) pair is named twice. `block_columns`: entry k * 256 + m, k = i * 8 + j, names a block column in [j * 16, (j + 1) * 16).
All inputs are finite; a program needn't handle non-finite values.
Results may differ from the reference program's by a relative error of at most 0.0003.
Values may be sent and summed in bfloat16 or wider, within the bound.
No kernel may reach another device: no remote copies, remote signals or barrier semaphores. Data moves between devices by JAX's collectives and lax.ppermute only.
A program may use at most 128 MiB of HBM per device.

```python
import jax
import jax.numpy as jnp
from jax import lax

BS = 128
PANEL = 128
S = 256
BR_DEV = 4
NNZ_DEV = 256
RB = 32
CB = 16
NBR = 128
ORDER = 16384
NBLK = 8192


def block_pattern(key):
    slot_count = RB * CB
    device_count = NBLK // NNZ_DEV
    grid_width = RB // BR_DEV
    raw_draw = jax.random.randint(jax.random.fold_in(key, 7), (device_count, slot_count), 0, 2 ** 31 // slot_count - 1)
    scores = raw_draw * slot_count + jnp.arange(slot_count, dtype=jnp.int32)[None, :]
    ranked, chosen = lax.top_k(scores, NNZ_DEV)
    device_ids = jnp.arange(device_count, dtype=jnp.int32)[:, None]
    grid_row = device_ids // grid_width
    grid_col = device_ids % grid_width
    row_list = grid_row * RB + chosen // CB
    col_list = grid_col * CB + chosen % CB
    return (row_list.reshape(-1).astype(jnp.int32), col_list.reshape(-1).astype(jnp.int32))


def draw_block_rows(key, part):
    return block_pattern(key)[0]


def draw_block_columns(key, part):
    return block_pattern(key)[1]


def draw_block_values(key, part):
    row_list = block_pattern(key)[0]
    owner_count = NBR // BR_DEV
    order_draw = jax.random.permutation(jax.random.fold_in(key, 13), owner_count)
    exponent = order_draw.astype(jnp.float32) / max(owner_count - 1, 1)
    owner_scale = jnp.exp(exponent * jnp.log(16.0))
    row_scale = owner_scale[row_list // BR_DEV]
    raw_values = jnp.clip(jax.random.normal(jax.random.fold_in(key, 11), (NBLK, BS, BS), jnp.float32), -6.0, 6.0)
    fan_scale = (BS * NNZ_DEV // BR_DEV) ** (-0.5)
    values = raw_values * fan_scale * row_scale[:, None, None]
    return values.astype(jnp.bfloat16)


def shard_levels(rng, dims, shards, low, high):
    factor_of = 1.0
    for dim, parts in shards:
        draws = jax.random.uniform(jax.random.fold_in(jax.random.fold_in(rng, 6), dim), (parts,), jnp.float32, low / len(shards), high / len(shards))
        factor_of = factor_of * jnp.repeat(jnp.exp(draws), dims[dim] // parts).reshape((-1,) + (1,) * (len(dims) - 1 - dim))
    return factor_of


def gaussian(stream_key, shape, scale, most, shards=(), kind=jnp.bfloat16):
    values = scale * jax.random.normal(stream_key, shape, jnp.float32)
    if shards:
        values = values * shard_levels(stream_key, shape, shards, -0.22, 0.18)
    return jnp.clip(values, -most, most).astype(kind)


def setup_inputs(seed: int = 0) -> dict:
    keys = jax.random.split(jax.random.key(seed), 5)
    return {
        "gaussian_sketch": gaussian(keys[0], (ORDER, S), 1.0, 6.0, ((0, 32),)),
        "block_values": draw_block_values(jax.random.fold_in(keys[4], 71), 0),
        "block_rows": draw_block_rows(jax.random.fold_in(keys[4], 71), 0),
        "block_columns": draw_block_columns(jax.random.fold_in(keys[4], 71), 0),
    }


def upper_parts(gram):
    lower_factor = jnp.linalg.cholesky(gram)
    identity = jnp.eye(gram.shape[0], dtype=gram.dtype)
    inverse = lax.linalg.triangular_solve(lower_factor, identity, left_side=True, lower=True)
    return (lower_factor.T, inverse.T)

def sketch_product(gaussian_sketch, block_values, block_rows, block_columns):
    sketch_blocks = gaussian_sketch.astype(jnp.float32).reshape(NBR, BS, S)
    group_count = NBLK // NNZ_DEV

    def advance(counter, summed):
        offset = (counter * NNZ_DEV).astype(jnp.int32)
        values = lax.dynamic_slice_in_dim(block_values, offset, NNZ_DEV, 0).astype(jnp.float32)
        row_ids = lax.dynamic_slice_in_dim(block_rows, offset, NNZ_DEV, 0).astype(jnp.int32)
        col_ids = lax.dynamic_slice_in_dim(block_columns, offset, NNZ_DEV, 0).astype(jnp.int32)
        picked = jnp.take(sketch_blocks, col_ids, axis=0)
        product = jnp.einsum('gab,gbs->gas', values, picked, precision=lax.Precision.HIGHEST)
        return summed.at[row_ids].add(product)
    initial = jnp.zeros((NBR, BS, S), jnp.float32)
    summed = lax.fori_loop(0, group_count, advance, initial)
    return summed.reshape(ORDER, S)

def reference(gaussian_sketch, block_values, block_rows, block_columns):
    high = lax.Precision.HIGHEST
    sketched = sketch_product(gaussian_sketch, block_values, block_rows, block_columns)
    first_part = sketched[:, :PANEL]
    second_part = sketched[:, PANEL:]
    gram_one = jnp.dot(first_part.T, first_part, precision=high) / ORDER
    upper_one, inverse_one = upper_parts(gram_one)
    basis_one = jnp.dot(first_part, inverse_one, precision=high)
    coupling = jnp.dot(basis_one.T, second_part, precision=high) / ORDER
    remainder = second_part - jnp.dot(basis_one, coupling, precision=high)
    gram_two = jnp.dot(remainder.T, remainder, precision=high) / ORDER
    upper_two, inverse_two = upper_parts(gram_two)
    basis_two = jnp.dot(remainder, inverse_two, precision=high)
    range_basis = jnp.concatenate([basis_one, basis_two], axis=1)
    top_rows = jnp.concatenate([upper_one, coupling], axis=1)
    bottom_rows = jnp.concatenate([jnp.zeros_like(upper_two), upper_two], axis=1)
    upper_factor = jnp.concatenate([top_rows, bottom_rows], axis=0)
    return (range_basis, upper_factor)
```

```python
import functools
import math

import jax
import jax.numpy as jnp
from jax import lax
from jax.experimental import pallas as pl
from jax.experimental.pallas import tpu as pltpu
from jax.sharding import PartitionSpec as P

PANEL = 128
BS = 128
LEVELS = 32700.0
OCTAVE = 64.0
DENSE_BYTES = 32 * 2**20


def upper_parts(gram):
    lower_factor = jnp.linalg.cholesky(gram)
    identity = jnp.eye(gram.shape[0], dtype=gram.dtype)
    inverse = lax.linalg.triangular_solve(lower_factor, identity, left_side=True, lower=True)
    return (lower_factor.T, inverse.T)


def exchange(value, axis, mask):
    size = lax.axis_size(axis)
    return lax.ppermute(value, axis, [(i, i ^ mask) for i in range(size)])


def scatter_kernel(slots, values, dense, zeros, taken, sem):
    n_slots = dense.shape[0]
    n_blocks = values.shape[0]
    zeros[...] = jnp.zeros_like(zeros)

    @pl.loop(0, n_slots)
    def _(s):
        taken[s] = 0

    @pl.loop(0, n_blocks)
    def _(b):
        slot = slots[b]
        taken[slot] = 1
        pltpu.make_async_copy(values.at[b], dense.at[slot], sem).start()

    @pl.loop(0, n_slots)
    def _(s):
        @pl.when(taken[s] == 0)
        def _():
            pltpu.make_async_copy(zeros, dense.at[s], sem).start()

    pltpu.make_async_copy(dense, dense, sem).wait()


def scatter_blocks(slots, values, n_slots):
    return pl.pallas_call(
        scatter_kernel,
        out_shape=jax.ShapeDtypeStruct((n_slots, BS, BS), values.dtype),
        grid_spec=pltpu.PrefetchScalarGridSpec(
            num_scalar_prefetch=1,
            grid=(),
            in_specs=[pl.BlockSpec(memory_space=pl.ANY)],
            out_specs=pl.BlockSpec(memory_space=pl.ANY),
            scratch_shapes=[
                pltpu.VMEM((BS, BS), values.dtype),
                pltpu.SMEM((n_slots,), jnp.int32),
                pltpu.SemaphoreType.DMA,
            ],
        ),
        compiler_params=pltpu.CompilerParams(vmem_limit_bytes=8 * 2**20),
        cost_estimate=pl.CostEstimate(flops=0, bytes_accessed=48 * 2**20, transcendentals=0),
    )(slots, values)


def dense_dot(a_ref, x_ref):
    rows, cols = a_ref.shape[:2]
    lhs = jnp.concatenate(
        [jnp.concatenate([a_ref[r, c] for c in range(cols)], axis=1) for r in range(rows)], axis=0
    )
    return jnp.dot(lhs, x_ref[...], preferred_element_type=jnp.float32)


def far_kernel(a_ref, x_ref, o_ref):
    o_ref[0] = dense_dot(a_ref, x_ref)


def quantize(total, o_ref):
    n = total.shape[0] // BS
    width = total.shape[1]
    row = lax.broadcasted_iota(jnp.int32, (16, width), 0)
    tail = jnp.zeros((16, width), jnp.float32)
    for b in range(n):
        part = total[b * BS : (b + 1) * BS]
        top = jnp.maximum(jnp.max(jnp.abs(part), axis=0, keepdims=True), 1e-30)
        step = jnp.ceil(jnp.log(top) * (OCTAVE / math.log(2.0)))
        scaled = part * (jnp.exp(step * (-math.log(2.0) / OCTAVE)) * LEVELS)
        o_ref[b * BS : (b + 1) * BS, :] = jnp.round(scaled).astype(jnp.int32).astype(jnp.int16)
        tail = jnp.where(row == b, jnp.broadcast_to(step, tail.shape), tail)
    o_ref[n * BS :, :] = tail.astype(jnp.int32).astype(jnp.int16)


def dequantize(q_ref):
    n = (q_ref.shape[0] - 16) // BS
    tail = q_ref[n * BS :, :].astype(jnp.int32).astype(jnp.float32)
    parts = []
    for b in range(n):
        scale = jnp.exp(tail[b : b + 1] * (math.log(2.0) / OCTAVE)) * (1.0 / LEVELS)
        parts.append(q_ref[b * BS : (b + 1) * BS, :].astype(jnp.int32).astype(jnp.float32) * scale)
    return jnp.concatenate(parts, axis=0)


def send_kernel(a_ref, x_ref, r_ref, *o_refs):
    total = dense_dot(a_ref, x_ref) + r_ref[0]
    for i, o_ref in enumerate(o_refs):

        @pl.when(pl.program_id(0) == i)
        def _(o_ref=o_ref):
            quantize(total, o_ref)


def own_kernel(a_ref, x_ref, r_ref, o_ref):
    o_ref[...] = dense_dot(a_ref, x_ref) + r_ref[0]


def reduce_kernel(core, own_ref, *refs):
    *q_refs, s_ref, mine_ref, other_ref, pack = refs
    total = own_ref[...]
    for q_ref in q_refs:
        total = total + dequantize(q_ref)
    s_ref[...] = total
    gram_store(total, pack)
    half = pack.shape[0] // 2
    c = core[0]
    mine_ref[...] = pack[pl.ds(pl.multiple_of(c * half, 8), half), :]
    other_ref[...] = pack[pl.ds(pl.multiple_of((1 - c) * half, 8), half), :]


def gram_store(total, pack):
    high = total.astype(jnp.bfloat16)
    low = (total - high.astype(jnp.float32)).astype(jnp.bfloat16)
    dims = (((0,), (0,)), ((), ()))
    dot = functools.partial(lax.dot_general, dimension_numbers=dims, preferred_element_type=jnp.float32)
    cross = dot(high, low)
    gram = dot(high, high) + dot(low, low) + cross + cross.T
    pack[0:PANEL, :] = gram[:PANEL, :PANEL]
    pack[PANEL : 2 * PANEL, :] = gram[:PANEL, PANEL:]
    pack[2 * PANEL : 3 * PANEL, :] = gram[PANEL:, PANEL:]


def whole(shape):
    return pl.BlockSpec(shape, lambda *_: (0,) * len(shape))


def dense_sketch(gaussian_sketch, block_values, local_rows, local_cols, grid_rows, grid_cols):
    size_col = lax.axis_size("col")
    chips = size_col // 2
    shard_rows, width = gaussian_sketch.shape
    group = shard_rows // BS
    me = lax.axis_index("col")
    owner = local_rows // group
    peer_core = (owner + me) % 2
    near = (owner // 2) ^ (me // 2)
    place = ((1 - peer_core) * chips + near) * group + local_rows % group
    slots = place * grid_cols + local_cols
    dense = scatter_blocks(slots, block_values, grid_rows * grid_cols)
    dense = dense.reshape(2 * chips * group, grid_cols, BS, BS)
    sketch = lax.all_gather(gaussian_sketch, "row", axis=0, tiled=True)

    params = pltpu.CompilerParams(vmem_limit_bytes=32 * 2**20)
    flops = 2 * shard_rows * grid_cols * BS * width
    bytes_a = 2 * shard_rows * grid_cols * BS

    def cost(n):
        return pl.CostEstimate(flops=n * flops, bytes_accessed=n * bytes_a, transcendentals=0)

    def a_spec(first):
        return pl.BlockSpec((group, grid_cols, BS, BS), lambda i: (i + first, 0, 0, 0))

    x_spec = whole(sketch.shape)
    r_block = (1, shard_rows, width)
    far = pl.pallas_call(
        far_kernel,
        grid=(chips,),
        in_specs=[a_spec(0), x_spec],
        out_specs=pl.BlockSpec(r_block, lambda i: (i, 0, 0)),
        out_shape=jax.ShapeDtypeStruct((chips, shard_rows, width), jnp.float32),
        compiler_params=params,
        cost_estimate=cost(chips),
    )(dense, sketch)
    near_sum = exchange(far, "col", 1)
    sent = jax.ShapeDtypeStruct((shard_rows + 16, width), jnp.int16)
    coded = pl.pallas_call(
        send_kernel,
        grid=(chips - 1,),
        in_specs=[a_spec(chips + 1), x_spec, pl.BlockSpec(r_block, lambda i: (i + 1, 0, 0))],
        out_specs=[whole(sent.shape)] * (chips - 1),
        out_shape=[sent] * (chips - 1),
        compiler_params=params,
        cost_estimate=cost(chips - 1),
    )(dense, sketch, near_sum)
    got = [exchange(q, "col", 2 * (i + 1)) for i, q in enumerate(coded)]
    own = pl.pallas_call(
        own_kernel,
        grid=(1,),
        in_specs=[a_spec(chips), x_spec, pl.BlockSpec(r_block, lambda i: (0, 0, 0))],
        out_specs=whole((shard_rows, width)),
        out_shape=jax.ShapeDtypeStruct((shard_rows, width), jnp.float32),
        compiler_params=params,
        cost_estimate=cost(1),
    )(dense, sketch, near_sum)
    return own, got


def tile_product(sketch_blocks, block_values, local_rows, local_cols, tile_rows):
    group_size = math.gcd(block_values.shape[0], 64)
    col_width = sketch_blocks.shape[2]

    def advance(counter, summed):
        offset = (counter * group_size).astype(jnp.int32)
        values = lax.dynamic_slice_in_dim(block_values, offset, group_size, 0)
        row_ids = lax.dynamic_slice_in_dim(local_rows, offset, group_size, 0)
        col_ids = lax.dynamic_slice_in_dim(local_cols, offset, group_size, 0)
        picked = jnp.take(sketch_blocks, col_ids, axis=0)
        product = jnp.einsum("gab,gbs->gas", values, picked, preferred_element_type=jnp.float32)
        return summed.at[row_ids].add(product)

    initial = jnp.zeros((tile_rows, block_values.shape[1], col_width), jnp.float32)
    summed = lax.fori_loop(0, block_values.shape[0] // group_size, advance, initial)
    return summed.reshape(tile_rows * block_values.shape[1], col_width)


def looped_sketch(gaussian_sketch, block_values, local_rows, local_cols, grid_rows, grid_cols):
    gathered = lax.all_gather(gaussian_sketch, "row", axis=0, tiled=True)
    sketch_blocks = gathered.reshape(grid_cols, BS, gathered.shape[1])
    partial_value = tile_product(sketch_blocks, block_values, local_rows, local_cols, grid_rows)
    return lax.psum_scatter(partial_value, "col", scatter_dimension=0, tiled=True), []


def direct_sum(value, axis, low_bit, bits):
    total = value
    for mask in range(1, 2**bits):
        total = total + exchange(value, axis, mask << low_bit)
    return total


def sum_over_axis(value, axis, low_bit):
    bits = lax.axis_size(axis).bit_length() - 1
    while low_bit < bits:
        take = min(2, bits - low_bit)
        value = direct_sum(value, axis, low_bit, take)
        low_bit += take
    return value


def sum_over_mesh(mine, other, core):
    mine = mine + exchange(other, "col", 1)
    mine = sum_over_axis(mine, "col", 1)
    mine = sum_over_axis(mine, "row", 0)
    other = exchange(mine, "col", 1)
    first = core == 0
    return jnp.concatenate([jnp.where(first, mine, other), jnp.where(first, other, mine)], axis=0)


def on_device(gaussian_sketch, block_values, block_rows, block_columns):
    high = lax.Precision.HIGHEST
    size_row = lax.axis_size("row")
    size_col = lax.axis_size("col")
    shard_rows, width = gaussian_sketch.shape
    grid_rows = shard_rows * size_col // BS
    grid_cols = shard_rows * size_row // BS
    local_rows = block_rows - lax.axis_index("row") * grid_rows
    local_cols = block_columns - lax.axis_index("col") * grid_cols
    dense = 2 * grid_rows * grid_cols * BS * BS <= DENSE_BYTES
    sketch = dense_sketch if dense else looped_sketch
    own, got = sketch(
        gaussian_sketch, block_values, local_rows, local_cols, grid_rows, grid_cols
    )
    core = lax.axis_index("col") % 2
    half = jax.ShapeDtypeStruct((3 * PANEL // 2, PANEL), jnp.float32)
    sketched, mine, other = pl.pallas_call(
        reduce_kernel,
        grid_spec=pltpu.PrefetchScalarGridSpec(
            num_scalar_prefetch=1,
            grid=(1,),
            in_specs=[whole(own.shape)] + [whole(q.shape) for q in got],
            out_specs=[whole(own.shape), whole(half.shape), whole(half.shape)],
            scratch_shapes=[pltpu.VMEM((3 * PANEL, PANEL), jnp.float32)],
        ),
        out_shape=[jax.ShapeDtypeStruct(own.shape, jnp.float32), half, half],
        compiler_params=pltpu.CompilerParams(vmem_limit_bytes=32 * 2**20),
    )(core.reshape(1), own, *got)
    order_total = shard_rows * size_row * size_col
    gram = sum_over_mesh(mine, other, core) / order_total
    upper_one, inverse_one = upper_parts(gram[:PANEL])
    coupling = jnp.dot(inverse_one.T, gram[PANEL : 2 * PANEL], precision=high)
    gram_two = gram[2 * PANEL :] - jnp.dot(coupling.T, coupling, precision=high)
    upper_two, inverse_two = upper_parts(gram_two)
    mixed = -jnp.dot(inverse_one, jnp.dot(coupling, inverse_two, precision=high), precision=high)
    zero = jnp.zeros_like(upper_two)
    inverse = jnp.block([[inverse_one, mixed], [zero, inverse_two]])
    range_basis = jnp.dot(sketched, inverse, precision=high)
    upper_factor = jnp.block([[upper_one, coupling], [zero, upper_two]])
    return (range_basis, upper_factor)


def solution(mesh):
    return jax.shard_map(
        on_device,
        mesh=mesh,
        in_specs=(
            P(("col", "row"), None),
            P(("row", "col"), None, None),
            P(("row", "col")),
            P(("row", "col")),
        ),
        out_specs=(P(("row", "col"), None), P()),
        check_vma=False,
    )
```

```python
import functools
import math

import jax
import jax.numpy as jnp
from jax import lax
from jax.experimental import pallas as pl
from jax.experimental.pallas import tpu as pltpu
from jax.sharding import PartitionSpec as P

PANEL = 128
BS = 128
LEVELS = 32700.0
OCTAVE = 64.0
DENSE_BYTES = 32 * 2**20
STEP = 4


def exchange(value, axis, mask):
    size = lax.axis_size(axis)
    return lax.ppermute(value, axis, [(i, i ^ mask) for i in range(size)])


def scatter_kernel(slots, values, dense, sem):
    n_slots = dense.shape[0]
    n_blocks = values.shape[0]

    @pl.loop(0, n_slots)
    def _(s):
        dense[s] = jnp.zeros(dense.shape[1:], dense.dtype)

    @pl.loop(0, n_blocks)
    def _(b):
        pltpu.make_async_copy(values.at[b], dense.at[slots[b]], sem).start()

    pltpu.make_async_copy(values, values, sem).wait()


def scatter_blocks(slots, values, n_slots):
    return pl.pallas_call(
        scatter_kernel,
        out_shape=pltpu.VMEM((n_slots, BS, BS), values.dtype),
        grid_spec=pltpu.PrefetchScalarGridSpec(
            num_scalar_prefetch=1,
            grid=(),
            in_specs=[pl.BlockSpec(memory_space=pltpu.HBM)],
            out_specs=pl.BlockSpec(memory_space=pltpu.VMEM),
            scratch_shapes=[pltpu.SemaphoreType.DMA],
        ),
        compiler_params=pltpu.CompilerParams(vmem_limit_bytes=4 * 2**20),
        cost_estimate=pl.CostEstimate(flops=0, bytes_accessed=24 * 2**20, transcendentals=0),
    )(slots, pltpu.with_memory_space_constraint(values, pltpu.HBM))


def dense_dot(a_ref, x_refs, chunk):
    group = a_ref.shape[1]
    span = a_ref.shape[2] // len(x_refs)
    total = None
    for k, x_ref in enumerate(x_refs):
        lhs = jnp.concatenate(
            [
                jnp.concatenate([a_ref[chunk, r, k * span + c] for c in range(span)], axis=1)
                for r in range(group)
            ],
            axis=0,
        )
        part = jnp.dot(lhs, x_ref[...], preferred_element_type=jnp.float32)
        total = part if total is None else total + part
    return total


def product_kernel(first, a_ref, *refs):
    *x_refs, o_ref = refs
    o_ref[0] = dense_dot(a_ref, x_refs, pl.program_id(0) + first)


def quantize(total, o_ref):
    n = total.shape[0] // BS
    width = total.shape[1]
    row = lax.broadcasted_iota(jnp.int32, (16, width), 0)
    tail = jnp.zeros((16, width), jnp.float32)
    for b in range(n):
        part = total[b * BS : (b + 1) * BS]
        top = jnp.maximum(jnp.max(jnp.abs(part), axis=0, keepdims=True), 1e-30)
        step = jnp.ceil(jnp.log(top) * (OCTAVE / math.log(2.0)))
        scaled = part * (jnp.exp(step * (-math.log(2.0) / OCTAVE)) * LEVELS)
        o_ref[b * BS : (b + 1) * BS, :] = jnp.round(scaled).astype(jnp.int32).astype(jnp.int16)
        tail = jnp.where(row == b, jnp.broadcast_to(step, tail.shape), tail)
    o_ref[n * BS :, :] = tail.astype(jnp.int32).astype(jnp.int16)


def dequantize(q_ref):
    n = (q_ref.shape[0] - 16) // BS
    tail = q_ref[n * BS :, :].astype(jnp.int32).astype(jnp.float32)
    parts = []
    for b in range(n):
        scale = jnp.exp(tail[b : b + 1] * (math.log(2.0) / OCTAVE)) * (1.0 / LEVELS)
        parts.append(q_ref[b * BS : (b + 1) * BS, :].astype(jnp.int32).astype(jnp.float32) * scale)
    return jnp.concatenate(parts, axis=0)


def code_kernel(a_ref, b_ref, own_ref, *o_refs):
    total = a_ref[0] + b_ref[0]
    i = pl.program_id(0)
    for j, o_ref in enumerate(o_refs):

        @pl.when(i == j)
        def _(o_ref=o_ref):
            quantize(total, o_ref)

    @pl.when(i == len(o_refs))
    def _():
        own_ref[...] = total


def reduce_kernel(core, *refs):
    *in_refs, s_ref, mine_ref, other_ref, pack = refs
    total = None
    for ref in in_refs:
        term = dequantize(ref) if ref.dtype == jnp.int16 else ref[...]
        total = term if total is None else total + term
    s_ref[...] = total
    gram_store(total, pack)
    half = pack.shape[0] // 2
    c = core[0]
    mine_ref[...] = pack[pl.ds(pl.multiple_of(c * half, 8), half), :]
    other_ref[...] = pack[pl.ds(pl.multiple_of((1 - c) * half, 8), half), :]


def gram_store(total, pack):
    high = total.astype(jnp.bfloat16)
    low = (total - high.astype(jnp.float32)).astype(jnp.bfloat16)
    dims = (((0,), (0,)), ((), ()))
    dot = functools.partial(lax.dot_general, dimension_numbers=dims, preferred_element_type=jnp.float32)
    cross = dot(high, low)
    gram = dot(high, high) + dot(low, low) + cross + cross.T
    pack[0:PANEL, :] = gram[:PANEL, :PANEL]
    pack[PANEL : 2 * PANEL, :] = gram[:PANEL, PANEL:]
    pack[2 * PANEL : 3 * PANEL, :] = gram[PANEL:, PANEL:]


def split(x, terms):
    out = []
    for _ in range(terms):
        part = x.astype(jnp.bfloat16)
        out.append(part)
        x = x - part.astype(jnp.float32)
    return out


PAIRS = ((0, 0), (0, 1), (1, 0), (1, 1), (0, 2), (2, 0))


def factor(gram):
    n = gram.shape[0]
    sub = lax.broadcasted_iota(jnp.int32, (8, n), 0)
    lane = lax.broadcasted_iota(jnp.int32, (8, n), 1)
    left = [gram[8 * i : 8 * i + 8] for i in range(n // 8)]
    right = [(lane == sub + 8 * i).astype(jnp.float32) for i in range(n // 8)]

    def row(x, k):
        return jnp.broadcast_to(x[k : k + 1], x.shape)

    for first in range(0, n // 8, STEP):
        last = first + STEP
        for b in range(first, last):
            cols = {
                t: [jnp.broadcast_to(left[t][:, 8 * b + k : 8 * b + k + 1], (8, n)) for k in range(8)]
                for t in range(b, last)
            }
            for k in range(8):
                pivot = row(cols[b][k], k)
                root = lax.rsqrt(pivot)
                root = root * (1.5 - 0.5 * pivot * root * root)
                mult = {t: cols[t][k] * root for t in range(b, last)}
                for j in range(k + 1, 8):
                    other = row(mult[b], j)
                    for t in range(b, last):
                        cols[t][j] = cols[t][j] - mult[t] * other
                top_left, top_right = row(left[b], k) * root, row(right[b], k) * root
                below = jnp.where(sub > k, mult[b], 0.0)
                left[b] = jnp.where(sub == k, top_left, left[b] - below * top_left)
                right[b] = jnp.where(sub == k, top_right, right[b] - below * top_right)
                for t in range(b + 1, last):
                    left[t] = left[t] - mult[t] * top_left
                    right[t] = right[t] - mult[t] * top_right
        if last < n // 8:
            u = split(jnp.concatenate(left[first:last], axis=0), 3)
            v = split(jnp.concatenate(right[first:last], axis=0), 3)
            lhs = jnp.concatenate([u[i] for i, _ in PAIRS], axis=0)
            rhs = jnp.concatenate(
                [jnp.concatenate([u[j] for _, j in PAIRS], axis=0), jnp.concatenate([v[j] for _, j in PAIRS], axis=0)],
                axis=1,
            )
            change = lax.dot_general(lhs, rhs, (((0,), (0,)), ((), ())), preferred_element_type=jnp.float32)
            for t in range(last, n // 8):
                left[t] = left[t] - change[8 * t : 8 * t + 8, :n]
                right[t] = right[t] - change[8 * t : 8 * t + 8, n:]
    upper = jnp.concatenate([jnp.where(lane >= sub + 8 * i, x, 0.0) for i, x in enumerate(left)], axis=0)
    return upper, jnp.concatenate(right, axis=0)


def dot3(a, b, dims):
    (ah, al), (bh, bl) = split(a, 2), split(b, 2)
    dot = functools.partial(
        lax.dot_general, dimension_numbers=(dims, ((), ())), preferred_element_type=jnp.float32
    )
    return dot(ah, bh) + (dot(ah, bl) + dot(al, bh))


def full_dot(a, b, dims):
    return lax.dot_general(
        a, b, (dims, ((), ())), precision=lax.Precision.HIGHEST, preferred_element_type=jnp.float32
    )


NN, NT, TN = ((1,), (0,)), ((1,), (1,)), ((0,), (0,))


def tail_kernel(scale, core, mine_ref, other_ref, s_ref, basis_ref, upper_ref, pack):
    half = pack.shape[0] // 2
    c = core[0]
    pack[pl.ds(pl.multiple_of(c * half, 8), half), :] = mine_ref[...] * scale
    pack[pl.ds(pl.multiple_of((1 - c) * half, 8), half), :] = other_ref[...] * scale
    gram_one, cross, gram_two = (pack[i * PANEL : (i + 1) * PANEL, :] for i in range(3))
    upper_one, low_one = factor(gram_one)
    coupling = full_dot(low_one, cross, NN)
    upper_two, low_two = factor(gram_two - full_dot(coupling, coupling, TN))
    mixed = -full_dot(low_two, full_dot(coupling, low_one, TN), NN)
    zero = jnp.zeros_like(upper_one)
    upper_ref[0:PANEL, 0:PANEL] = upper_one
    upper_ref[0:PANEL, PANEL:] = coupling
    upper_ref[PANEL:, 0:PANEL] = zero
    upper_ref[PANEL:, PANEL:] = upper_two
    first, second = s_ref[:, 0:PANEL], s_ref[...]
    basis_ref[:, 0:PANEL] = dot3(first, low_one, NT)
    basis_ref[:, PANEL:] = dot3(second, jnp.concatenate([mixed, low_two], axis=1), NT)


def whole(shape):
    return pl.BlockSpec(shape, lambda *_: (0,) * len(shape))


def gather_row(value):
    bits = lax.axis_size("row").bit_length() - 1
    shards = [value]
    for bit in reversed(range(bits)):
        shards = shards + [exchange(v, "row", 1 << bit) for v in shards]
    order = [0]
    for bit in reversed(range(bits)):
        order = order + [k | 1 << bit for k in order]
    return [shards[order.index(k)] for k in range(2**bits)]


def dense_sketch(gaussian_sketch, block_values, local_rows, local_cols, grid_rows, grid_cols):
    size_col = lax.axis_size("col")
    chips = size_col // 2
    shard_rows, width = gaussian_sketch.shape
    group = shard_rows // BS
    me = lax.axis_index("col")
    owner = local_rows // group
    peer_core = (owner + me) % 2
    near = (owner // 2) ^ (me // 2)
    place = ((1 - peer_core) * chips + near) * group + local_rows % group
    shard = (local_cols // group) ^ lax.axis_index("row")
    slots = place * grid_cols + shard * group + local_cols % group
    dense = scatter_blocks(slots, block_values, grid_rows * grid_cols)
    dense = dense.reshape(2 * chips, group, grid_cols, BS, BS)
    shards = gather_row(gaussian_sketch)
    n = len(shards)

    params = pltpu.CompilerParams(vmem_limit_bytes=12 * 2**20)
    flops = 2 * shard_rows * grid_cols * BS * width
    bytes_a = 2 * shard_rows * grid_cols * BS

    def cost(n):
        return pl.CostEstimate(flops=n * flops, bytes_accessed=n * bytes_a, transcendentals=0)

    held = pl.BlockSpec(memory_space=pltpu.VMEM)
    r_block = (1, shard_rows, width)
    def product(first):
        return pl.pallas_call(
            functools.partial(product_kernel, first),
            grid=(chips,),
            in_specs=[held] * (n + 1),
            out_specs=pl.BlockSpec(r_block, lambda i: (i, 0, 0)),
            out_shape=jax.ShapeDtypeStruct((chips, shard_rows, width), jnp.float32),
            compiler_params=params,
            cost_estimate=cost(chips),
        )(dense, *shards)

    peer_sum = exchange(product(0), "col", 1)
    near_sum = product(chips)
    sent = jax.ShapeDtypeStruct((shard_rows + 16, width), jnp.int16)
    own_last = pl.BlockSpec(r_block, lambda i: ((i + 1) % chips, 0, 0))
    own_shape = (shard_rows, width)
    own, *coded = pl.pallas_call(
        code_kernel,
        grid=(chips,),
        in_specs=[own_last, own_last],
        out_specs=[whole(own_shape)] + [whole(sent.shape)] * (chips - 1),
        out_shape=[jax.ShapeDtypeStruct(own_shape, jnp.float32)] + [sent] * (chips - 1),
        compiler_params=params,
    )(near_sum, peer_sum)
    return [own] + [exchange(q, "col", 2 * (i + 1)) for i, q in enumerate(coded)]


def tile_product(sketch_blocks, block_values, local_rows, local_cols, tile_rows):
    group_size = math.gcd(block_values.shape[0], 64)
    col_width = sketch_blocks.shape[2]

    def advance(counter, summed):
        offset = (counter * group_size).astype(jnp.int32)
        values = lax.dynamic_slice_in_dim(block_values, offset, group_size, 0)
        row_ids = lax.dynamic_slice_in_dim(local_rows, offset, group_size, 0)
        col_ids = lax.dynamic_slice_in_dim(local_cols, offset, group_size, 0)
        picked = jnp.take(sketch_blocks, col_ids, axis=0)
        product = jnp.einsum("gab,gbs->gas", values, picked, preferred_element_type=jnp.float32)
        return summed.at[row_ids].add(product)

    initial = jnp.zeros((tile_rows, block_values.shape[1], col_width), jnp.float32)
    summed = lax.fori_loop(0, block_values.shape[0] // group_size, advance, initial)
    return summed.reshape(tile_rows * block_values.shape[1], col_width)


def looped_sketch(gaussian_sketch, block_values, local_rows, local_cols, grid_rows, grid_cols):
    gathered = lax.all_gather(gaussian_sketch, "row", axis=0, tiled=True)
    sketch_blocks = gathered.reshape(grid_cols, BS, gathered.shape[1])
    partial_value = tile_product(sketch_blocks, block_values, local_rows, local_cols, grid_rows)
    return [lax.psum_scatter(partial_value, "col", scatter_dimension=0, tiled=True)]


def direct_sum(value, axis, low_bit, bits):
    terms = [value] + [exchange(value, axis, mask << low_bit) for mask in range(1, 2**bits)]
    while len(terms) > 1:
        terms = [a + b for a, b in zip(terms[0::2], terms[1::2])]
    return terms[0]


def sum_over_axis(value, axis, low_bit):
    bits = lax.axis_size(axis).bit_length() - 1
    while low_bit < bits:
        take = min(2, bits - low_bit)
        value = direct_sum(value, axis, low_bit, take)
        low_bit += take
    return value


def sum_over_mesh(mine, other, core):
    mine = mine + exchange(other, "col", 1)
    mine = sum_over_axis(mine, "col", 1)
    mine = sum_over_axis(mine, "row", 0)
    return mine, exchange(mine, "col", 1)


def on_device(gaussian_sketch, block_values, block_rows, block_columns):
    size_row = lax.axis_size("row")
    size_col = lax.axis_size("col")
    shard_rows, width = gaussian_sketch.shape
    grid_rows = shard_rows * size_col // BS
    grid_cols = shard_rows * size_row // BS
    local_rows = block_rows - lax.axis_index("row") * grid_rows
    local_cols = block_columns - lax.axis_index("col") * grid_cols
    dense = 2 * grid_rows * grid_cols * BS * BS <= DENSE_BYTES
    sketch = dense_sketch if dense else looped_sketch
    terms = sketch(
        gaussian_sketch, block_values, local_rows, local_cols, grid_rows, grid_cols
    )
    core = lax.axis_index("col") % 2
    half = jax.ShapeDtypeStruct((3 * PANEL // 2, PANEL), jnp.float32)
    sketched, mine, other = pl.pallas_call(
        reduce_kernel,
        grid_spec=pltpu.PrefetchScalarGridSpec(
            num_scalar_prefetch=1,
            grid=(1,),
            in_specs=[whole(t.shape) for t in terms],
            out_specs=[whole((shard_rows, width)), whole(half.shape), whole(half.shape)],
            scratch_shapes=[pltpu.VMEM((3 * PANEL, PANEL), jnp.float32)],
        ),
        out_shape=[jax.ShapeDtypeStruct((shard_rows, width), jnp.float32), half, half],
        compiler_params=pltpu.CompilerParams(vmem_limit_bytes=12 * 2**20),
    )(core.reshape(1), *terms)
    order_total = shard_rows * size_row * size_col
    mine, other = sum_over_mesh(mine, other, core)
    range_basis, upper_factor = pl.pallas_call(
        functools.partial(tail_kernel, 1.0 / order_total),
        grid_spec=pltpu.PrefetchScalarGridSpec(
            num_scalar_prefetch=1,
            grid=(1,),
            in_specs=[whole(half.shape), whole(half.shape), whole(sketched.shape)],
            out_specs=[whole(sketched.shape), whole((width, width))],
            scratch_shapes=[pltpu.VMEM((3 * PANEL, PANEL), jnp.float32)],
        ),
        out_shape=[
            jax.ShapeDtypeStruct(sketched.shape, jnp.float32),
            jax.ShapeDtypeStruct((width, width), jnp.float32),
        ],
        compiler_params=pltpu.CompilerParams(vmem_limit_bytes=16 * 2**20),
    )(core.reshape(1), mine, other, sketched)
    return (range_basis, upper_factor)


def solution(mesh):
    return jax.shard_map(
        on_device,
        mesh=mesh,
        in_specs=(
            P(("col", "row"), None),
            P(("row", "col"), None, None),
            P(("row", "col")),
            P(("row", "col")),
        ),
        out_specs=(P(("row", "col"), None), P()),
        check_vma=False,
    )
```

```python
import functools
import math

import jax
import jax.numpy as jnp
from jax import lax
from jax.experimental import pallas as pl
from jax.experimental.pallas import tpu as pltpu
from jax.sharding import PartitionSpec as P

PANEL = 128
BS = 128
LEVELS = 32700.0
OCTAVE = 64.0
DENSE_BYTES = 32 * 2**20
STEP = 4
PACK = 2 * PANEL + 16


def exchange(value, axis, mask):
    size = lax.axis_size(axis)
    return lax.ppermute(value, axis, [(i, i ^ mask) for i in range(size)])


def scatter_kernel(slots, values, dense, taken, sem):
    n_slots = dense.shape[0]
    n_blocks = values.shape[0]

    @pl.loop(0, n_slots)
    def _(s):
        taken[s] = 0

    @pl.loop(0, n_blocks)
    def _(b):
        slot = slots[b]
        taken[slot] = 1
        pltpu.make_async_copy(values.at[b], dense.at[slot], sem).start()

    @pl.loop(0, n_slots)
    def _(s):
        @pl.when(taken[s] == 0)
        def _():
            dense[s] = jnp.zeros(dense.shape[1:], dense.dtype)

    pltpu.make_async_copy(values, values, sem).wait()


def scatter_blocks(slots, values, n_slots):
    return pl.pallas_call(
        scatter_kernel,
        out_shape=pltpu.VMEM((n_slots, BS, BS), values.dtype),
        grid_spec=pltpu.PrefetchScalarGridSpec(
            num_scalar_prefetch=1,
            grid=(),
            in_specs=[pl.BlockSpec(memory_space=pltpu.HBM)],
            out_specs=pl.BlockSpec(memory_space=pltpu.VMEM),
            scratch_shapes=[pltpu.SMEM((n_slots,), jnp.int32), pltpu.SemaphoreType.DMA],
        ),
        compiler_params=pltpu.CompilerParams(vmem_limit_bytes=4 * 2**20),
        cost_estimate=pl.CostEstimate(flops=0, bytes_accessed=24 * 2**20, transcendentals=0),
    )(slots, pltpu.with_memory_space_constraint(values, pltpu.HBM))


def dense_dot(a_ref, x_refs, shards, chunk):
    group = a_ref.shape[1]
    total = None
    for k, x_ref in zip(shards, x_refs):
        lhs = jnp.concatenate(
            [
                jnp.concatenate([a_ref[chunk, r, k * group + c] for c in range(group)], axis=1)
                for r in range(group)
            ],
            axis=0,
        )
        part = jnp.dot(lhs, x_ref[...], preferred_element_type=jnp.float32)
        total = part if total is None else total + part
    return total


def product_kernel(first, shards, a_ref, *refs):
    *in_refs, o_ref = refs
    total = dense_dot(a_ref, in_refs, shards, pl.program_id(0) + first)
    o_ref[0] = total + in_refs[-1][0] if len(in_refs) > len(shards) else total


def quantize(total, o_ref):
    n = total.shape[0] // BS
    width = total.shape[1]
    row = lax.broadcasted_iota(jnp.int32, (16, width), 0)
    tail = jnp.zeros((16, width), jnp.float32)
    for b in range(n):
        part = total[b * BS : (b + 1) * BS]
        top = jnp.maximum(jnp.max(jnp.abs(part), axis=0, keepdims=True), 1e-30)
        step = jnp.ceil(jnp.log(top) * (OCTAVE / math.log(2.0)))
        scaled = part * (jnp.exp(step * (-math.log(2.0) / OCTAVE)) * LEVELS)
        o_ref[b * BS : (b + 1) * BS, :] = jnp.round(scaled).astype(jnp.int32).astype(jnp.int16)
        tail = jnp.where(row == b, jnp.broadcast_to(step, tail.shape), tail)
    o_ref[n * BS :, :] = tail.astype(jnp.int32).astype(jnp.int16)


def dequantize(q_ref):
    n = (q_ref.shape[0] - 16) // BS
    tail = q_ref[n * BS :, :].astype(jnp.int32).astype(jnp.float32)
    parts = []
    for b in range(n):
        scale = jnp.exp(tail[b : b + 1] * (math.log(2.0) / OCTAVE)) * (1.0 / LEVELS)
        parts.append(q_ref[b * BS : (b + 1) * BS, :].astype(jnp.int32).astype(jnp.float32) * scale)
    return jnp.concatenate(parts, axis=0)


def code_kernel(a_ref, b_ref, own_ref, *o_refs):
    total = a_ref[0] + b_ref[0]
    i = pl.program_id(0)
    for j, o_ref in enumerate(o_refs):

        @pl.when(i == j)
        def _(o_ref=o_ref):
            quantize(total, o_ref)

    @pl.when(i == len(o_refs))
    def _():
        own_ref[...] = total


def reduce_kernel(core, *refs):
    *in_refs, s_ref, mine_ref, other_ref, pack = refs
    total = None
    for ref in in_refs:
        term = dequantize(ref) if ref.dtype == jnp.int16 else ref[...]
        total = term if total is None else total + term
    s_ref[...] = total
    gram_store(total, pack)
    half = pack.shape[0] // 2
    c = core[0]
    mine_ref[...] = pack[pl.ds(pl.multiple_of(c * half, 8), half), :]
    other_ref[...] = pack[pl.ds(pl.multiple_of((1 - c) * half, 8), half), :]


def gram_store(total, pack):
    high = total.astype(jnp.bfloat16)
    low = (total - high.astype(jnp.float32)).astype(jnp.bfloat16)
    dims = (((0,), (0,)), ((), ()))
    dot = functools.partial(lax.dot_general, dimension_numbers=dims, preferred_element_type=jnp.float32)
    cross = dot(high, low)
    gram = dot(high, high) + dot(low, low) + cross + cross.T
    row = lax.broadcasted_iota(jnp.int32, (PANEL, PANEL), 0)
    lane = lax.broadcasted_iota(jnp.int32, (PANEL, PANEL), 1)
    second = gram[PANEL:, PANEL:]
    pack[0:PANEL, :] = jnp.where(lane >= row, gram[:PANEL, :PANEL], second)
    pack[PANEL : 2 * PANEL, :] = gram[:PANEL, PANEL:]
    diagonal = jnp.sum(jnp.where(lane == row, second, 0.0), axis=0, keepdims=True)
    pack[2 * PANEL :, :] = jnp.broadcast_to(diagonal, (PACK - 2 * PANEL, PANEL))


def split(x, terms):
    out = []
    for _ in range(terms):
        part = x.astype(jnp.bfloat16)
        out.append(part)
        x = x - part.astype(jnp.float32)
    return out


PAIRS = ((0, 0), (0, 1), (1, 0), (1, 1), (0, 2), (2, 0))


def factor(gram):
    n = gram.shape[0]
    sub = lax.broadcasted_iota(jnp.int32, (8, n), 0)
    lane = lax.broadcasted_iota(jnp.int32, (8, n), 1)
    left = [gram[8 * i : 8 * i + 8] for i in range(n // 8)]
    right = [(lane == sub + 8 * i).astype(jnp.float32) for i in range(n // 8)]

    def row(x, k):
        return jnp.broadcast_to(x[k : k + 1], x.shape)

    for first in range(0, n // 8, STEP):
        last = first + STEP
        for b in range(first, last):
            cols = {
                t: [jnp.broadcast_to(left[t][:, 8 * b + k : 8 * b + k + 1], (8, n)) for k in range(8)]
                for t in range(b, last)
            }
            for k in range(8):
                pivot = row(cols[b][k], k)
                root = lax.rsqrt(pivot)
                root = root * (1.5 - 0.5 * pivot * root * root)
                mult = {t: cols[t][k] * root for t in range(b, last)}
                for j in range(k + 1, 8):
                    other = row(mult[b], j)
                    for t in range(b, last):
                        cols[t][j] = cols[t][j] - mult[t] * other
                top_left, top_right = row(left[b], k) * root, row(right[b], k) * root
                below = jnp.where(sub > k, mult[b], 0.0)
                left[b] = jnp.where(sub == k, top_left, left[b] - below * top_left)
                right[b] = jnp.where(sub == k, top_right, right[b] - below * top_right)
                for t in range(b + 1, last):
                    left[t] = left[t] - mult[t] * top_left
                    right[t] = right[t] - mult[t] * top_right
        if last < n // 8:
            u = split(jnp.concatenate(left[first:last], axis=0), 3)
            v = split(jnp.concatenate(right[first:last], axis=0), 3)
            lhs = jnp.concatenate([u[i] for i, _ in PAIRS], axis=0)
            rhs = jnp.concatenate(
                [jnp.concatenate([u[j] for _, j in PAIRS], axis=0), jnp.concatenate([v[j] for _, j in PAIRS], axis=0)],
                axis=1,
            )
            change = lax.dot_general(lhs, rhs, (((0,), (0,)), ((), ())), preferred_element_type=jnp.float32)
            for t in range(last, n // 8):
                left[t] = left[t] - change[8 * t : 8 * t + 8, :n]
                right[t] = right[t] - change[8 * t : 8 * t + 8, n:]
    upper = jnp.concatenate([jnp.where(lane >= sub + 8 * i, x, 0.0) for i, x in enumerate(left)], axis=0)
    return upper, jnp.concatenate(right, axis=0)


def dot3(a, b, dims):
    (ah, al), (bh, bl) = split(a, 2), split(b, 2)
    dot = functools.partial(
        lax.dot_general, dimension_numbers=(dims, ((), ())), preferred_element_type=jnp.float32
    )
    return dot(ah, bh) + (dot(ah, bl) + dot(al, bh))


def full_dot(a, b, dims):
    return lax.dot_general(
        a, b, (dims, ((), ())), precision=lax.Precision.HIGHEST, preferred_element_type=jnp.float32
    )


NN, NT, TN = ((1,), (0,)), ((1,), (1,)), ((0,), (0,))


def tail_kernel(scale, core, mine_ref, other_ref, s_ref, basis_ref, upper_ref, pack):
    half = pack.shape[0] // 2
    c = core[0]
    pack[pl.ds(pl.multiple_of(c * half, 8), half), :] = mine_ref[...] * scale
    pack[pl.ds(pl.multiple_of((1 - c) * half, 8), half), :] = other_ref[...] * scale
    row = lax.broadcasted_iota(jnp.int32, (PANEL, PANEL), 0)
    lane = lax.broadcasted_iota(jnp.int32, (PANEL, PANEL), 1)
    both, cross = pack[0:PANEL, :], pack[PANEL : 2 * PANEL, :]
    turned = both.T
    gram_one = jnp.where(lane >= row, both, turned)
    diagonal = jnp.broadcast_to(pack[2 * PANEL : 2 * PANEL + 1, :], both.shape)
    gram_two = jnp.where(lane == row, diagonal, jnp.where(lane < row, both, turned))
    upper_one, low_one = factor(gram_one)
    coupling = full_dot(low_one, cross, NN)
    upper_two, low_two = factor(gram_two - full_dot(coupling, coupling, TN))
    mixed = -full_dot(low_two, full_dot(coupling, low_one, TN), NN)
    zero = jnp.zeros_like(upper_one)
    upper_ref[0:PANEL, 0:PANEL] = upper_one
    upper_ref[0:PANEL, PANEL:] = coupling
    upper_ref[PANEL:, 0:PANEL] = zero
    upper_ref[PANEL:, PANEL:] = upper_two
    first, second = s_ref[:, 0:PANEL], s_ref[...]
    basis_ref[:, 0:PANEL] = dot3(first, low_one, NT)
    basis_ref[:, PANEL:] = dot3(second, jnp.concatenate([mixed, low_two], axis=1), NT)


def whole(shape):
    return pl.BlockSpec(shape, lambda *_: (0,) * len(shape))


def gather_row(value, ready):
    bits = lax.axis_size("row").bit_length() - 1
    shards = {0: value}
    for bit in reversed(range(bits)):
        for k, v in list(shards.items()):
            if bit == 0 and k:
                v, ready = lax.optimization_barrier((v, ready))
            shards[k | 1 << bit] = exchange(v, "row", 1 << bit)
    return [shards[k] for k in range(2**bits)], ready


def dense_sketch(gaussian_sketch, block_values, local_rows, local_cols, grid_rows, grid_cols):
    size_col = lax.axis_size("col")
    chips = size_col // 2
    shard_rows, width = gaussian_sketch.shape
    group = shard_rows // BS
    me = lax.axis_index("col")
    owner = local_rows // group
    peer_core = (owner + me) % 2
    near = (owner // 2) ^ (me // 2)
    place = ((1 - peer_core) * chips + near) * group + local_rows % group
    shard = (local_cols // group) ^ lax.axis_index("row")
    slots = place * grid_cols + shard * group + local_cols % group
    dense = scatter_blocks(slots, block_values, grid_rows * grid_cols)
    dense = dense.reshape(2 * chips, group, grid_cols, BS, BS)
    shards, dense = gather_row(gaussian_sketch, dense)
    late = [k for k in range(len(shards)) if k % 2 and k > 1]
    early = [k for k in range(len(shards)) if k not in late]

    params = pltpu.CompilerParams(vmem_limit_bytes=12 * 2**20)
    flops = 2 * shard_rows * grid_cols * BS * width
    bytes_a = 2 * shard_rows * grid_cols * BS

    def cost(n):
        return pl.CostEstimate(flops=n * flops, bytes_accessed=n * bytes_a, transcendentals=0)

    held = pl.BlockSpec(memory_space=pltpu.VMEM)
    r_block = (1, shard_rows, width)
    def product(first, chosen, *added):
        block = pl.BlockSpec(r_block, lambda i: (i, 0, 0))
        return pl.pallas_call(
            functools.partial(product_kernel, first, chosen),
            grid=(chips,),
            in_specs=[held] * (len(chosen) + 1) + [block] * len(added),
            out_specs=block,
            out_shape=jax.ShapeDtypeStruct((chips, shard_rows, width), jnp.float32),
            compiler_params=params,
            cost_estimate=cost(chips),
        )(dense, *[shards[k] for k in chosen], *added)

    far, near = product(0, early), product(chips, early)
    if late:
        far = product(0, late, far)
    peer_sum = exchange(far, "col", 1)
    near_sum = product(chips, late, near) if late else near
    sent = jax.ShapeDtypeStruct((shard_rows + 16, width), jnp.int16)
    own_last = pl.BlockSpec(r_block, lambda i: ((i + 1) % chips, 0, 0))
    own_shape = (shard_rows, width)
    own, *coded = pl.pallas_call(
        code_kernel,
        grid=(chips,),
        in_specs=[own_last, own_last],
        out_specs=[whole(own_shape)] + [whole(sent.shape)] * (chips - 1),
        out_shape=[jax.ShapeDtypeStruct(own_shape, jnp.float32)] + [sent] * (chips - 1),
        compiler_params=params,
    )(near_sum, peer_sum)
    return [own] + [exchange(q, "col", 2 * (i + 1)) for i, q in enumerate(coded)]


def tile_product(sketch_blocks, block_values, local_rows, local_cols, tile_rows):
    group_size = math.gcd(block_values.shape[0], 64)
    col_width = sketch_blocks.shape[2]

    def advance(counter, summed):
        offset = (counter * group_size).astype(jnp.int32)
        values = lax.dynamic_slice_in_dim(block_values, offset, group_size, 0)
        row_ids = lax.dynamic_slice_in_dim(local_rows, offset, group_size, 0)
        col_ids = lax.dynamic_slice_in_dim(local_cols, offset, group_size, 0)
        picked = jnp.take(sketch_blocks, col_ids, axis=0)
        product = jnp.einsum("gab,gbs->gas", values, picked, preferred_element_type=jnp.float32)
        return summed.at[row_ids].add(product)

    initial = jnp.zeros((tile_rows, block_values.shape[1], col_width), jnp.float32)
    summed = lax.fori_loop(0, block_values.shape[0] // group_size, advance, initial)
    return summed.reshape(tile_rows * block_values.shape[1], col_width)


def looped_sketch(gaussian_sketch, block_values, local_rows, local_cols, grid_rows, grid_cols):
    gathered = lax.all_gather(gaussian_sketch, "row", axis=0, tiled=True)
    sketch_blocks = gathered.reshape(grid_cols, BS, gathered.shape[1])
    partial_value = tile_product(sketch_blocks, block_values, local_rows, local_cols, grid_rows)
    return [lax.psum_scatter(partial_value, "col", scatter_dimension=0, tiled=True)]


def direct_sum(value, axis, low_bit, bits):
    terms = [value] + [exchange(value, axis, mask << low_bit) for mask in range(1, 2**bits)]
    while len(terms) > 1:
        terms = [a + b for a, b in zip(terms[0::2], terms[1::2])]
    return terms[0]


def sum_over_axis(value, axis, low_bit):
    bits = lax.axis_size(axis).bit_length() - 1
    while low_bit < bits:
        take = min(2, bits - low_bit)
        value = direct_sum(value, axis, low_bit, take)
        low_bit += take
    return value


def sum_over_mesh(mine, other, core):
    mine = mine + exchange(other, "col", 1)
    mine = sum_over_axis(mine, "col", 1)
    mine = sum_over_axis(mine, "row", 0)
    return mine, exchange(mine, "col", 1)


def on_device(gaussian_sketch, block_values, block_rows, block_columns):
    size_row = lax.axis_size("row")
    size_col = lax.axis_size("col")
    shard_rows, width = gaussian_sketch.shape
    grid_rows = shard_rows * size_col // BS
    grid_cols = shard_rows * size_row // BS
    local_rows = block_rows - lax.axis_index("row") * grid_rows
    local_cols = block_columns - lax.axis_index("col") * grid_cols
    dense = 2 * grid_rows * grid_cols * BS * BS <= DENSE_BYTES
    sketch = dense_sketch if dense else looped_sketch
    terms = sketch(
        gaussian_sketch, block_values, local_rows, local_cols, grid_rows, grid_cols
    )
    core = lax.axis_index("col") % 2
    half = jax.ShapeDtypeStruct((PACK // 2, PANEL), jnp.float32)
    sketched, mine, other = pl.pallas_call(
        reduce_kernel,
        grid_spec=pltpu.PrefetchScalarGridSpec(
            num_scalar_prefetch=1,
            grid=(1,),
            in_specs=[whole(t.shape) for t in terms],
            out_specs=[whole((shard_rows, width)), whole(half.shape), whole(half.shape)],
            scratch_shapes=[pltpu.VMEM((PACK, PANEL), jnp.float32)],
        ),
        out_shape=[jax.ShapeDtypeStruct((shard_rows, width), jnp.float32), half, half],
        compiler_params=pltpu.CompilerParams(vmem_limit_bytes=12 * 2**20),
    )(core.reshape(1), *terms)
    order_total = shard_rows * size_row * size_col
    mine, other = sum_over_mesh(mine, other, core)
    range_basis, upper_factor = pl.pallas_call(
        functools.partial(tail_kernel, 1.0 / order_total),
        grid_spec=pltpu.PrefetchScalarGridSpec(
            num_scalar_prefetch=1,
            grid=(1,),
            in_specs=[whole(half.shape), whole(half.shape), whole(sketched.shape)],
            out_specs=[whole(sketched.shape), whole((width, width))],
            scratch_shapes=[pltpu.VMEM((PACK, PANEL), jnp.float32)],
        ),
        out_shape=[
            jax.ShapeDtypeStruct(sketched.shape, jnp.float32),
            jax.ShapeDtypeStruct((width, width), jnp.float32),
        ],
        compiler_params=pltpu.CompilerParams(vmem_limit_bytes=16 * 2**20),
    )(core.reshape(1), mine, other, sketched)
    return (range_basis, upper_factor)


def solution(mesh):
    return jax.shard_map(
        on_device,
        mesh=mesh,
        in_specs=(
            P(("col", "row"), None),
            P(("row", "col"), None, None),
            P(("row", "col")),
            P(("row", "col")),
        ),
        out_specs=(P(("row", "col"), None), P()),
        check_vma=False,
    )
```

```python
import functools
import math

import jax
import jax.numpy as jnp
from jax import lax
from jax.experimental import pallas as pl
from jax.experimental.pallas import tpu as pltpu
from jax.sharding import PartitionSpec as P

PANEL = 128
BS = 128
LEVELS = 32700.0
OCTAVE = 64.0
DENSE_BYTES = 32 * 2**20
STEP = 4
PACK = 2 * PANEL + 16


def exchange(value, axis, mask):
    size = lax.axis_size(axis)
    return lax.ppermute(value, axis, [(i, i ^ mask) for i in range(size)])


def scatter_kernel(slots, values, dense, sem):
    step = math.gcd(8, math.gcd(dense.shape[0], values.shape[0]))

    @pl.loop(0, dense.shape[0] // step)
    def _(s):
        dense[pl.ds(s * step, step)] = jnp.zeros((step, *dense.shape[1:]), dense.dtype)

    @pl.loop(0, values.shape[0] // step)
    def _(b):
        for u in range(step):
            block = b * step + u
            pltpu.make_async_copy(values.at[block], dense.at[slots[block]], sem).start()

    pltpu.make_async_copy(values, values, sem).wait()


def scatter_blocks(slots, values, n_slots):
    return pl.pallas_call(
        scatter_kernel,
        out_shape=pltpu.VMEM((n_slots, BS, BS), values.dtype),
        grid_spec=pltpu.PrefetchScalarGridSpec(
            num_scalar_prefetch=1,
            grid=(),
            in_specs=[pl.BlockSpec(memory_space=pltpu.HBM)],
            out_specs=pl.BlockSpec(memory_space=pltpu.VMEM),
            scratch_shapes=[pltpu.SemaphoreType.DMA],
        ),
        compiler_params=pltpu.CompilerParams(vmem_limit_bytes=4 * 2**20),
        cost_estimate=pl.CostEstimate(flops=0, bytes_accessed=24 * 2**20, transcendentals=0),
    )(slots, pltpu.with_memory_space_constraint(values, pltpu.HBM))


def dense_dot(a_ref, x_refs, shards, chunk):
    group = a_ref.shape[1]
    total = None
    for k, x_ref in zip(shards, x_refs):
        lhs = jnp.concatenate(
            [
                jnp.concatenate([a_ref[chunk, r, k * group + c] for c in range(group)], axis=1)
                for r in range(group)
            ],
            axis=0,
        )
        part = jnp.dot(lhs, x_ref[...], preferred_element_type=jnp.float32)
        total = part if total is None else total + part
    return total


def product_kernel(first, shards, a_ref, *refs):
    *in_refs, o_ref = refs
    total = dense_dot(a_ref, in_refs, shards, pl.program_id(0) + first)
    added = in_refs[len(shards) :]
    o_ref[0] = total + added[0][0] if added else total


def quantize(total, o_ref):
    n = total.shape[0] // BS
    width = total.shape[1]
    row = lax.broadcasted_iota(jnp.int32, (16, width), 0)
    tail = jnp.zeros((16, width), jnp.float32)
    for b in range(n):
        part = total[b * BS : (b + 1) * BS]
        top = jnp.maximum(jnp.max(jnp.abs(part), axis=0, keepdims=True), 1e-30)
        step = jnp.ceil(jnp.log(top) * (OCTAVE / math.log(2.0)))
        scaled = part * (jnp.exp(step * (-math.log(2.0) / OCTAVE)) * LEVELS)
        o_ref[b * BS : (b + 1) * BS, :] = jnp.round(scaled).astype(jnp.int32).astype(jnp.int16)
        tail = jnp.where(row == b, jnp.broadcast_to(step, tail.shape), tail)
    o_ref[n * BS :, :] = tail.astype(jnp.int32).astype(jnp.int16)


def dequantize(q_ref):
    n = (q_ref.shape[0] - 16) // BS
    tail = q_ref[n * BS :, :].astype(jnp.int32).astype(jnp.float32)
    parts = []
    for b in range(n):
        scale = jnp.exp(tail[b : b + 1] * (math.log(2.0) / OCTAVE)) * (1.0 / LEVELS)
        parts.append(q_ref[b * BS : (b + 1) * BS, :].astype(jnp.int32).astype(jnp.float32) * scale)
    return jnp.concatenate(parts, axis=0)


def code_kernel(a_ref, b_ref, *o_refs):
    total = a_ref[0] + b_ref[0]
    for j, o_ref in enumerate(o_refs):

        @pl.when(pl.program_id(0) == j)
        def _(o_ref=o_ref):
            if o_ref.dtype == jnp.int16:
                quantize(total, o_ref)
            else:
                o_ref[...] = total


def reduce_kernel(core, *refs):
    *in_refs, s_ref, mine_ref, other_ref, pack = refs
    total = None
    for ref in in_refs:
        term = dequantize(ref) if ref.dtype == jnp.int16 else ref[...]
        total = term if total is None else total + term
    s_ref[...] = total
    gram_store(total, pack)
    half = pack.shape[0] // 2
    c = core[0]
    mine_ref[...] = pack[pl.ds(pl.multiple_of(c * half, 8), half), :]
    other_ref[...] = pack[pl.ds(pl.multiple_of((1 - c) * half, 8), half), :]


def gram_store(total, pack):
    high = total.astype(jnp.bfloat16)
    low = (total - high.astype(jnp.float32)).astype(jnp.bfloat16)
    dims = (((0,), (0,)), ((), ()))
    dot = functools.partial(lax.dot_general, dimension_numbers=dims, preferred_element_type=jnp.float32)
    cross = dot(high, low)
    gram = dot(high, high) + dot(low, low) + cross + cross.T
    row = lax.broadcasted_iota(jnp.int32, (PANEL, PANEL), 0)
    lane = lax.broadcasted_iota(jnp.int32, (PANEL, PANEL), 1)
    second = gram[PANEL:, PANEL:]
    pack[0:PANEL, :] = jnp.where(lane >= row, gram[:PANEL, :PANEL], second)
    pack[PANEL : 2 * PANEL, :] = gram[:PANEL, PANEL:]
    diagonal = jnp.sum(jnp.where(lane == row, second, 0.0), axis=0, keepdims=True)
    pack[2 * PANEL :, :] = jnp.broadcast_to(diagonal, (PACK - 2 * PANEL, PANEL))


def split(x, terms):
    out = []
    for _ in range(terms):
        part = x.astype(jnp.bfloat16)
        out.append(part)
        x = x - part.astype(jnp.float32)
    return out


PAIRS = ((0, 0), (0, 1), (1, 0), (1, 1), (0, 2), (2, 0))


def factor(gram):
    n = gram.shape[0]
    eye = lax.broadcasted_iota(jnp.int32, (n, n), 0) == lax.broadcasted_iota(jnp.int32, (n, n), 1)
    picked = jnp.where(eye, gram, 0.0)
    diagonal = jnp.sum(picked, axis=0, keepdims=True)
    inverse_row = lax.rsqrt(diagonal)
    inverse_col = lax.rsqrt(jnp.sum(picked, axis=1, keepdims=True))
    gram = gram * inverse_row * inverse_col

    sub = lax.broadcasted_iota(jnp.int32, (8, n), 0)
    lane = lax.broadcasted_iota(jnp.int32, (8, n), 1)
    left = [gram[8 * i : 8 * i + 8] for i in range(n // 8)]
    right = [(lane == sub + 8 * i).astype(jnp.float32) for i in range(n // 8)]

    def row(x, k):
        return jnp.broadcast_to(x[k : k + 1], x.shape)

    for first in range(0, n // 8, STEP):
        last = first + STEP
        for b in range(first, last):
            cols = {
                t: [jnp.broadcast_to(left[t][:, 8 * b + k : 8 * b + k + 1], (8, n)) for k in range(8)]
                for t in range(b, last)
            }
            for k in range(0, 8, 2):
                p, q, r = row(cols[b][k], k), row(cols[b][k], k + 1), row(cols[b][k + 1], k + 1)
                root_p = lax.rsqrt(p)
                ratio = q * root_p
                det = p * r - q * q
                root_r = lax.rsqrt(det) * (p * root_p)
                one = {t: cols[t][k] * root_p for t in range(b, last)}
                two = {t: (cols[t][k + 1] - one[t] * ratio) * root_r for t in range(b, last)}
                for j in range(k + 2, 8):
                    u, v = row(one[b], j), row(two[b], j)
                    for t in range(b, last):
                        cols[t][j] = cols[t][j] - one[t] * u - two[t] * v
                below_one = jnp.where(sub > k + 1, one[b], 0.0)
                below_two = jnp.where(sub > k + 1, two[b], 0.0)
                for side in (left, right):
                    top = row(side[b], k) * root_p
                    low = (row(side[b], k + 1) - top * ratio) * root_r
                    rest = side[b] - below_one * top - below_two * low
                    side[b] = jnp.where(sub == k, top, jnp.where(sub == k + 1, low, rest))
                    for t in range(b + 1, last):
                        side[t] = side[t] - one[t] * top - two[t] * low
        if last < n // 8:
            u = split(jnp.concatenate(left[first:last], axis=0), 3)
            v = split(jnp.concatenate(right[first:last], axis=0), 3)
            lhs = jnp.concatenate([u[i] for i, _ in PAIRS], axis=0)
            rhs = jnp.concatenate(
                [jnp.concatenate([u[j] for _, j in PAIRS], axis=0), jnp.concatenate([v[j] for _, j in PAIRS], axis=0)],
                axis=1,
            )
            change = lax.dot_general(lhs, rhs, (((0,), (0,)), ((), ())), preferred_element_type=jnp.float32)
            for t in range(last, n // 8):
                left[t] = left[t] - change[8 * t : 8 * t + 8, :n]
                right[t] = right[t] - change[8 * t : 8 * t + 8, n:]
    upper = jnp.concatenate([jnp.where(lane >= sub + 8 * i, x, 0.0) for i, x in enumerate(left)], axis=0)
    return upper * (diagonal * inverse_row), jnp.concatenate(right, axis=0) * inverse_row


def dot3(a, b, dims):
    (ah, al), (bh, bl) = split(a, 2), split(b, 2)
    dot = functools.partial(
        lax.dot_general, dimension_numbers=(dims, ((), ())), preferred_element_type=jnp.float32
    )
    return dot(ah, bh) + (dot(ah, bl) + dot(al, bh))


def full_dot(a, b, dims):
    return lax.dot_general(
        a, b, (dims, ((), ())), precision=lax.Precision.HIGHEST, preferred_element_type=jnp.float32
    )


NN, NT, TN = ((1,), (0,)), ((1,), (1,)), ((0,), (0,))


def tail_kernel(scale, core, mine_ref, other_ref, s_ref, basis_ref, upper_ref, pack):
    half = pack.shape[0] // 2
    c = core[0]
    pack[pl.ds(pl.multiple_of(c * half, 8), half), :] = mine_ref[...] * scale
    pack[pl.ds(pl.multiple_of((1 - c) * half, 8), half), :] = other_ref[...] * scale
    row = lax.broadcasted_iota(jnp.int32, (PANEL, PANEL), 0)
    lane = lax.broadcasted_iota(jnp.int32, (PANEL, PANEL), 1)
    both, cross = pack[0:PANEL, :], pack[PANEL : 2 * PANEL, :]
    turned = both.T
    gram_one = jnp.where(lane >= row, both, turned)
    diagonal = jnp.broadcast_to(pack[2 * PANEL : 2 * PANEL + 1, :], both.shape)
    gram_two = jnp.where(lane == row, diagonal, jnp.where(lane < row, both, turned))
    upper_one, low_one = factor(gram_one)
    coupling = full_dot(low_one, cross, NN)
    upper_two, low_two = factor(gram_two - full_dot(coupling, coupling, TN))
    mixed = -full_dot(low_two, full_dot(coupling, low_one, TN), NN)
    zero = jnp.zeros_like(upper_one)
    upper_ref[0:PANEL, 0:PANEL] = upper_one
    upper_ref[0:PANEL, PANEL:] = coupling
    upper_ref[PANEL:, 0:PANEL] = zero
    upper_ref[PANEL:, PANEL:] = upper_two
    first, second = s_ref[:, 0:PANEL], s_ref[...]
    basis_ref[:, 0:PANEL] = dot3(first, low_one, NT)
    basis_ref[:, PANEL:] = dot3(second, jnp.concatenate([mixed, low_two], axis=1), NT)


def whole(shape):
    return pl.BlockSpec(shape, lambda *_: (0,) * len(shape))


def gather_row(value, ready):
    bits = lax.axis_size("row").bit_length() - 1
    shards = {0: value}
    for bit in reversed(range(bits)):
        for k, v in list(shards.items()):
            if bit == 0 and k:
                v, ready = lax.optimization_barrier((v, ready))
            shards[k | 1 << bit] = exchange(v, "row", 1 << bit)
    return [shards[k] for k in range(2**bits)], ready


def dense_sketch(gaussian_sketch, block_values, local_rows, local_cols, grid_rows, grid_cols):
    size_col = lax.axis_size("col")
    chips = size_col // 2
    shard_rows, width = gaussian_sketch.shape
    group = shard_rows // BS
    me = lax.axis_index("col")
    owner = local_rows // group
    peer_core = (owner + me) % 2
    near = ((owner // 2 ^ me // 2) + chips - 1) % chips
    place = ((1 - peer_core) * chips + near) * group + local_rows % group
    shard = (local_cols // group) ^ lax.axis_index("row")
    slots = place * grid_cols + shard * group + local_cols % group
    dense = scatter_blocks(slots, block_values, grid_rows * grid_cols)
    dense = dense.reshape(2 * chips, group, grid_cols, BS, BS)
    shards, dense = gather_row(gaussian_sketch, dense)
    late = [k for k in range(len(shards)) if k % 2 and k > 1]
    early = [k for k in range(len(shards)) if k not in late]

    params = pltpu.CompilerParams(vmem_limit_bytes=12 * 2**20)
    flops = 2 * shard_rows * grid_cols * BS * width
    bytes_a = 2 * shard_rows * grid_cols * BS

    def cost(n):
        return pl.CostEstimate(flops=n * flops, bytes_accessed=n * bytes_a, transcendentals=0)

    held = pl.BlockSpec(memory_space=pltpu.VMEM)
    r_block = (1, shard_rows, width)
    def block(first):
        return pl.BlockSpec(r_block, lambda i: (i + first, 0, 0))

    def product(first, count, chosen, *added):
        return pl.pallas_call(
            functools.partial(product_kernel, first, chosen),
            grid=(count,),
            in_specs=[held] * (len(chosen) + 1) + [block(first)] * len(added),
            out_specs=block(0),
            out_shape=jax.ShapeDtypeStruct((count, shard_rows, width), jnp.float32),
            compiler_params=params,
            cost_estimate=cost(count),
        )(dense, *[shards[k] for k in chosen], *added)

    first_sum = product(0, 2 * chips, early)
    parts = [(0, chips // 2), (chips // 2, chips - chips // 2)]
    peer = [exchange(product(at, n, late, first_sum), "col", 1) for at, n in parts]
    near = [product(chips + at, n, late, first_sum) for at, n in parts]
    sent = jax.ShapeDtypeStruct((shard_rows + 16, width), jnp.int16)
    kept = jax.ShapeDtypeStruct((shard_rows, width), jnp.float32)
    terms = []
    for (at, n), mine, theirs in zip(parts, near, peer):
        shapes = [kept if at + i == chips - 1 else sent for i in range(n)]
        done = pl.pallas_call(
            code_kernel,
            grid=(n,),
            in_specs=[block(0), block(0)],
            out_specs=[whole(x.shape) for x in shapes],
            out_shape=shapes,
            compiler_params=params,
        )(mine, theirs)
        for i, x in enumerate(done):
            terms.append(x if x.dtype == jnp.float32 else exchange(x, "col", 2 * (at + i + 1)))
    return terms


def tile_product(sketch_blocks, block_values, local_rows, local_cols, tile_rows):
    group_size = math.gcd(block_values.shape[0], 64)
    col_width = sketch_blocks.shape[2]

    def advance(counter, summed):
        offset = (counter * group_size).astype(jnp.int32)
        values = lax.dynamic_slice_in_dim(block_values, offset, group_size, 0)
        row_ids = lax.dynamic_slice_in_dim(local_rows, offset, group_size, 0)
        col_ids = lax.dynamic_slice_in_dim(local_cols, offset, group_size, 0)
        picked = jnp.take(sketch_blocks, col_ids, axis=0)
        product = jnp.einsum("gab,gbs->gas", values, picked, preferred_element_type=jnp.float32)
        return summed.at[row_ids].add(product)

    initial = jnp.zeros((tile_rows, block_values.shape[1], col_width), jnp.float32)
    summed = lax.fori_loop(0, block_values.shape[0] // group_size, advance, initial)
    return summed.reshape(tile_rows * block_values.shape[1], col_width)


def looped_sketch(gaussian_sketch, block_values, local_rows, local_cols, grid_rows, grid_cols):
    gathered = lax.all_gather(gaussian_sketch, "row", axis=0, tiled=True)
    sketch_blocks = gathered.reshape(grid_cols, BS, gathered.shape[1])
    partial_value = tile_product(sketch_blocks, block_values, local_rows, local_cols, grid_rows)
    return [lax.psum_scatter(partial_value, "col", scatter_dimension=0, tiled=True)]


def direct_sum(value, axis, low_bit, bits):
    terms = [value] + [exchange(value, axis, mask << low_bit) for mask in range(1, 2**bits)]
    while len(terms) > 1:
        terms = [a + b for a, b in zip(terms[0::2], terms[1::2])]
    return terms[0]


def sum_over_axis(value, axis, low_bit):
    bits = lax.axis_size(axis).bit_length() - 1
    while low_bit < bits:
        take = min(2, bits - low_bit)
        value = direct_sum(value, axis, low_bit, take)
        low_bit += take
    return value


def sum_over_mesh(mine, other, core):
    mine = mine + exchange(other, "col", 1)
    mine = sum_over_axis(mine, "col", 1)
    mine = sum_over_axis(mine, "row", 0)
    return mine, exchange(mine, "col", 1)


def on_device(gaussian_sketch, block_values, block_rows, block_columns):
    size_row = lax.axis_size("row")
    size_col = lax.axis_size("col")
    shard_rows, width = gaussian_sketch.shape
    grid_rows = shard_rows * size_col // BS
    grid_cols = shard_rows * size_row // BS
    local_rows = block_rows - lax.axis_index("row") * grid_rows
    local_cols = block_columns - lax.axis_index("col") * grid_cols
    dense = 2 * grid_rows * grid_cols * BS * BS <= DENSE_BYTES
    sketch = dense_sketch if dense else looped_sketch
    terms = sketch(
        gaussian_sketch, block_values, local_rows, local_cols, grid_rows, grid_cols
    )
    core = lax.axis_index("col") % 2
    half = jax.ShapeDtypeStruct((PACK // 2, PANEL), jnp.float32)
    sketched, mine, other = pl.pallas_call(
        reduce_kernel,
        grid_spec=pltpu.PrefetchScalarGridSpec(
            num_scalar_prefetch=1,
            grid=(1,),
            in_specs=[whole(t.shape) for t in terms],
            out_specs=[whole((shard_rows, width)), whole(half.shape), whole(half.shape)],
            scratch_shapes=[pltpu.VMEM((PACK, PANEL), jnp.float32)],
        ),
        out_shape=[jax.ShapeDtypeStruct((shard_rows, width), jnp.float32), half, half],
        compiler_params=pltpu.CompilerParams(vmem_limit_bytes=12 * 2**20),
    )(core.reshape(1), *terms)
    order_total = shard_rows * size_row * size_col
    mine, other = sum_over_mesh(mine, other, core)
    range_basis, upper_factor = pl.pallas_call(
        functools.partial(tail_kernel, 1.0 / order_total),
        grid_spec=pltpu.PrefetchScalarGridSpec(
            num_scalar_prefetch=1,
            grid=(1,),
            in_specs=[whole(half.shape), whole(half.shape), whole(sketched.shape)],
            out_specs=[whole(sketched.shape), whole((width, width))],
            scratch_shapes=[pltpu.VMEM((PACK, PANEL), jnp.float32)],
        ),
        out_shape=[
            jax.ShapeDtypeStruct(sketched.shape, jnp.float32),
            jax.ShapeDtypeStruct((width, width), jnp.float32),
        ],
        compiler_params=pltpu.CompilerParams(vmem_limit_bytes=16 * 2**20),
    )(core.reshape(1), mine, other, sketched)
    return (range_basis, upper_factor)


def solution(mesh):
    return jax.shard_map(
        on_device,
        mesh=mesh,
        in_specs=(
            P(("col", "row"), None),
            P(("row", "col"), None, None),
            P(("row", "col")),
            P(("row", "col")),
        ),
        out_specs=(P(("row", "col"), None), P()),
        check_vma=False,
    )
```

```python
import functools
import math

import jax
import jax.numpy as jnp
from jax import lax
from jax.experimental import pallas as pl
from jax.experimental.pallas import tpu as pltpu
from jax.sharding import PartitionSpec as P

PANEL = 128
BS = 128
LEVELS = 32700.0
OCTAVE = 64.0
DENSE_BYTES = 32 * 2**20
STEP = 4
PACK = 2 * PANEL + 16


def exchange(value, axis, mask):
    size = lax.axis_size(axis)
    return lax.ppermute(value, axis, [(i, i ^ mask) for i in range(size)])


def scatter_kernel(slots, values, dense, sem):
    step = math.gcd(8, math.gcd(dense.shape[0], values.shape[0]))

    @pl.loop(0, dense.shape[0] // step)
    def _(s):
        dense[pl.ds(s * step, step)] = jnp.zeros((step, *dense.shape[1:]), dense.dtype)

    @pl.loop(0, values.shape[0] // step)
    def _(b):
        for u in range(step):
            block = b * step + u
            pltpu.make_async_copy(values.at[block], dense.at[slots[block]], sem).start()

    pltpu.make_async_copy(values, values, sem).wait()


def scatter_blocks(slots, values, n_slots):
    return pl.pallas_call(
        scatter_kernel,
        out_shape=pltpu.VMEM((n_slots, BS, BS), values.dtype),
        grid_spec=pltpu.PrefetchScalarGridSpec(
            num_scalar_prefetch=1,
            grid=(),
            in_specs=[pl.BlockSpec(memory_space=pltpu.HBM)],
            out_specs=pl.BlockSpec(memory_space=pltpu.VMEM),
            scratch_shapes=[pltpu.SemaphoreType.DMA],
        ),
        compiler_params=pltpu.CompilerParams(vmem_limit_bytes=4 * 2**20),
        cost_estimate=pl.CostEstimate(flops=0, bytes_accessed=24 * 2**20, transcendentals=0),
    )(slots, pltpu.with_memory_space_constraint(values, pltpu.HBM))


def dense_dot(a_ref, x_refs, starts, chunk):
    total = None
    for start, x_ref in zip(starts, x_refs):
        span = x_ref.shape[0] // BS
        lhs = jnp.concatenate(
            [
                jnp.concatenate([a_ref[chunk, r, start + c] for c in range(span)], axis=1)
                for r in range(a_ref.shape[1])
            ],
            axis=0,
        )
        part = jnp.dot(lhs, x_ref[...], preferred_element_type=jnp.float32)
        total = part if total is None else total + part
    return total


def product_kernel(first, starts, a_ref, *refs):
    *in_refs, o_ref = refs
    total = dense_dot(a_ref, in_refs, starts, pl.program_id(0) + first)
    added = in_refs[len(starts) :]
    o_ref[0] = total + added[0][0] if added else total


def quantize(total, o_ref):
    n = total.shape[0] // BS
    width = total.shape[1]
    row = lax.broadcasted_iota(jnp.int32, (16, width), 0)
    tail = jnp.zeros((16, width), jnp.float32)
    for b in range(n):
        part = total[b * BS : (b + 1) * BS]
        top = jnp.maximum(jnp.max(jnp.abs(part), axis=0, keepdims=True), 1e-30)
        step = jnp.ceil(jnp.log(top) * (OCTAVE / math.log(2.0)))
        scaled = part * (jnp.exp(step * (-math.log(2.0) / OCTAVE)) * LEVELS)
        o_ref[b * BS : (b + 1) * BS, :] = jnp.round(scaled).astype(jnp.int32).astype(jnp.int16)
        tail = jnp.where(row == b, jnp.broadcast_to(step, tail.shape), tail)
    o_ref[n * BS :, :] = tail.astype(jnp.int32).astype(jnp.int16)


def dequantize(q_ref):
    n = (q_ref.shape[0] - 16) // BS
    tail = q_ref[n * BS :, :].astype(jnp.int32).astype(jnp.float32)
    parts = []
    for b in range(n):
        scale = jnp.exp(tail[b : b + 1] * (math.log(2.0) / OCTAVE)) * (1.0 / LEVELS)
        parts.append(q_ref[b * BS : (b + 1) * BS, :].astype(jnp.int32).astype(jnp.float32) * scale)
    return jnp.concatenate(parts, axis=0)


def code_kernel(a_ref, b_ref, *o_refs):
    total = a_ref[0] + b_ref[0]
    for j, o_ref in enumerate(o_refs):

        @pl.when(pl.program_id(0) == j)
        def _(o_ref=o_ref):
            if o_ref.dtype == jnp.int16:
                quantize(total, o_ref)
            else:
                o_ref[...] = total


def reduce_kernel(core, *refs):
    *in_refs, s_ref, mine_ref, other_ref, pack = refs
    total = None
    for ref in in_refs:
        term = dequantize(ref) if ref.dtype == jnp.int16 else ref[...]
        total = term if total is None else total + term
    s_ref[...] = total
    gram_store(total, pack)
    half = pack.shape[0] // 2
    c = core[0]
    mine_ref[...] = pack[pl.ds(pl.multiple_of(c * half, 8), half), :]
    other_ref[...] = pack[pl.ds(pl.multiple_of((1 - c) * half, 8), half), :]


def gram_store(total, pack):
    high = total.astype(jnp.bfloat16)
    low = (total - high.astype(jnp.float32)).astype(jnp.bfloat16)
    dims = (((0,), (0,)), ((), ()))
    dot = functools.partial(lax.dot_general, dimension_numbers=dims, preferred_element_type=jnp.float32)
    cross = dot(high, low)
    gram = dot(high, high) + dot(low, low) + cross + cross.T
    row = lax.broadcasted_iota(jnp.int32, (PANEL, PANEL), 0)
    lane = lax.broadcasted_iota(jnp.int32, (PANEL, PANEL), 1)
    second = gram[PANEL:, PANEL:]
    pack[0:PANEL, :] = jnp.where(lane >= row, gram[:PANEL, :PANEL], second)
    pack[PANEL : 2 * PANEL, :] = gram[:PANEL, PANEL:]
    diagonal = jnp.sum(jnp.where(lane == row, second, 0.0), axis=0, keepdims=True)
    pack[2 * PANEL :, :] = jnp.broadcast_to(diagonal, (PACK - 2 * PANEL, PANEL))


def split(x, terms):
    out = []
    for _ in range(terms):
        part = x.astype(jnp.bfloat16)
        out.append(part)
        x = x - part.astype(jnp.float32)
    return out


PAIRS = ((0, 0), (0, 1), (1, 0), (1, 1), (0, 2), (2, 0))


def factor(gram):
    n = gram.shape[0]
    eye = lax.broadcasted_iota(jnp.int32, (n, n), 0) == lax.broadcasted_iota(jnp.int32, (n, n), 1)
    picked = jnp.where(eye, gram, 0.0)
    diagonal = jnp.sum(picked, axis=0, keepdims=True)
    inverse_row = lax.rsqrt(diagonal)
    inverse_col = lax.rsqrt(jnp.sum(picked, axis=1, keepdims=True))
    gram = gram * inverse_row * inverse_col

    sub = lax.broadcasted_iota(jnp.int32, (8, n), 0)
    lane = lax.broadcasted_iota(jnp.int32, (8, n), 1)
    left = [gram[8 * i : 8 * i + 8] for i in range(n // 8)]
    right = [(lane == sub + 8 * i).astype(jnp.float32) for i in range(n // 8)]

    def row(x, k):
        return jnp.broadcast_to(x[k : k + 1], x.shape)

    for first in range(0, n // 8, STEP):
        last = first + STEP
        for b in range(first, last):
            cols = {
                t: [jnp.broadcast_to(left[t][:, 8 * b + k : 8 * b + k + 1], (8, n)) for k in range(8)]
                for t in range(b, last)
            }
            for k in range(0, 8, 2):
                p, q, r = row(cols[b][k], k), row(cols[b][k], k + 1), row(cols[b][k + 1], k + 1)
                root_p = lax.rsqrt(p)
                ratio = q * root_p
                det = p * r - q * q
                root_r = lax.rsqrt(det) * (p * root_p)
                one = {t: cols[t][k] * root_p for t in range(b, last)}
                two = {t: (cols[t][k + 1] - one[t] * ratio) * root_r for t in range(b, last)}
                for j in range(k + 2, 8):
                    u, v = row(one[b], j), row(two[b], j)
                    for t in range(b, last):
                        cols[t][j] = cols[t][j] - one[t] * u - two[t] * v
                below_one = jnp.where(sub > k + 1, one[b], 0.0)
                below_two = jnp.where(sub > k + 1, two[b], 0.0)
                for side in (left, right):
                    top = row(side[b], k) * root_p
                    low = (row(side[b], k + 1) - top * ratio) * root_r
                    rest = side[b] - below_one * top - below_two * low
                    side[b] = jnp.where(sub == k, top, jnp.where(sub == k + 1, low, rest))
                    for t in range(b + 1, last):
                        side[t] = side[t] - one[t] * top - two[t] * low
        if last < n // 8:
            u = split(jnp.concatenate(left[first:last], axis=0), 3)
            v = split(jnp.concatenate(right[first:last], axis=0), 3)
            lhs = jnp.concatenate([u[i] for i, _ in PAIRS], axis=0)
            rhs = jnp.concatenate(
                [jnp.concatenate([u[j] for _, j in PAIRS], axis=0), jnp.concatenate([v[j] for _, j in PAIRS], axis=0)],
                axis=1,
            )
            change = lax.dot_general(lhs, rhs, (((0,), (0,)), ((), ())), preferred_element_type=jnp.float32)
            for t in range(last, n // 8):
                left[t] = left[t] - change[8 * t : 8 * t + 8, :n]
                right[t] = right[t] - change[8 * t : 8 * t + 8, n:]
    upper = jnp.concatenate([jnp.where(lane >= sub + 8 * i, x, 0.0) for i, x in enumerate(left)], axis=0)
    return upper * (diagonal * inverse_row), jnp.concatenate(right, axis=0) * inverse_row


def dot3(a, b, dims):
    (ah, al), (bh, bl) = split(a, 2), split(b, 2)
    dot = functools.partial(
        lax.dot_general, dimension_numbers=(dims, ((), ())), preferred_element_type=jnp.float32
    )
    return dot(ah, bh) + (dot(ah, bl) + dot(al, bh))


def full_dot(a, b, dims):
    return lax.dot_general(
        a, b, (dims, ((), ())), precision=lax.Precision.HIGHEST, preferred_element_type=jnp.float32
    )


NN, NT, TN = ((1,), (0,)), ((1,), (1,)), ((0,), (0,))


def tail_kernel(scale, core, mine_ref, other_ref, s_ref, basis_ref, upper_ref, pack):
    half = pack.shape[0] // 2
    c = core[0]
    pack[pl.ds(pl.multiple_of(c * half, 8), half), :] = mine_ref[...] * scale
    pack[pl.ds(pl.multiple_of((1 - c) * half, 8), half), :] = other_ref[...] * scale
    row = lax.broadcasted_iota(jnp.int32, (PANEL, PANEL), 0)
    lane = lax.broadcasted_iota(jnp.int32, (PANEL, PANEL), 1)
    both, cross = pack[0:PANEL, :], pack[PANEL : 2 * PANEL, :]
    turned = both.T
    gram_one = jnp.where(lane >= row, both, turned)
    diagonal = jnp.broadcast_to(pack[2 * PANEL : 2 * PANEL + 1, :], both.shape)
    gram_two = jnp.where(lane == row, diagonal, jnp.where(lane < row, both, turned))
    upper_one, low_one = factor(gram_one)
    coupling = full_dot(low_one, cross, NN)
    upper_two, low_two = factor(gram_two - full_dot(coupling, coupling, TN))
    mixed = -full_dot(low_two, full_dot(coupling, low_one, TN), NN)
    zero = jnp.zeros_like(upper_one)
    upper_ref[0:PANEL, 0:PANEL] = upper_one
    upper_ref[0:PANEL, PANEL:] = coupling
    upper_ref[PANEL:, 0:PANEL] = zero
    upper_ref[PANEL:, PANEL:] = upper_two
    first, second = s_ref[:, 0:PANEL], s_ref[...]
    basis_ref[:, 0:PANEL] = dot3(first, low_one, NT)
    basis_ref[:, PANEL:] = dot3(second, jnp.concatenate([mixed, low_two], axis=1), NT)


def whole(shape):
    return pl.BlockSpec(shape, lambda *_: (0,) * len(shape))


def gather_row(value):
    bits = lax.axis_size("row").bit_length() - 1
    half = value.shape[0] // 2
    shards = {0: [value], 1: [exchange(value, "row", 1)]}
    for bit in reversed(range(1, bits)):
        for k, pieces in list(shards.items()):
            if k != 1:
                pieces = pieces if k else [value[:half], value[half:]]
                shards[k | 1 << bit] = [exchange(p, "row", 1 << bit) for p in pieces]
    return shards


def dense_sketch(gaussian_sketch, block_values, local_rows, local_cols, grid_rows, grid_cols):
    size_col = lax.axis_size("col")
    chips = size_col // 2
    shard_rows, width = gaussian_sketch.shape
    group = shard_rows // BS
    me = lax.axis_index("col")
    owner = local_rows // group
    peer_core = (owner + me) % 2
    near = ((owner // 2 ^ me // 2) + chips - 1) % chips
    place = ((1 - peer_core) * chips + near) * group + local_rows % group
    shard = (local_cols // group) ^ lax.axis_index("row")
    slots = place * grid_cols + shard * group + local_cols % group
    dense = scatter_blocks(slots, block_values, grid_rows * grid_cols)
    dense = dense.reshape(2 * chips, group, grid_cols, BS, BS)
    shards = gather_row(gaussian_sketch)
    relayed = [k for k in shards if k > 1]

    params = pltpu.CompilerParams(vmem_limit_bytes=12 * 2**20)
    flops = 2 * shard_rows * grid_cols * BS * width
    bytes_a = 2 * shard_rows * grid_cols * BS

    def cost(n):
        return pl.CostEstimate(flops=n * flops, bytes_accessed=n * bytes_a, transcendentals=0)

    held = pl.BlockSpec(memory_space=pltpu.VMEM)
    r_block = (1, shard_rows, width)
    def block(first):
        return pl.BlockSpec(r_block, lambda i: (i + first, 0, 0))

    def product(first, count, pieces, *added):
        starts, refs = zip(*pieces)
        return pl.pallas_call(
            functools.partial(product_kernel, first, starts),
            grid=(count,),
            in_specs=[held] * (len(refs) + 1) + [block(first)] * len(added),
            out_specs=block(0),
            out_shape=jax.ShapeDtypeStruct((count, shard_rows, width), jnp.float32),
            compiler_params=params,
            cost_estimate=cost(count),
        )(dense, *refs, *added)

    def placed(k, h, piece):
        return (k * group + (h * group // 2), piece)

    late, sums, now = [], [], [placed(k, 0, shards[k][0]) for k in (0, 1)]
    for h in range(2 if relayed else 1):
        for k in relayed:
            piece, dense, *sums = lax.optimization_barrier((shards[k][h], dense, *sums))
            late.append(placed(k + 1, h, exchange(piece, "row", 1)))
            now.append(placed(k, h, piece))
        sums = [product(0, 2 * chips, now, *sums)]
        now = []
    first_sum = sums[0]
    parts = [(0, chips // 2), (chips // 2, chips - chips // 2)]
    def finish(first, count):
        if late:
            return product(first, count, late, first_sum)
        return first_sum[first : first + count]

    peer = [exchange(finish(at, n), "col", 1) for at, n in parts]
    near = [finish(chips + at, n) for at, n in parts]
    sent = jax.ShapeDtypeStruct((shard_rows + 16, width), jnp.int16)
    kept = jax.ShapeDtypeStruct((shard_rows, width), jnp.float32)
    terms = []
    for (at, n), mine, theirs in zip(parts, near, peer):
        shapes = [kept if at + i == chips - 1 else sent for i in range(n)]
        done = pl.pallas_call(
            code_kernel,
            grid=(n,),
            in_specs=[block(0), block(0)],
            out_specs=[whole(x.shape) for x in shapes],
            out_shape=shapes,
            compiler_params=params,
        )(mine, theirs)
        for i, x in enumerate(done):
            terms.append(x if x.dtype == jnp.float32 else exchange(x, "col", 2 * (at + i + 1)))
    return terms


def tile_product(sketch_blocks, block_values, local_rows, local_cols, tile_rows):
    group_size = math.gcd(block_values.shape[0], 64)
    col_width = sketch_blocks.shape[2]

    def advance(counter, summed):
        offset = (counter * group_size).astype(jnp.int32)
        values = lax.dynamic_slice_in_dim(block_values, offset, group_size, 0)
        row_ids = lax.dynamic_slice_in_dim(local_rows, offset, group_size, 0)
        col_ids = lax.dynamic_slice_in_dim(local_cols, offset, group_size, 0)
        picked = jnp.take(sketch_blocks, col_ids, axis=0)
        product = jnp.einsum("gab,gbs->gas", values, picked, preferred_element_type=jnp.float32)
        return summed.at[row_ids].add(product)

    initial = jnp.zeros((tile_rows, block_values.shape[1], col_width), jnp.float32)
    summed = lax.fori_loop(0, block_values.shape[0] // group_size, advance, initial)
    return summed.reshape(tile_rows * block_values.shape[1], col_width)


def looped_sketch(gaussian_sketch, block_values, local_rows, local_cols, grid_rows, grid_cols):
    gathered = lax.all_gather(gaussian_sketch, "row", axis=0, tiled=True)
    sketch_blocks = gathered.reshape(grid_cols, BS, gathered.shape[1])
    partial_value = tile_product(sketch_blocks, block_values, local_rows, local_cols, grid_rows)
    return [lax.psum_scatter(partial_value, "col", scatter_dimension=0, tiled=True)]


def direct_sum(value, axis, low_bit, bits):
    terms = {0: value}
    for mask in reversed(range(1, 2**bits)):
        terms[mask] = exchange(value, axis, mask << low_bit)
    terms = [terms[mask] for mask in range(2**bits)]
    while len(terms) > 1:
        terms = [a + b for a, b in zip(terms[0::2], terms[1::2])]
    return terms[0]


def sum_over_axis(value, axis, low_bit):
    bits = lax.axis_size(axis).bit_length() - 1
    while low_bit < bits:
        take = min(2, bits - low_bit)
        value = direct_sum(value, axis, low_bit, take)
        low_bit += take
    return value


def sum_over_mesh(mine, other, core):
    mine = mine + exchange(other, "col", 1)
    mine = sum_over_axis(mine, "col", 1)
    mine = sum_over_axis(mine, "row", 0)
    return mine, exchange(mine, "col", 1)


def on_device(gaussian_sketch, block_values, block_rows, block_columns):
    size_row = lax.axis_size("row")
    size_col = lax.axis_size("col")
    shard_rows, width = gaussian_sketch.shape
    grid_rows = shard_rows * size_col // BS
    grid_cols = shard_rows * size_row // BS
    local_rows = block_rows - lax.axis_index("row") * grid_rows
    local_cols = block_columns - lax.axis_index("col") * grid_cols
    dense = 2 * grid_rows * grid_cols * BS * BS <= DENSE_BYTES
    sketch = dense_sketch if dense else looped_sketch
    terms = sketch(
        gaussian_sketch, block_values, local_rows, local_cols, grid_rows, grid_cols
    )
    core = lax.axis_index("col") % 2
    half = jax.ShapeDtypeStruct((PACK // 2, PANEL), jnp.float32)
    sketched, mine, other = pl.pallas_call(
        reduce_kernel,
        grid_spec=pltpu.PrefetchScalarGridSpec(
            num_scalar_prefetch=1,
            grid=(1,),
            in_specs=[whole(t.shape) for t in terms],
            out_specs=[whole((shard_rows, width)), whole(half.shape), whole(half.shape)],
            scratch_shapes=[pltpu.VMEM((PACK, PANEL), jnp.float32)],
        ),
        out_shape=[jax.ShapeDtypeStruct((shard_rows, width), jnp.float32), half, half],
        compiler_params=pltpu.CompilerParams(vmem_limit_bytes=12 * 2**20),
    )(core.reshape(1), *terms)
    order_total = shard_rows * size_row * size_col
    mine, other = sum_over_mesh(mine, other, core)
    range_basis, upper_factor = pl.pallas_call(
        functools.partial(tail_kernel, 1.0 / order_total),
        grid_spec=pltpu.PrefetchScalarGridSpec(
            num_scalar_prefetch=1,
            grid=(1,),
            in_specs=[whole(half.shape), whole(half.shape), whole(sketched.shape)],
            out_specs=[whole(sketched.shape), whole((width, width))],
            scratch_shapes=[pltpu.VMEM((PACK, PANEL), jnp.float32)],
        ),
        out_shape=[
            jax.ShapeDtypeStruct(sketched.shape, jnp.float32),
            jax.ShapeDtypeStruct((width, width), jnp.float32),
        ],
        compiler_params=pltpu.CompilerParams(vmem_limit_bytes=16 * 2**20),
    )(core.reshape(1), mine, other, sketched)
    return (range_basis, upper_factor)


def solution(mesh):
    return jax.shard_map(
        on_device,
        mesh=mesh,
        in_specs=(
            P(("col", "row"), None),
            P(("row", "col"), None, None),
            P(("row", "col")),
            P(("row", "col")),
        ),
        out_specs=(P(("row", "col"), None), P()),
        check_vma=False,
    )
```

```python
import functools
import math

import jax
import jax.numpy as jnp
from jax import lax
from jax.experimental import pallas as pl
from jax.experimental.pallas import tpu as pltpu
from jax.sharding import PartitionSpec as P

PANEL = 128
BS = 128
LEVELS = 32700.0
OCTAVE = 64.0
DENSE_BYTES = 32 * 2**20
STEP = 4
PACK = 2 * PANEL + 16
TOP = PANEL // 2
REST = PACK // 2 - TOP


def exchange(value, axis, mask):
    size = lax.axis_size(axis)
    return lax.ppermute(value, axis, [(i, i ^ mask) for i in range(size)])


def scatter_kernel(slots, values, dense, sem):
    step = math.gcd(8, math.gcd(dense.shape[0], values.shape[0]))

    @pl.loop(0, dense.shape[0] // step)
    def _(s):
        dense[pl.ds(s * step, step)] = jnp.zeros((step, *dense.shape[1:]), dense.dtype)

    @pl.loop(0, values.shape[0] // step)
    def _(b):
        for u in range(step):
            block = b * step + u
            pltpu.make_async_copy(values.at[block], dense.at[slots[block]], sem).start()

    pltpu.make_async_copy(values, values, sem).wait()


def scatter_blocks(slots, values, n_slots):
    return pl.pallas_call(
        scatter_kernel,
        out_shape=pltpu.VMEM((n_slots, BS, BS), values.dtype),
        grid_spec=pltpu.PrefetchScalarGridSpec(
            num_scalar_prefetch=1,
            grid=(),
            in_specs=[pl.BlockSpec(memory_space=pltpu.HBM)],
            out_specs=pl.BlockSpec(memory_space=pltpu.VMEM),
            scratch_shapes=[pltpu.SemaphoreType.DMA],
        ),
        compiler_params=pltpu.CompilerParams(vmem_limit_bytes=4 * 2**20),
        cost_estimate=pl.CostEstimate(flops=0, bytes_accessed=24 * 2**20, transcendentals=0),
    )(slots, pltpu.with_memory_space_constraint(values, pltpu.HBM))


def dense_dot(a_ref, x_refs, shards, chunk):
    group = a_ref.shape[1]
    total = None
    for k, x_ref in zip(shards, x_refs):
        lhs = jnp.concatenate(
            [
                jnp.concatenate([a_ref[chunk, r, k * group + c] for c in range(group)], axis=1)
                for r in range(group)
            ],
            axis=0,
        )
        part = jnp.dot(lhs, x_ref[...], preferred_element_type=jnp.float32)
        total = part if total is None else total + part
    return total


def product_kernel(first, shards, a_ref, *refs):
    *in_refs, o_ref = refs
    total = dense_dot(a_ref, in_refs, shards, pl.program_id(0) + first)
    added = in_refs[len(shards) :]
    o_ref[0] = total + added[0][0] if added else total


def quantize(total, o_ref):
    n = total.shape[0] // BS
    width = total.shape[1]
    row = lax.broadcasted_iota(jnp.int32, (16, width), 0)
    tail = jnp.zeros((16, width), jnp.float32)
    for b in range(n):
        part = total[b * BS : (b + 1) * BS]
        top = jnp.maximum(jnp.max(jnp.abs(part), axis=0, keepdims=True), 1e-30)
        step = jnp.ceil(jnp.log(top) * (OCTAVE / math.log(2.0)))
        scaled = part * (jnp.exp(step * (-math.log(2.0) / OCTAVE)) * LEVELS)
        o_ref[b * BS : (b + 1) * BS, :] = jnp.round(scaled).astype(jnp.int32).astype(jnp.int16)
        tail = jnp.where(row == b, jnp.broadcast_to(step, tail.shape), tail)
    o_ref[n * BS :, :] = tail.astype(jnp.int32).astype(jnp.int16)


def dequantize(q_ref):
    n = (q_ref.shape[0] - 16) // BS
    tail = q_ref[n * BS :, :].astype(jnp.int32).astype(jnp.float32)
    parts = []
    for b in range(n):
        scale = jnp.exp(tail[b : b + 1] * (math.log(2.0) / OCTAVE)) * (1.0 / LEVELS)
        parts.append(q_ref[b * BS : (b + 1) * BS, :].astype(jnp.int32).astype(jnp.float32) * scale)
    return jnp.concatenate(parts, axis=0)


def code_kernel(a_ref, b_ref, *o_refs):
    total = a_ref[0] + b_ref[0]
    for j, o_ref in enumerate(o_refs):

        @pl.when(pl.program_id(0) == j)
        def _(o_ref=o_ref):
            if o_ref.dtype == jnp.int16:
                quantize(total, o_ref)
            else:
                o_ref[...] = total


def reduce_kernel(core, *refs):
    *in_refs, s_ref, mine_ref, other_ref, pack = refs
    total = None
    for ref in in_refs:
        term = dequantize(ref) if ref.dtype == jnp.int16 else ref[...]
        total = term if total is None else total + term
    s_ref[...] = total
    gram_store(total, pack)
    for ref, c in ((mine_ref, core[0]), (other_ref, 1 - core[0])):
        ref[:TOP, :] = pack[pl.ds(pl.multiple_of(c * TOP, 8), TOP), :]
        ref[TOP:, :] = pack[pl.ds(pl.multiple_of(2 * TOP + c * REST, 8), REST), :]


def gram_store(total, pack):
    high = total.astype(jnp.bfloat16)
    low = (total - high.astype(jnp.float32)).astype(jnp.bfloat16)
    dims = (((0,), (0,)), ((), ()))
    dot = functools.partial(lax.dot_general, dimension_numbers=dims, preferred_element_type=jnp.float32)
    cross = dot(high, low)
    gram = dot(high, high) + dot(low, low) + cross + cross.T
    row = lax.broadcasted_iota(jnp.int32, (PANEL, PANEL), 0)
    lane = lax.broadcasted_iota(jnp.int32, (PANEL, PANEL), 1)
    second = gram[PANEL:, PANEL:]
    pack[0:PANEL, :] = jnp.where(lane >= row, gram[:PANEL, :PANEL], second)
    pack[PANEL : 2 * PANEL, :] = gram[:PANEL, PANEL:]
    diagonal = jnp.sum(jnp.where(lane == row, second, 0.0), axis=0, keepdims=True)
    pack[2 * PANEL :, :] = jnp.broadcast_to(diagonal, (PACK - 2 * PANEL, PANEL))


def split(x, terms):
    out = []
    for _ in range(terms):
        part = x.astype(jnp.bfloat16)
        out.append(part)
        x = x - part.astype(jnp.float32)
    return out


PAIRS = ((0, 0), (0, 1), (1, 0), (1, 1), (0, 2), (2, 0))


def factor(gram):
    n = gram.shape[0]
    eye = lax.broadcasted_iota(jnp.int32, (n, n), 0) == lax.broadcasted_iota(jnp.int32, (n, n), 1)
    picked = jnp.where(eye, gram, 0.0)
    diagonal = jnp.sum(picked, axis=0, keepdims=True)
    inverse_row = lax.rsqrt(diagonal)
    inverse_col = lax.rsqrt(jnp.sum(picked, axis=1, keepdims=True))
    gram = gram * inverse_row * inverse_col

    sub = lax.broadcasted_iota(jnp.int32, (8, n), 0)
    lane = lax.broadcasted_iota(jnp.int32, (8, n), 1)
    left = [gram[8 * i : 8 * i + 8] for i in range(n // 8)]
    right = [(lane == sub + 8 * i).astype(jnp.float32) for i in range(n // 8)]

    def row(x, k):
        return jnp.broadcast_to(x[k : k + 1], x.shape)

    for first in range(0, n // 8, STEP):
        last = first + STEP
        for b in range(first, last):
            cols = {
                t: [jnp.broadcast_to(left[t][:, 8 * b + k : 8 * b + k + 1], (8, n)) for k in range(8)]
                for t in range(b, last)
            }
            for k in range(0, 8, 2):
                p, q, r = row(cols[b][k], k), row(cols[b][k], k + 1), row(cols[b][k + 1], k + 1)
                root_p = lax.rsqrt(p)
                ratio = q * root_p
                det = p * r - q * q
                root_r = lax.rsqrt(det) * (p * root_p)
                one = {t: cols[t][k] * root_p for t in range(b, last)}
                two = {t: (cols[t][k + 1] - one[t] * ratio) * root_r for t in range(b, last)}
                for j in range(k + 2, 8):
                    u, v = row(one[b], j), row(two[b], j)
                    for t in range(b, last):
                        cols[t][j] = cols[t][j] - one[t] * u - two[t] * v
                below_one = jnp.where(sub > k + 1, one[b], 0.0)
                below_two = jnp.where(sub > k + 1, two[b], 0.0)
                for side in (left, right):
                    top = row(side[b], k) * root_p
                    low = (row(side[b], k + 1) - top * ratio) * root_r
                    rest = side[b] - below_one * top - below_two * low
                    side[b] = jnp.where(sub == k, top, jnp.where(sub == k + 1, low, rest))
                    for t in range(b + 1, last):
                        side[t] = side[t] - one[t] * top - two[t] * low
        if last < n // 8:
            u = split(jnp.concatenate(left[first:last], axis=0), 3)
            v = split(jnp.concatenate(right[first:last], axis=0), 3)
            lhs = jnp.concatenate([u[i] for i, _ in PAIRS], axis=0)
            rhs = jnp.concatenate(
                [jnp.concatenate([u[j] for _, j in PAIRS], axis=0), jnp.concatenate([v[j] for _, j in PAIRS], axis=0)],
                axis=1,
            )
            change = lax.dot_general(lhs, rhs, (((0,), (0,)), ((), ())), preferred_element_type=jnp.float32)
            for t in range(last, n // 8):
                left[t] = left[t] - change[8 * t : 8 * t + 8, :n]
                right[t] = right[t] - change[8 * t : 8 * t + 8, n:]
    upper = jnp.concatenate([jnp.where(lane >= sub + 8 * i, x, 0.0) for i, x in enumerate(left)], axis=0)
    return upper * (diagonal * inverse_row), jnp.concatenate(right, axis=0) * inverse_row


def dot3(a, b, dims):
    (ah, al), (bh, bl) = split(a, 2), split(b, 2)
    dot = functools.partial(
        lax.dot_general, dimension_numbers=(dims, ((), ())), preferred_element_type=jnp.float32
    )
    return dot(ah, bh) + (dot(ah, bl) + dot(al, bh))


def full_dot(a, b, dims):
    return lax.dot_general(
        a, b, (dims, ((), ())), precision=lax.Precision.HIGHEST, preferred_element_type=jnp.float32
    )


NN, NT, TN = ((1,), (0,)), ((1,), (1,)), ((0,), (0,))


def joined(scale, core, mine_ref, other_ref, both):
    half = mine_ref.shape[0]
    both[pl.ds(pl.multiple_of(core[0] * half, 8), half), :] = mine_ref[...] * scale
    both[pl.ds(pl.multiple_of((1 - core[0]) * half, 8), half), :] = other_ref[...] * scale
    return both[...]


def place():
    row = lax.broadcasted_iota(jnp.int32, (PANEL, PANEL), 0)
    return row, lax.broadcasted_iota(jnp.int32, (PANEL, PANEL), 1)


def first_kernel(scale, core, mine_ref, other_ref, s_ref, upper_ref, low_ref, basis_ref, side_ref, both):
    triangles = joined(scale, core, mine_ref, other_ref, both)
    row, lane = place()
    turned = triangles.T
    upper_ref[...], low = factor(jnp.where(lane >= row, triangles, turned))
    low_ref[...] = low
    side_ref[...] = jnp.where(lane < row, triangles, turned)
    basis_ref[...] = dot3(s_ref[:, 0:PANEL], low, NT)


def second_kernel(
    scale, core, mine_ref, other_ref, s_ref, first_ref, low_ref, one_ref, side_ref, basis_ref, upper_ref, both
):
    rest = joined(scale, core, mine_ref, other_ref, both)
    row, lane = place()
    low_one = low_ref[...]
    coupling = full_dot(low_one, rest[:PANEL], NN)
    diagonal = jnp.broadcast_to(rest[PANEL : PANEL + 1], (PANEL, PANEL))
    gram_two = jnp.where(lane == row, diagonal, side_ref[...])
    upper_two, low_two = factor(gram_two - full_dot(coupling, coupling, TN))
    mixed = -full_dot(low_two, full_dot(coupling, low_one, TN), NN)
    upper_ref[0:PANEL, 0:PANEL] = first_ref[...]
    upper_ref[0:PANEL, PANEL:] = coupling
    upper_ref[PANEL:, 0:PANEL] = jnp.zeros_like(coupling)
    upper_ref[PANEL:, PANEL:] = upper_two
    basis_ref[:, 0:PANEL] = one_ref[...]
    basis_ref[:, PANEL:] = dot3(s_ref[...], jnp.concatenate([mixed, low_two], axis=1), NT)


def whole(shape):
    return pl.BlockSpec(shape, lambda *_: (0,) * len(shape))


def gather_row(value, ready):
    bits = lax.axis_size("row").bit_length() - 1
    shards = {0: value}
    for bit in reversed(range(bits)):
        for k, v in list(shards.items()):
            if bit == 0 and k:
                v, ready = lax.optimization_barrier((v, ready))
            shards[k | 1 << bit] = exchange(v, "row", 1 << bit)
    return [shards[k] for k in range(2**bits)], ready


def dense_sketch(gaussian_sketch, block_values, local_rows, local_cols, grid_rows, grid_cols):
    size_col = lax.axis_size("col")
    chips = size_col // 2
    shard_rows, width = gaussian_sketch.shape
    group = shard_rows // BS
    me = lax.axis_index("col")
    owner = local_rows // group
    peer_core = (owner + me) % 2
    near = ((owner // 2 ^ me // 2) + chips - 1) % chips
    place = ((1 - peer_core) * chips + near) * group + local_rows % group
    shard = (local_cols // group) ^ lax.axis_index("row")
    slots = place * grid_cols + shard * group + local_cols % group
    dense = scatter_blocks(slots, block_values, grid_rows * grid_cols)
    dense = dense.reshape(2 * chips, group, grid_cols, BS, BS)
    shards, dense = gather_row(gaussian_sketch, dense)
    late = [k for k in range(len(shards)) if k % 2 and k > 1]
    early = [k for k in range(len(shards)) if k not in late]

    params = pltpu.CompilerParams(vmem_limit_bytes=12 * 2**20)
    flops = 2 * shard_rows * grid_cols * BS * width
    bytes_a = 2 * shard_rows * grid_cols * BS

    def cost(n):
        return pl.CostEstimate(flops=n * flops, bytes_accessed=n * bytes_a, transcendentals=0)

    held = pl.BlockSpec(memory_space=pltpu.VMEM)
    r_block = (1, shard_rows, width)
    def block(first):
        return pl.BlockSpec(r_block, lambda i: (i + first, 0, 0))

    def product(first, count, chosen, *added):
        return pl.pallas_call(
            functools.partial(product_kernel, first, chosen),
            grid=(count,),
            in_specs=[held] * (len(chosen) + 1) + [block(first)] * len(added),
            out_specs=block(0),
            out_shape=jax.ShapeDtypeStruct((count, shard_rows, width), jnp.float32),
            compiler_params=params,
            cost_estimate=cost(count),
        )(dense, *[shards[k] for k in chosen], *added)

    first_sum = product(0, 2 * chips, early)
    parts = [(0, chips // 2), (chips // 2, chips - chips // 2)]
    peer = [exchange(product(at, n, late, first_sum), "col", 1) for at, n in parts]
    near = [product(chips + at, n, late, first_sum) for at, n in parts]
    sent = jax.ShapeDtypeStruct((shard_rows + 16, width), jnp.int16)
    kept = jax.ShapeDtypeStruct((shard_rows, width), jnp.float32)
    terms = []
    for (at, n), mine, theirs in zip(parts, near, peer):
        shapes = [kept if at + i == chips - 1 else sent for i in range(n)]
        done = pl.pallas_call(
            code_kernel,
            grid=(n,),
            in_specs=[block(0), block(0)],
            out_specs=[whole(x.shape) for x in shapes],
            out_shape=shapes,
            compiler_params=params,
        )(mine, theirs)
        for i, x in enumerate(done):
            terms.append(x if x.dtype == jnp.float32 else exchange(x, "col", 2 * (at + i + 1)))
    return terms


def tile_product(sketch_blocks, block_values, local_rows, local_cols, tile_rows):
    group_size = math.gcd(block_values.shape[0], 64)
    col_width = sketch_blocks.shape[2]

    def advance(counter, summed):
        offset = (counter * group_size).astype(jnp.int32)
        values = lax.dynamic_slice_in_dim(block_values, offset, group_size, 0)
        row_ids = lax.dynamic_slice_in_dim(local_rows, offset, group_size, 0)
        col_ids = lax.dynamic_slice_in_dim(local_cols, offset, group_size, 0)
        picked = jnp.take(sketch_blocks, col_ids, axis=0)
        product = jnp.einsum("gab,gbs->gas", values, picked, preferred_element_type=jnp.float32)
        return summed.at[row_ids].add(product)

    initial = jnp.zeros((tile_rows, block_values.shape[1], col_width), jnp.float32)
    summed = lax.fori_loop(0, block_values.shape[0] // group_size, advance, initial)
    return summed.reshape(tile_rows * block_values.shape[1], col_width)


def looped_sketch(gaussian_sketch, block_values, local_rows, local_cols, grid_rows, grid_cols):
    gathered = lax.all_gather(gaussian_sketch, "row", axis=0, tiled=True)
    sketch_blocks = gathered.reshape(grid_cols, BS, gathered.shape[1])
    partial_value = tile_product(sketch_blocks, block_values, local_rows, local_cols, grid_rows)
    return [lax.psum_scatter(partial_value, "col", scatter_dimension=0, tiled=True)]


def direct_terms(value, axis, low_bit, bits):
    terms = {0: value}
    for mask in reversed(range(1, 2**bits)):
        terms[mask] = exchange(value, axis, mask << low_bit)
    return [terms[mask] for mask in range(2**bits)]


def pair_sum(terms):
    while len(terms) > 1:
        terms = [a + b for a, b in zip(terms[0::2], terms[1::2])]
    return terms[0]


def axis_terms(value, axis, low_bit):
    bits = lax.axis_size(axis).bit_length() - 1
    while bits - low_bit > 2:
        value = pair_sum(direct_terms(value, axis, low_bit, 2))
        low_bit += 2
    return direct_terms(value, axis, low_bit, bits - low_bit)


def finish_sum(terms):
    value = pair_sum(terms)
    return value, exchange(value, "col", 1)


def on_device(gaussian_sketch, block_values, block_rows, block_columns):
    size_row = lax.axis_size("row")
    size_col = lax.axis_size("col")
    shard_rows, width = gaussian_sketch.shape
    grid_rows = shard_rows * size_col // BS
    grid_cols = shard_rows * size_row // BS
    local_rows = block_rows - lax.axis_index("row") * grid_rows
    local_cols = block_columns - lax.axis_index("col") * grid_cols
    dense = 2 * grid_rows * grid_cols * BS * BS <= DENSE_BYTES
    sketch = dense_sketch if dense else looped_sketch
    terms = sketch(
        gaussian_sketch, block_values, local_rows, local_cols, grid_rows, grid_cols
    )
    core = lax.axis_index("col") % 2
    half = jax.ShapeDtypeStruct((PACK // 2, PANEL), jnp.float32)
    sketched, mine, other = pl.pallas_call(
        reduce_kernel,
        grid_spec=pltpu.PrefetchScalarGridSpec(
            num_scalar_prefetch=1,
            grid=(1,),
            in_specs=[whole(t.shape) for t in terms],
            out_specs=[whole((shard_rows, width)), whole(half.shape), whole(half.shape)],
            scratch_shapes=[pltpu.VMEM((PACK, PANEL), jnp.float32)],
        ),
        out_shape=[jax.ShapeDtypeStruct((shard_rows, width), jnp.float32), half, half],
        compiler_params=pltpu.CompilerParams(vmem_limit_bytes=12 * 2**20),
    )(core.reshape(1), *terms)
    order_total = shard_rows * size_row * size_col
    mine = mine + exchange(other, "col", 1)
    mine = pair_sum(axis_terms(mine, "col", 1))
    triangles = finish_sum(axis_terms(mine[:TOP], "row", 0))
    rest = axis_terms(mine[TOP:], "row", 0)
    square = jax.ShapeDtypeStruct((PANEL, PANEL), jnp.float32)
    one = jax.ShapeDtypeStruct((shard_rows, PANEL), jnp.float32)

    def solve(kernel, outs, rows, *args):
        return pl.pallas_call(
            functools.partial(kernel, 1.0 / order_total),
            grid_spec=pltpu.PrefetchScalarGridSpec(
                num_scalar_prefetch=1,
                grid=(1,),
                in_specs=[whole(x.shape) for x in args],
                out_specs=[whole(x.shape) for x in outs],
                scratch_shapes=[pltpu.VMEM((rows, PANEL), jnp.float32)],
            ),
            out_shape=outs,
            compiler_params=pltpu.CompilerParams(vmem_limit_bytes=12 * 2**20),
            cost_estimate=pl.CostEstimate(flops=2**32, bytes_accessed=2**21, transcendentals=0),
        )(core.reshape(1), *args)

    upper_one, low_one, basis_one, side = solve(
        first_kernel, [square, square, one, square], PANEL, *triangles, sketched
    )
    *rest, low_one = lax.optimization_barrier((*rest, low_one))
    range_basis, upper_factor = solve(
        second_kernel,
        [
            jax.ShapeDtypeStruct((shard_rows, width), jnp.float32),
            jax.ShapeDtypeStruct((width, width), jnp.float32),
        ],
        2 * REST,
        *finish_sum(rest),
        sketched,
        upper_one,
        low_one,
        basis_one,
        side,
    )
    return (range_basis, upper_factor)


def solution(mesh):
    return jax.shard_map(
        on_device,
        mesh=mesh,
        in_specs=(
            P(("col", "row"), None),
            P(("row", "col"), None, None),
            P(("row", "col")),
            P(("row", "col")),
        ),
        out_specs=(P(("row", "col"), None), P()),
        check_vma=False,
    )
```

```python
import functools
import math

import jax
import jax.numpy as jnp
from jax import lax
from jax.experimental import pallas as pl
from jax.experimental.pallas import tpu as pltpu
from jax.sharding import PartitionSpec as P

PANEL = 128
BS = 128
LEVELS = 32700.0
OCTAVE = 64.0
DENSE_BYTES = 32 * 2**20
STEP = 4
PACK = 2 * PANEL + 16


def exchange(value, axis, mask):
    size = lax.axis_size(axis)
    return lax.ppermute(value, axis, [(i, i ^ mask) for i in range(size)])


def scatter_kernel(slots, values, dense, sem):
    step = math.gcd(8, math.gcd(dense.shape[0], values.shape[0]))

    @pl.loop(0, dense.shape[0] // step)
    def _(s):
        dense[pl.ds(s * step, step)] = jnp.zeros((step, *dense.shape[1:]), dense.dtype)

    @pl.loop(0, values.shape[0] // step)
    def _(b):
        for u in range(step):
            block = b * step + u
            pltpu.make_async_copy(values.at[block], dense.at[slots[block]], sem).start()

    pltpu.make_async_copy(values, values, sem).wait()


def scatter_blocks(slots, values, n_slots):
    return pl.pallas_call(
        scatter_kernel,
        out_shape=pltpu.VMEM((n_slots, BS, BS), values.dtype),
        grid_spec=pltpu.PrefetchScalarGridSpec(
            num_scalar_prefetch=1,
            grid=(),
            in_specs=[pl.BlockSpec(memory_space=pltpu.HBM)],
            out_specs=pl.BlockSpec(memory_space=pltpu.VMEM),
            scratch_shapes=[pltpu.SemaphoreType.DMA],
        ),
        compiler_params=pltpu.CompilerParams(vmem_limit_bytes=4 * 2**20),
        cost_estimate=pl.CostEstimate(flops=0, bytes_accessed=24 * 2**20, transcendentals=0),
    )(slots, pltpu.with_memory_space_constraint(values, pltpu.HBM))


def dense_dot(a_ref, x_refs, shards, chunk):
    group = a_ref.shape[1]
    total = None
    for k, x_ref in zip(shards, x_refs):
        lhs = jnp.concatenate(
            [
                jnp.concatenate([a_ref[chunk, r, k * group + c] for c in range(group)], axis=1)
                for r in range(group)
            ],
            axis=0,
        )
        part = jnp.dot(lhs, x_ref[...], preferred_element_type=jnp.float32)
        total = part if total is None else total + part
    return total


def product_kernel(first, shards, a_ref, *refs):
    *in_refs, o_ref = refs
    total = dense_dot(a_ref, in_refs, shards, pl.program_id(0) + first)
    added = in_refs[len(shards) :]
    o_ref[0] = total + added[0][0] if added else total


def quantize(total, o_ref):
    n = total.shape[0] // BS
    width = total.shape[1]
    row = lax.broadcasted_iota(jnp.int32, (16, width), 0)
    tail = jnp.zeros((16, width), jnp.float32)
    for b in range(n):
        part = total[b * BS : (b + 1) * BS]
        top = jnp.maximum(jnp.max(jnp.abs(part), axis=0, keepdims=True), 1e-30)
        step = jnp.ceil(jnp.log(top) * (OCTAVE / math.log(2.0)))
        scaled = part * (jnp.exp(step * (-math.log(2.0) / OCTAVE)) * LEVELS)
        o_ref[b * BS : (b + 1) * BS, :] = jnp.round(scaled).astype(jnp.int32).astype(jnp.int16)
        tail = jnp.where(row == b, jnp.broadcast_to(step, tail.shape), tail)
    o_ref[n * BS :, :] = tail.astype(jnp.int32).astype(jnp.int16)


def dequantize(q_ref):
    n = (q_ref.shape[0] - 16) // BS
    tail = q_ref[n * BS :, :].astype(jnp.int32).astype(jnp.float32)
    parts = []
    for b in range(n):
        scale = jnp.exp(tail[b : b + 1] * (math.log(2.0) / OCTAVE)) * (1.0 / LEVELS)
        parts.append(q_ref[b * BS : (b + 1) * BS, :].astype(jnp.int32).astype(jnp.float32) * scale)
    return jnp.concatenate(parts, axis=0)


def code_kernel(a_ref, b_ref, *o_refs):
    total = a_ref[0] + b_ref[0]
    for j, o_ref in enumerate(o_refs):

        @pl.when(pl.program_id(0) == j)
        def _(o_ref=o_ref):
            if o_ref.dtype == jnp.int16:
                quantize(total, o_ref)
            else:
                o_ref[...] = total


def reduce_kernel(core, *refs):
    *in_refs, s_ref, mine_ref, other_ref, pack = refs
    total = None
    for ref in in_refs:
        term = dequantize(ref) if ref.dtype == jnp.int16 else ref[...]
        total = term if total is None else total + term
    s_ref[...] = total
    gram_store(total, pack)
    half = pack.shape[0] // 2
    c = core[0]
    mine_ref[...] = pack[pl.ds(pl.multiple_of(c * half, 8), half), :]
    other_ref[...] = pack[pl.ds(pl.multiple_of((1 - c) * half, 8), half), :]


def gram_store(total, pack):
    high = total.astype(jnp.bfloat16)
    low = (total - high.astype(jnp.float32)).astype(jnp.bfloat16)
    dims = (((0,), (0,)), ((), ()))
    dot = functools.partial(lax.dot_general, dimension_numbers=dims, preferred_element_type=jnp.float32)
    cross = dot(high, low)
    gram = dot(high, high) + dot(low, low) + cross + cross.T
    row = lax.broadcasted_iota(jnp.int32, (PANEL, PANEL), 0)
    lane = lax.broadcasted_iota(jnp.int32, (PANEL, PANEL), 1)
    second = gram[PANEL:, PANEL:]
    pack[0:PANEL, :] = jnp.where(lane >= row, gram[:PANEL, :PANEL], second)
    pack[PANEL : 2 * PANEL, :] = gram[:PANEL, PANEL:]
    diagonal = jnp.sum(jnp.where(lane == row, second, 0.0), axis=0, keepdims=True)
    pack[2 * PANEL :, :] = jnp.broadcast_to(diagonal, (PACK - 2 * PANEL, PANEL))


def split(x, terms):
    out = []
    for _ in range(terms):
        part = x.astype(jnp.bfloat16)
        out.append(part)
        x = x - part.astype(jnp.float32)
    return out


PAIRS = ((0, 0), (0, 1), (1, 0), (1, 1), (0, 2), (2, 0))


def factor(gram):
    n = gram.shape[0]
    eye = lax.broadcasted_iota(jnp.int32, (n, n), 0) == lax.broadcasted_iota(jnp.int32, (n, n), 1)
    picked = jnp.where(eye, gram, 0.0)
    diagonal = jnp.sum(picked, axis=0, keepdims=True)
    inverse_row = lax.rsqrt(diagonal)
    inverse_col = lax.rsqrt(jnp.sum(picked, axis=1, keepdims=True))
    gram = gram * inverse_row * inverse_col

    sub = lax.broadcasted_iota(jnp.int32, (8, n), 0)
    lane = lax.broadcasted_iota(jnp.int32, (8, n), 1)
    left = [gram[8 * i : 8 * i + 8] for i in range(n // 8)]
    right = [(lane == sub + 8 * i).astype(jnp.float32) for i in range(n // 8)]

    def row(x, k):
        return jnp.broadcast_to(x[k : k + 1], x.shape)

    for first in range(0, n // 8, STEP):
        last = first + STEP
        for b in range(first, last):
            cols = {
                t: [jnp.broadcast_to(left[t][:, 8 * b + k : 8 * b + k + 1], (8, n)) for k in range(8)]
                for t in range(b, last)
            }
            for k in range(0, 8, 2):
                p, q, r = row(cols[b][k], k), row(cols[b][k], k + 1), row(cols[b][k + 1], k + 1)
                root_p = lax.rsqrt(p)
                ratio = q * root_p
                det = p * r - q * q
                root_r = lax.rsqrt(det) * (p * root_p)
                one = {t: cols[t][k] * root_p for t in range(b, last)}
                two = {t: (cols[t][k + 1] - one[t] * ratio) * root_r for t in range(b, last)}
                for j in range(k + 2, 8):
                    u, v = row(one[b], j), row(two[b], j)
                    for t in range(b, last):
                        cols[t][j] = cols[t][j] - one[t] * u - two[t] * v
                below_one = jnp.where(sub > k + 1, one[b], 0.0)
                below_two = jnp.where(sub > k + 1, two[b], 0.0)
                for side in (left, right):
                    top = row(side[b], k) * root_p
                    low = (row(side[b], k + 1) - top * ratio) * root_r
                    rest = side[b] - below_one * top - below_two * low
                    side[b] = jnp.where(sub == k, top, jnp.where(sub == k + 1, low, rest))
                    for t in range(b + 1, last):
                        side[t] = side[t] - one[t] * top - two[t] * low
        if last < n // 8:
            u = split(jnp.concatenate(left[first:last], axis=0), 3)
            v = split(jnp.concatenate(right[first:last], axis=0), 3)
            lhs = jnp.concatenate([u[i] for i, _ in PAIRS], axis=0)
            rhs = jnp.concatenate(
                [jnp.concatenate([u[j] for _, j in PAIRS], axis=0), jnp.concatenate([v[j] for _, j in PAIRS], axis=0)],
                axis=1,
            )
            change = lax.dot_general(lhs, rhs, (((0,), (0,)), ((), ())), preferred_element_type=jnp.float32)
            for t in range(last, n // 8):
                left[t] = left[t] - change[8 * t : 8 * t + 8, :n]
                right[t] = right[t] - change[8 * t : 8 * t + 8, n:]
    upper = jnp.concatenate([jnp.where(lane >= sub + 8 * i, x, 0.0) for i, x in enumerate(left)], axis=0)
    return upper * (diagonal * inverse_row), jnp.concatenate(right, axis=0) * inverse_row


def dot3(a, b, dims):
    (ah, al), (bh, bl) = split(a, 2), split(b, 2)
    dot = functools.partial(
        lax.dot_general, dimension_numbers=(dims, ((), ())), preferred_element_type=jnp.float32
    )
    return dot(ah, bh) + (dot(ah, bl) + dot(al, bh))


def full_dot(a, b, dims):
    return lax.dot_general(
        a, b, (dims, ((), ())), precision=lax.Precision.HIGHEST, preferred_element_type=jnp.float32
    )


NN, NT, TN = ((1,), (0,)), ((1,), (1,)), ((0,), (0,))


def tail_kernel(scale, core, mine_ref, other_ref, s_ref, basis_ref, upper_ref, pack):
    half = pack.shape[0] // 2
    c = core[0]
    pack[pl.ds(pl.multiple_of(c * half, 8), half), :] = mine_ref[...] * scale
    pack[pl.ds(pl.multiple_of((1 - c) * half, 8), half), :] = other_ref[...] * scale
    row = lax.broadcasted_iota(jnp.int32, (PANEL, PANEL), 0)
    lane = lax.broadcasted_iota(jnp.int32, (PANEL, PANEL), 1)
    both, cross = pack[0:PANEL, :], pack[PANEL : 2 * PANEL, :]
    turned = both.T
    gram_one = jnp.where(lane >= row, both, turned)
    diagonal = jnp.broadcast_to(pack[2 * PANEL : 2 * PANEL + 1, :], both.shape)
    gram_two = jnp.where(lane == row, diagonal, jnp.where(lane < row, both, turned))
    upper_one, low_one = factor(gram_one)
    coupling = full_dot(low_one, cross, NN)
    basis_one = dot3(s_ref[:, 0:PANEL], low_one, NT)
    basis_ref[:, 0:PANEL] = basis_one
    remainder = s_ref[:, PANEL:] - dot3(basis_one, coupling, NN)
    upper_two, low_two = factor(gram_two - full_dot(coupling, coupling, TN))
    upper_ref[0:PANEL, 0:PANEL] = upper_one
    upper_ref[0:PANEL, PANEL:] = coupling
    upper_ref[PANEL:, 0:PANEL] = jnp.zeros_like(upper_one)
    upper_ref[PANEL:, PANEL:] = upper_two
    basis_ref[:, PANEL:] = dot3(remainder, low_two, NT)


def whole(shape):
    return pl.BlockSpec(shape, lambda *_: (0,) * len(shape))


def gather_row(value, ready):
    bits = lax.axis_size("row").bit_length() - 1
    shards = {0: value}
    for bit in reversed(range(bits)):
        for k, v in list(shards.items()):
            if bit == 0 and k:
                v, ready = lax.optimization_barrier((v, ready))
            shards[k | 1 << bit] = exchange(v, "row", 1 << bit)
    return [shards[k] for k in range(2**bits)], ready


def dense_sketch(gaussian_sketch, block_values, local_rows, local_cols, grid_rows, grid_cols):
    size_col = lax.axis_size("col")
    chips = size_col // 2
    shard_rows, width = gaussian_sketch.shape
    group = shard_rows // BS
    me = lax.axis_index("col")
    owner = local_rows // group
    peer_core = (owner + me) % 2
    near = ((owner // 2 ^ me // 2) + chips - 1) % chips
    place = ((1 - peer_core) * chips + near) * group + local_rows % group
    shard = (local_cols // group) ^ lax.axis_index("row")
    slots = place * grid_cols + shard * group + local_cols % group
    dense = scatter_blocks(slots, block_values, grid_rows * grid_cols)
    dense = dense.reshape(2 * chips, group, grid_cols, BS, BS)
    shards, dense = gather_row(gaussian_sketch, dense)
    late = [k for k in range(len(shards)) if k % 2 and k > 1]
    early = [k for k in range(len(shards)) if k not in late]

    params = pltpu.CompilerParams(vmem_limit_bytes=12 * 2**20)
    flops = 2 * shard_rows * grid_cols * BS * width
    bytes_a = 2 * shard_rows * grid_cols * BS

    def cost(n):
        return pl.CostEstimate(flops=n * flops, bytes_accessed=n * bytes_a, transcendentals=0)

    held = pl.BlockSpec(memory_space=pltpu.VMEM)
    r_block = (1, shard_rows, width)
    def block(first):
        return pl.BlockSpec(r_block, lambda i: (i + first, 0, 0))

    def product(first, count, chosen, *added):
        return pl.pallas_call(
            functools.partial(product_kernel, first, chosen),
            grid=(count,),
            in_specs=[held] * (len(chosen) + 1) + [block(first)] * len(added),
            out_specs=block(0),
            out_shape=jax.ShapeDtypeStruct((count, shard_rows, width), jnp.float32),
            compiler_params=params,
            cost_estimate=cost(count),
        )(dense, *[shards[k] for k in chosen], *added)

    first_sum = product(0, 2 * chips, early)
    parts = [(0, chips // 2), (chips // 2, chips - chips // 2)]
    peer = [exchange(product(at, n, late, first_sum), "col", 1) for at, n in parts]
    near = [product(chips + at, n, late, first_sum) for at, n in parts]
    sent = jax.ShapeDtypeStruct((shard_rows + 16, width), jnp.int16)
    kept = jax.ShapeDtypeStruct((shard_rows, width), jnp.float32)
    terms = []
    for (at, n), mine, theirs in zip(parts, near, peer):
        shapes = [kept if at + i == chips - 1 else sent for i in range(n)]
        done = pl.pallas_call(
            code_kernel,
            grid=(n,),
            in_specs=[block(0), block(0)],
            out_specs=[whole(x.shape) for x in shapes],
            out_shape=shapes,
            compiler_params=params,
        )(mine, theirs)
        for i, x in enumerate(done):
            terms.append(x if x.dtype == jnp.float32 else exchange(x, "col", 2 * (at + i + 1)))
    return terms


def tile_product(sketch_blocks, block_values, local_rows, local_cols, tile_rows):
    group_size = math.gcd(block_values.shape[0], 64)
    col_width = sketch_blocks.shape[2]

    def advance(counter, summed):
        offset = (counter * group_size).astype(jnp.int32)
        values = lax.dynamic_slice_in_dim(block_values, offset, group_size, 0)
        row_ids = lax.dynamic_slice_in_dim(local_rows, offset, group_size, 0)
        col_ids = lax.dynamic_slice_in_dim(local_cols, offset, group_size, 0)
        picked = jnp.take(sketch_blocks, col_ids, axis=0)
        product = jnp.einsum("gab,gbs->gas", values, picked, preferred_element_type=jnp.float32)
        return summed.at[row_ids].add(product)

    initial = jnp.zeros((tile_rows, block_values.shape[1], col_width), jnp.float32)
    summed = lax.fori_loop(0, block_values.shape[0] // group_size, advance, initial)
    return summed.reshape(tile_rows * block_values.shape[1], col_width)


def looped_sketch(gaussian_sketch, block_values, local_rows, local_cols, grid_rows, grid_cols):
    gathered = lax.all_gather(gaussian_sketch, "row", axis=0, tiled=True)
    sketch_blocks = gathered.reshape(grid_cols, BS, gathered.shape[1])
    partial_value = tile_product(sketch_blocks, block_values, local_rows, local_cols, grid_rows)
    return [lax.psum_scatter(partial_value, "col", scatter_dimension=0, tiled=True)]


def direct_sum(value, axis, low_bit, bits):
    t = [value] + [exchange(value, axis, mask << low_bit) for mask in range(1, 2**bits)]
    if bits == 1:
        return t[0] + t[1]
    if axis == "col":
        return (t[2] + t[3]) + (t[0] + t[1])
    return (t[3] + t[2]) + (t[1] + t[0])


def sum_over_axis(value, axis, low_bit):
    bits = lax.axis_size(axis).bit_length() - 1
    while low_bit < bits:
        take = min(2, bits - low_bit)
        value = direct_sum(value, axis, low_bit, take)
        low_bit += take
    return value


def sum_over_mesh(mine, other, core):
    mine = mine + exchange(other, "col", 1)
    mine = sum_over_axis(mine, "col", 1)
    mine = sum_over_axis(mine, "row", 0)
    return mine, exchange(mine, "col", 1)


def on_device(gaussian_sketch, block_values, block_rows, block_columns):
    size_row = lax.axis_size("row")
    size_col = lax.axis_size("col")
    shard_rows, width = gaussian_sketch.shape
    grid_rows = shard_rows * size_col // BS
    grid_cols = shard_rows * size_row // BS
    local_rows = block_rows - lax.axis_index("row") * grid_rows
    local_cols = block_columns - lax.axis_index("col") * grid_cols
    dense = 2 * grid_rows * grid_cols * BS * BS <= DENSE_BYTES
    sketch = dense_sketch if dense else looped_sketch
    terms = sketch(
        gaussian_sketch, block_values, local_rows, local_cols, grid_rows, grid_cols
    )
    core = lax.axis_index("col") % 2
    half = jax.ShapeDtypeStruct((PACK // 2, PANEL), jnp.float32)
    sketched, mine, other = pl.pallas_call(
        reduce_kernel,
        grid_spec=pltpu.PrefetchScalarGridSpec(
            num_scalar_prefetch=1,
            grid=(1,),
            in_specs=[whole(t.shape) for t in terms],
            out_specs=[whole((shard_rows, width)), whole(half.shape), whole(half.shape)],
            scratch_shapes=[pltpu.VMEM((PACK, PANEL), jnp.float32)],
        ),
        out_shape=[jax.ShapeDtypeStruct((shard_rows, width), jnp.float32), half, half],
        compiler_params=pltpu.CompilerParams(vmem_limit_bytes=12 * 2**20),
    )(core.reshape(1), *terms)
    order_total = shard_rows * size_row * size_col
    mine, other = sum_over_mesh(mine, other, core)
    range_basis, upper_factor = pl.pallas_call(
        functools.partial(tail_kernel, 1.0 / order_total),
        grid_spec=pltpu.PrefetchScalarGridSpec(
            num_scalar_prefetch=1,
            grid=(1,),
            in_specs=[whole(half.shape), whole(half.shape), whole(sketched.shape)],
            out_specs=[whole(sketched.shape), whole((width, width))],
            scratch_shapes=[pltpu.VMEM((PACK, PANEL), jnp.float32)],
        ),
        out_shape=[
            jax.ShapeDtypeStruct(sketched.shape, jnp.float32),
            jax.ShapeDtypeStruct((width, width), jnp.float32),
        ],
        compiler_params=pltpu.CompilerParams(vmem_limit_bytes=16 * 2**20),
    )(core.reshape(1), mine, other, sketched)
    return (range_basis, upper_factor)


def solution(mesh):
    return jax.shard_map(
        on_device,
        mesh=mesh,
        in_specs=(
            P(("col", "row"), None),
            P(("row", "col"), None, None),
            P(("row", "col")),
            P(("row", "col")),
        ),
        out_specs=(P(("row", "col"), None), P()),
        check_vma=False,
    )
```

```python
import functools
import math

import jax
import jax.numpy as jnp
from jax import lax
from jax.experimental import pallas as pl
from jax.experimental.pallas import tpu as pltpu
from jax.sharding import PartitionSpec as P

PANEL = 128
BS = 128
LEVELS = 32700.0
OCTAVE = 64.0
DENSE_BYTES = 32 * 2**20
STEP = 8
PACK = 2 * PANEL + 16


def exchange(value, axis, mask):
    size = lax.axis_size(axis)
    return lax.ppermute(value, axis, [(i, i ^ mask) for i in range(size)])


def scatter_kernel(slots, values, dense, sem):
    step = math.gcd(8, math.gcd(dense.shape[0], values.shape[0]))

    @pl.loop(0, dense.shape[0] // step)
    def _(s):
        dense[pl.ds(s * step, step)] = jnp.zeros((step, *dense.shape[1:]), dense.dtype)

    @pl.loop(0, values.shape[0] // step)
    def _(b):
        for u in range(step):
            block = b * step + u
            pltpu.make_async_copy(values.at[block], dense.at[slots[block]], sem).start()

    pltpu.make_async_copy(values, values, sem).wait()


def scatter_blocks(slots, values, n_slots):
    return pl.pallas_call(
        scatter_kernel,
        out_shape=pltpu.VMEM((n_slots, BS, BS), values.dtype),
        grid_spec=pltpu.PrefetchScalarGridSpec(
            num_scalar_prefetch=1,
            grid=(),
            in_specs=[pl.BlockSpec(memory_space=pltpu.HBM)],
            out_specs=pl.BlockSpec(memory_space=pltpu.VMEM),
            scratch_shapes=[pltpu.SemaphoreType.DMA],
        ),
        compiler_params=pltpu.CompilerParams(vmem_limit_bytes=4 * 2**20),
        cost_estimate=pl.CostEstimate(flops=0, bytes_accessed=24 * 2**20, transcendentals=0),
    )(slots, pltpu.with_memory_space_constraint(values, pltpu.HBM))


def dense_dot(a_ref, x_refs, shards, chunk):
    group = a_ref.shape[1]
    total = None
    for k, x_ref in zip(shards, x_refs):
        lhs = jnp.concatenate(
            [
                jnp.concatenate([a_ref[chunk, r, k * group + c] for c in range(group)], axis=1)
                for r in range(group)
            ],
            axis=0,
        )
        part = jnp.dot(lhs, x_ref[...], preferred_element_type=jnp.float32)
        total = part if total is None else total + part
    return total


def product_kernel(first, shards, a_ref, *refs):
    *in_refs, o_ref = refs
    total = dense_dot(a_ref, in_refs, shards, pl.program_id(0) + first)
    added = in_refs[len(shards) :]
    o_ref[0] = total + added[0][0] if added else total


def quantize(total, o_ref):
    n = total.shape[0] // BS
    width = total.shape[1]
    row = lax.broadcasted_iota(jnp.int32, (16, width), 0)
    tail = jnp.zeros((16, width), jnp.float32)
    for b in range(n):
        part = total[b * BS : (b + 1) * BS]
        top = jnp.maximum(jnp.max(jnp.abs(part), axis=0, keepdims=True), 1e-30)
        step = jnp.ceil(jnp.log(top) * (OCTAVE / math.log(2.0)))
        scaled = part * (jnp.exp(step * (-math.log(2.0) / OCTAVE)) * LEVELS)
        o_ref[b * BS : (b + 1) * BS, :] = jnp.round(scaled).astype(jnp.int32).astype(jnp.int16)
        tail = jnp.where(row == b, jnp.broadcast_to(step, tail.shape), tail)
    o_ref[n * BS :, :] = tail.astype(jnp.int32).astype(jnp.int16)


def dequantize(q_ref):
    n = (q_ref.shape[0] - 16) // BS
    tail = q_ref[n * BS :, :].astype(jnp.int32).astype(jnp.float32)
    parts = []
    for b in range(n):
        scale = jnp.exp(tail[b : b + 1] * (math.log(2.0) / OCTAVE)) * (1.0 / LEVELS)
        parts.append(q_ref[b * BS : (b + 1) * BS, :].astype(jnp.int32).astype(jnp.float32) * scale)
    return jnp.concatenate(parts, axis=0)


def code_kernel(a_ref, b_ref, *o_refs):
    total = a_ref[0] + b_ref[0]
    for j, o_ref in enumerate(o_refs):

        @pl.when(pl.program_id(0) == j)
        def _(o_ref=o_ref):
            if o_ref.dtype == jnp.int16:
                quantize(total, o_ref)
            else:
                o_ref[...] = total


def reduce_kernel(core, *refs):
    *in_refs, s_ref, mine_ref, other_ref, pack = refs
    total = None
    for ref in in_refs:
        term = dequantize(ref) if ref.dtype == jnp.int16 else ref[...]
        total = term if total is None else total + term
    s_ref[...] = total
    gram_store(total, pack)
    half = pack.shape[0] // 2
    c = core[0]
    mine_ref[...] = pack[pl.ds(pl.multiple_of(c * half, 8), half), :]
    other_ref[...] = pack[pl.ds(pl.multiple_of((1 - c) * half, 8), half), :]


def gram_store(total, pack):
    high = total.astype(jnp.bfloat16)
    low = (total - high.astype(jnp.float32)).astype(jnp.bfloat16)
    dims = (((0,), (0,)), ((), ()))
    dot = functools.partial(lax.dot_general, dimension_numbers=dims, preferred_element_type=jnp.float32)
    cross = dot(high, low)
    gram = dot(high, high) + dot(low, low) + cross + cross.T
    row = lax.broadcasted_iota(jnp.int32, (PANEL, PANEL), 0)
    lane = lax.broadcasted_iota(jnp.int32, (PANEL, PANEL), 1)
    second = gram[PANEL:, PANEL:]
    pack[0:PANEL, :] = jnp.where(lane >= row, gram[:PANEL, :PANEL], second)
    pack[PANEL : 2 * PANEL, :] = gram[:PANEL, PANEL:]
    diagonal = jnp.sum(jnp.where(lane == row, second, 0.0), axis=0, keepdims=True)
    pack[2 * PANEL :, :] = jnp.broadcast_to(diagonal, (PACK - 2 * PANEL, PANEL))


def split(x, terms):
    out = []
    for _ in range(terms):
        part = x.astype(jnp.bfloat16)
        out.append(part)
        x = x - part.astype(jnp.float32)
    return out


PAIRS = ((0, 0), (0, 1), (1, 0), (1, 1), (0, 2), (2, 0))


def lane_copy(x, k):
    return jnp.take_along_axis(x, jnp.full(x.shape, k, jnp.int32), axis=1, mode="promise_in_bounds")


def factor(gram):
    n = gram.shape[0]
    eye = lax.broadcasted_iota(jnp.int32, (n, n), 0) == lax.broadcasted_iota(jnp.int32, (n, n), 1)
    picked = jnp.where(eye, gram, 0.0)
    diagonal = jnp.sum(picked, axis=0, keepdims=True)
    inverse_row = lax.rsqrt(diagonal)
    inverse_col = lax.rsqrt(jnp.sum(picked, axis=1, keepdims=True))
    gram = gram * inverse_row * inverse_col

    sub = lax.broadcasted_iota(jnp.int32, (8, n), 0)
    lane = lax.broadcasted_iota(jnp.int32, (8, n), 1)
    left = [gram[8 * i : 8 * i + 8] for i in range(n // 8)]
    right = [(lane == sub + 8 * i).astype(jnp.float32) for i in range(n // 8)]

    def row(x, k):
        return jnp.broadcast_to(x[k : k + 1], x.shape)

    for first in range(0, n // 8, STEP):
        last = first + STEP
        for b in range(first, last):
            cols = {
                t: [lane_copy(left[t], 8 * b + k) for k in range(8)]
                for t in range(b, last)
            }
            spread = {(i, j): row(cols[b][j], i) for j in range(8) for i in range(j, 8)}
            low, root = {}, {}
            for k in range(0, 8, 2):
                p, q, r = spread[k, k], spread[k + 1, k], spread[k + 1, k + 1]
                root[k] = lax.rsqrt(p)
                low[k + 1, k] = q * root[k]
                root[k + 1] = lax.rsqrt(p * r - q * q) * (p * root[k])
                for i in range(k + 2, 8):
                    low[i, k] = spread[i, k] * root[k]
                    low[i, k + 1] = (spread[i, k + 1] - low[i, k] * low[k + 1, k]) * root[k + 1]
                for j in range(k + 2, 8):
                    for i in range(j, 8):
                        spread[i, j] = spread[i, j] - low[i, k] * low[j, k] - low[i, k + 1] * low[j, k + 1]

            def solve(terms):
                done = []
                for k, term in enumerate(terms):
                    for j in range(k):
                        term = term - done[j] * low[k, j]
                    done.append(term * root[k])
                return done

            mult = {t: solve(cols[t]) for t in range(b + 1, last)}
            for side in (left, right):
                tops = solve([row(side[b], k) for k in range(8)])
                side[b] = tops[0]
                for k in range(1, 8):
                    side[b] = jnp.where(sub == k, tops[k], side[b])
                for t in range(b + 1, last):
                    for k in range(8):
                        side[t] = side[t] - mult[t][k] * tops[k]
        if last < n // 8:
            u = split(jnp.concatenate(left[first:last], axis=0), 3)
            v = split(jnp.concatenate(right[first:last], axis=0), 3)
            lhs = jnp.concatenate([u[i] for i, _ in PAIRS], axis=0)
            rhs = jnp.concatenate(
                [jnp.concatenate([u[j] for _, j in PAIRS], axis=0), jnp.concatenate([v[j] for _, j in PAIRS], axis=0)],
                axis=1,
            )
            change = lax.dot_general(lhs, rhs, (((0,), (0,)), ((), ())), preferred_element_type=jnp.float32)
            for t in range(last, n // 8):
                left[t] = left[t] - change[8 * t : 8 * t + 8, :n]
                right[t] = right[t] - change[8 * t : 8 * t + 8, n:]
    upper = jnp.concatenate([jnp.where(lane >= sub + 8 * i, x, 0.0) for i, x in enumerate(left)], axis=0)
    return upper * (diagonal * inverse_row), jnp.concatenate(right, axis=0) * inverse_row


def dot3(a, b, dims):
    (ah, al), (bh, bl) = split(a, 2), split(b, 2)
    dot = functools.partial(
        lax.dot_general, dimension_numbers=(dims, ((), ())), preferred_element_type=jnp.float32
    )
    return dot(ah, bh) + (dot(ah, bl) + dot(al, bh))


def full_dot(a, b, dims):
    return lax.dot_general(
        a, b, (dims, ((), ())), precision=lax.Precision.HIGHEST, preferred_element_type=jnp.float32
    )


NN, NT, TN = ((1,), (0,)), ((1,), (1,)), ((0,), (0,))


def tail_kernel(scale, core, mine_ref, other_ref, s_ref, basis_ref, upper_ref, pack):
    half = pack.shape[0] // 2
    c = core[0]
    pack[pl.ds(pl.multiple_of(c * half, 8), half), :] = mine_ref[...] * scale
    pack[pl.ds(pl.multiple_of((1 - c) * half, 8), half), :] = other_ref[...] * scale
    row = lax.broadcasted_iota(jnp.int32, (PANEL, PANEL), 0)
    lane = lax.broadcasted_iota(jnp.int32, (PANEL, PANEL), 1)
    both, cross = pack[0:PANEL, :], pack[PANEL : 2 * PANEL, :]
    turned = both.T
    gram_one = jnp.where(lane >= row, both, turned)
    diagonal = jnp.broadcast_to(pack[2 * PANEL : 2 * PANEL + 1, :], both.shape)
    gram_two = jnp.where(lane == row, diagonal, jnp.where(lane < row, both, turned))
    upper_one, low_one = factor(gram_one)
    coupling = full_dot(low_one, cross, NN)
    basis_one = dot3(s_ref[:, 0:PANEL], low_one, NT)
    basis_ref[:, 0:PANEL] = basis_one
    remainder = s_ref[:, PANEL:] - dot3(basis_one, coupling, NN)
    upper_two, low_two = factor(gram_two - full_dot(coupling, coupling, TN))
    upper_ref[0:PANEL, 0:PANEL] = upper_one
    upper_ref[0:PANEL, PANEL:] = coupling
    upper_ref[PANEL:, 0:PANEL] = jnp.zeros_like(upper_one)
    upper_ref[PANEL:, PANEL:] = upper_two
    basis_ref[:, PANEL:] = dot3(remainder, low_two, NT)


def whole(shape):
    return pl.BlockSpec(shape, lambda *_: (0,) * len(shape))


def gather_row(value, ready):
    bits = lax.axis_size("row").bit_length() - 1
    shards = {0: value}
    for bit in reversed(range(bits)):
        for k, v in list(shards.items()):
            if bit == 0 and k:
                v, ready = lax.optimization_barrier((v, ready))
            shards[k | 1 << bit] = exchange(v, "row", 1 << bit)
    return [shards[k] for k in range(2**bits)], ready


def dense_sketch(gaussian_sketch, block_values, local_rows, local_cols, grid_rows, grid_cols):
    size_col = lax.axis_size("col")
    chips = size_col // 2
    shard_rows, width = gaussian_sketch.shape
    group = shard_rows // BS
    me = lax.axis_index("col")
    owner = local_rows // group
    peer_core = (owner + me) % 2
    near = ((owner // 2 ^ me // 2) + chips - 1) % chips
    place = ((1 - peer_core) * chips + near) * group + local_rows % group
    shard = (local_cols // group) ^ lax.axis_index("row")
    slots = place * grid_cols + shard * group + local_cols % group
    dense = scatter_blocks(slots, block_values, grid_rows * grid_cols)
    dense = dense.reshape(2 * chips, group, grid_cols, BS, BS)
    shards, dense = gather_row(gaussian_sketch, dense)
    late = [k for k in range(len(shards)) if k % 2 and k > 1]
    early = [k for k in range(len(shards)) if k not in late]

    params = pltpu.CompilerParams(vmem_limit_bytes=12 * 2**20)
    flops = 2 * shard_rows * grid_cols * BS * width
    bytes_a = 2 * shard_rows * grid_cols * BS

    def cost(n):
        return pl.CostEstimate(flops=n * flops, bytes_accessed=n * bytes_a, transcendentals=0)

    held = pl.BlockSpec(memory_space=pltpu.VMEM)
    r_block = (1, shard_rows, width)
    def block(first):
        return pl.BlockSpec(r_block, lambda i: (i + first, 0, 0))

    def product(first, count, chosen, *added):
        return pl.pallas_call(
            functools.partial(product_kernel, first, chosen),
            grid=(count,),
            in_specs=[held] * (len(chosen) + 1) + [block(first)] * len(added),
            out_specs=block(0),
            out_shape=jax.ShapeDtypeStruct((count, shard_rows, width), jnp.float32),
            compiler_params=params,
            cost_estimate=cost(count),
        )(dense, *[shards[k] for k in chosen], *added)

    first_sum = product(0, 2 * chips, early)
    parts = [(0, chips // 2), (chips // 2, chips - chips // 2)]
    peer = [exchange(product(at, n, late, first_sum), "col", 1) for at, n in parts]
    near = [product(chips + at, n, late, first_sum) for at, n in parts]
    sent = jax.ShapeDtypeStruct((shard_rows + 16, width), jnp.int16)
    kept = jax.ShapeDtypeStruct((shard_rows, width), jnp.float32)
    terms = []
    for (at, n), mine, theirs in zip(parts, near, peer):
        shapes = [kept if at + i == chips - 1 else sent for i in range(n)]
        done = pl.pallas_call(
            code_kernel,
            grid=(n,),
            in_specs=[block(0), block(0)],
            out_specs=[whole(x.shape) for x in shapes],
            out_shape=shapes,
            compiler_params=params,
        )(mine, theirs)
        for i, x in enumerate(done):
            terms.append(x if x.dtype == jnp.float32 else exchange(x, "col", 2 * (at + i + 1)))
    return terms


def tile_product(sketch_blocks, block_values, local_rows, local_cols, tile_rows):
    group_size = math.gcd(block_values.shape[0], 64)
    col_width = sketch_blocks.shape[2]

    def advance(counter, summed):
        offset = (counter * group_size).astype(jnp.int32)
        values = lax.dynamic_slice_in_dim(block_values, offset, group_size, 0)
        row_ids = lax.dynamic_slice_in_dim(local_rows, offset, group_size, 0)
        col_ids = lax.dynamic_slice_in_dim(local_cols, offset, group_size, 0)
        picked = jnp.take(sketch_blocks, col_ids, axis=0)
        product = jnp.einsum("gab,gbs->gas", values, picked, preferred_element_type=jnp.float32)
        return summed.at[row_ids].add(product)

    initial = jnp.zeros((tile_rows, block_values.shape[1], col_width), jnp.float32)
    summed = lax.fori_loop(0, block_values.shape[0] // group_size, advance, initial)
    return summed.reshape(tile_rows * block_values.shape[1], col_width)


def looped_sketch(gaussian_sketch, block_values, local_rows, local_cols, grid_rows, grid_cols):
    gathered = lax.all_gather(gaussian_sketch, "row", axis=0, tiled=True)
    sketch_blocks = gathered.reshape(grid_cols, BS, gathered.shape[1])
    partial_value = tile_product(sketch_blocks, block_values, local_rows, local_cols, grid_rows)
    return [lax.psum_scatter(partial_value, "col", scatter_dimension=0, tiled=True)]


def direct_sum(value, axis, low_bit, bits):
    t = [value] + [exchange(value, axis, mask << low_bit) for mask in range(1, 2**bits)]
    if bits == 1:
        return t[0] + t[1]
    if axis == "col":
        return (t[2] + t[3]) + (t[0] + t[1])
    return (t[3] + t[2]) + (t[1] + t[0])


def sum_over_axis(value, axis, low_bit):
    bits = lax.axis_size(axis).bit_length() - 1
    while low_bit < bits:
        take = min(2, bits - low_bit)
        value = direct_sum(value, axis, low_bit, take)
        low_bit += take
    return value


def sum_over_mesh(mine, other, core):
    mine = mine + exchange(other, "col", 1)
    mine = sum_over_axis(mine, "col", 1)
    mine = sum_over_axis(mine, "row", 0)
    return mine, exchange(mine, "col", 1)


def on_device(gaussian_sketch, block_values, block_rows, block_columns):
    size_row = lax.axis_size("row")
    size_col = lax.axis_size("col")
    shard_rows, width = gaussian_sketch.shape
    grid_rows = shard_rows * size_col // BS
    grid_cols = shard_rows * size_row // BS
    local_rows = block_rows - lax.axis_index("row") * grid_rows
    local_cols = block_columns - lax.axis_index("col") * grid_cols
    dense = 2 * grid_rows * grid_cols * BS * BS <= DENSE_BYTES
    sketch = dense_sketch if dense else looped_sketch
    terms = sketch(
        gaussian_sketch, block_values, local_rows, local_cols, grid_rows, grid_cols
    )
    core = lax.axis_index("col") % 2
    half = jax.ShapeDtypeStruct((PACK // 2, PANEL), jnp.float32)
    sketched, mine, other = pl.pallas_call(
        reduce_kernel,
        grid_spec=pltpu.PrefetchScalarGridSpec(
            num_scalar_prefetch=1,
            grid=(1,),
            in_specs=[whole(t.shape) for t in terms],
            out_specs=[whole((shard_rows, width)), whole(half.shape), whole(half.shape)],
            scratch_shapes=[pltpu.VMEM((PACK, PANEL), jnp.float32)],
        ),
        out_shape=[jax.ShapeDtypeStruct((shard_rows, width), jnp.float32), half, half],
        compiler_params=pltpu.CompilerParams(vmem_limit_bytes=12 * 2**20),
    )(core.reshape(1), *terms)
    order_total = shard_rows * size_row * size_col
    mine, other = sum_over_mesh(mine, other, core)
    range_basis, upper_factor = pl.pallas_call(
        functools.partial(tail_kernel, 1.0 / order_total),
        grid_spec=pltpu.PrefetchScalarGridSpec(
            num_scalar_prefetch=1,
            grid=(1,),
            in_specs=[whole(half.shape), whole(half.shape), whole(sketched.shape)],
            out_specs=[whole(sketched.shape), whole((width, width))],
            scratch_shapes=[pltpu.VMEM((PACK, PANEL), jnp.float32)],
        ),
        out_shape=[
            jax.ShapeDtypeStruct(sketched.shape, jnp.float32),
            jax.ShapeDtypeStruct((width, width), jnp.float32),
        ],
        compiler_params=pltpu.CompilerParams(vmem_limit_bytes=16 * 2**20),
    )(core.reshape(1), mine, other, sketched)
    return (range_basis, upper_factor)


def solution(mesh):
    return jax.shard_map(
        on_device,
        mesh=mesh,
        in_specs=(
            P(("col", "row"), None),
            P(("row", "col"), None, None),
            P(("row", "col")),
            P(("row", "col")),
        ),
        out_specs=(P(("row", "col"), None), P()),
        check_vma=False,
    )
```

```python
import functools
import math

import jax
import jax.numpy as jnp
from jax import lax
from jax.experimental import pallas as pl
from jax.experimental.pallas import tpu as pltpu
from jax.sharding import PartitionSpec as P

PANEL = 128
BS = 128
LEVELS = 32700.0
OCTAVE = 64.0
DENSE_BYTES = 32 * 2**20
STEP = 8
PACK = 2 * PANEL + 16


def exchange(value, axis, mask):
    size = lax.axis_size(axis)
    return lax.ppermute(value, axis, [(i, i ^ mask) for i in range(size)])


def scatter_kernel(slots, values, dense, sem):
    step = math.gcd(8, math.gcd(dense.shape[0], values.shape[0]))

    @pl.loop(0, dense.shape[0] // step)
    def _(s):
        dense[pl.ds(s * step, step)] = jnp.zeros((step, *dense.shape[1:]), dense.dtype)

    @pl.loop(0, values.shape[0] // step)
    def _(b):
        for u in range(step):
            block = b * step + u
            pltpu.make_async_copy(values.at[block], dense.at[slots[block]], sem).start()

    pltpu.make_async_copy(values, values, sem).wait()


def scatter_blocks(slots, values, n_slots):
    return pl.pallas_call(
        scatter_kernel,
        out_shape=pltpu.VMEM((n_slots, BS, BS), values.dtype),
        grid_spec=pltpu.PrefetchScalarGridSpec(
            num_scalar_prefetch=1,
            grid=(),
            in_specs=[pl.BlockSpec(memory_space=pltpu.HBM)],
            out_specs=pl.BlockSpec(memory_space=pltpu.VMEM),
            scratch_shapes=[pltpu.SemaphoreType.DMA],
        ),
        compiler_params=pltpu.CompilerParams(vmem_limit_bytes=4 * 2**20),
        cost_estimate=pl.CostEstimate(flops=0, bytes_accessed=24 * 2**20, transcendentals=0),
    )(slots, pltpu.with_memory_space_constraint(values, pltpu.HBM))


def dense_dot(a_ref, x_refs, shards, chunk):
    group = a_ref.shape[1]
    total = None
    for k, x_ref in zip(shards, x_refs):
        lhs = jnp.concatenate(
            [
                jnp.concatenate([a_ref[chunk, r, k * group + c] for c in range(group)], axis=1)
                for r in range(group)
            ],
            axis=0,
        )
        part = jnp.dot(lhs, x_ref[...], preferred_element_type=jnp.float32)
        total = part if total is None else total + part
    return total


def product_kernel(first, shards, a_ref, *refs):
    *in_refs, o_ref = refs
    total = dense_dot(a_ref, in_refs, shards, pl.program_id(0) + first)
    added = in_refs[len(shards) :]
    o_ref[0] = total + added[0][0] if added else total


def quantize(total, o_ref):
    n = total.shape[0] // BS
    width = total.shape[1]
    row = lax.broadcasted_iota(jnp.int32, (16, width), 0)
    tail = jnp.zeros((16, width), jnp.float32)
    for b in range(n):
        part = total[b * BS : (b + 1) * BS]
        top = jnp.maximum(jnp.max(jnp.abs(part), axis=0, keepdims=True), 1e-30)
        step = jnp.ceil(jnp.log(top) * (OCTAVE / math.log(2.0)))
        scaled = part * (jnp.exp(step * (-math.log(2.0) / OCTAVE)) * LEVELS)
        o_ref[b * BS : (b + 1) * BS, :] = jnp.round(scaled).astype(jnp.int32).astype(jnp.int16)
        tail = jnp.where(row == b, jnp.broadcast_to(step, tail.shape), tail)
    o_ref[n * BS :, :] = tail.astype(jnp.int32).astype(jnp.int16)


def dequantize(q_ref):
    n = (q_ref.shape[0] - 16) // BS
    tail = q_ref[n * BS :, :].astype(jnp.int32).astype(jnp.float32)
    parts = []
    for b in range(n):
        scale = jnp.exp(tail[b : b + 1] * (math.log(2.0) / OCTAVE)) * (1.0 / LEVELS)
        parts.append(q_ref[b * BS : (b + 1) * BS, :].astype(jnp.int32).astype(jnp.float32) * scale)
    return jnp.concatenate(parts, axis=0)


def code_kernel(a_ref, b_ref, *o_refs):
    total = a_ref[0] + b_ref[0]
    for j, o_ref in enumerate(o_refs):

        @pl.when(pl.program_id(0) == j)
        def _(o_ref=o_ref):
            if o_ref.dtype == jnp.int16:
                quantize(total, o_ref)
            else:
                o_ref[...] = total


def reduce_kernel(core, *refs):
    *in_refs, s_ref, mine_ref, other_ref, pack = refs
    total = None
    for ref in in_refs:
        term = dequantize(ref) if ref.dtype == jnp.int16 else ref[...]
        total = term if total is None else total + term
    s_ref[...] = total
    gram_store(total, pack)
    half = pack.shape[0] // 2
    c = core[0]
    mine_ref[...] = pack[pl.ds(pl.multiple_of(c * half, 8), half), :]
    other_ref[...] = pack[pl.ds(pl.multiple_of((1 - c) * half, 8), half), :]


def gram_store(total, pack):
    high = total.astype(jnp.bfloat16)
    low = (total - high.astype(jnp.float32)).astype(jnp.bfloat16)
    dims = (((0,), (0,)), ((), ()))
    dot = functools.partial(lax.dot_general, dimension_numbers=dims, preferred_element_type=jnp.float32)
    cross = dot(high, low)
    gram = dot(high, high) + dot(low, low) + cross + cross.T
    row = lax.broadcasted_iota(jnp.int32, (PANEL, PANEL), 0)
    lane = lax.broadcasted_iota(jnp.int32, (PANEL, PANEL), 1)
    second = gram[PANEL:, PANEL:]
    pack[0:PANEL, :] = jnp.where(lane >= row, gram[:PANEL, :PANEL], second)
    pack[PANEL : 2 * PANEL, :] = gram[:PANEL, PANEL:]
    diagonal = jnp.sum(jnp.where(lane == row, second, 0.0), axis=0, keepdims=True)
    pack[2 * PANEL :, :] = jnp.broadcast_to(diagonal, (PACK - 2 * PANEL, PANEL))


def split(x, terms):
    out = []
    for _ in range(terms):
        part = x.astype(jnp.bfloat16)
        out.append(part)
        x = x - part.astype(jnp.float32)
    return out


PAIRS = ((0, 0), (0, 1), (1, 0), (1, 1), (0, 2), (2, 0))


def lane_copy(x, k):
    return jnp.take_along_axis(x, jnp.full(x.shape, k, jnp.int32), axis=1, mode="promise_in_bounds")


def factor(gram):
    n = gram.shape[0]
    eye = lax.broadcasted_iota(jnp.int32, (n, n), 0) == lax.broadcasted_iota(jnp.int32, (n, n), 1)
    picked = jnp.where(eye, gram, 0.0)
    diagonal = jnp.sum(picked, axis=0, keepdims=True)
    inverse_row = lax.rsqrt(diagonal)
    inverse_col = lax.rsqrt(jnp.sum(picked, axis=1, keepdims=True))
    gram = gram * inverse_row * inverse_col

    sub = lax.broadcasted_iota(jnp.int32, (8, n), 0)
    lane = lax.broadcasted_iota(jnp.int32, (8, n), 1)
    left = [gram[8 * i : 8 * i + 8] for i in range(n // 8)]
    right = [(lane == sub + 8 * i).astype(jnp.float32) for i in range(n // 8)]

    def row(x, k):
        return jnp.broadcast_to(x[k : k + 1], x.shape)

    for first in range(0, n // 8, STEP):
        last = first + STEP
        for b in range(first, last):
            cols = {
                t: [lane_copy(left[t], 8 * b + k) for k in range(8)]
                for t in range(b, last)
            }
            spread = {(i, j): row(cols[b][j], i) for j in range(8) for i in range(j, 8)}
            low, root = {}, {}
            for k in range(0, 8, 2):
                p, q, r = spread[k, k], spread[k + 1, k], spread[k + 1, k + 1]
                root[k] = lax.rsqrt(p)
                low[k + 1, k] = q * root[k]
                root[k + 1] = lax.rsqrt(p * r - q * q) * (p * root[k])
                for i in range(k + 2, 8):
                    low[i, k] = spread[i, k] * root[k]
                    low[i, k + 1] = (spread[i, k + 1] - low[i, k] * low[k + 1, k]) * root[k + 1]
                for j in range(k + 2, 8):
                    for i in range(j, 8):
                        spread[i, j] = spread[i, j] - low[i, k] * low[j, k] - low[i, k + 1] * low[j, k + 1]

            def solve(terms):
                done = []
                for k, term in enumerate(terms):
                    for j in range(k):
                        term = term - done[j] * low[k, j]
                    done.append(term * root[k])
                return done

            mult = {t: solve(cols[t]) for t in range(b + 1, last)}
            for side in (left, right):
                tops = solve([row(side[b], k) for k in range(8)])
                side[b] = tops[0]
                for k in range(1, 8):
                    side[b] = jnp.where(sub == k, tops[k], side[b])
                for t in range(b + 1, last):
                    for k in range(8):
                        side[t] = side[t] - mult[t][k] * tops[k]
        if last < n // 8:
            u = split(jnp.concatenate(left[first:last], axis=0), 3)
            v = split(jnp.concatenate(right[first:last], axis=0), 3)
            lhs = jnp.concatenate([u[i] for i, _ in PAIRS], axis=0)
            rhs = jnp.concatenate(
                [jnp.concatenate([u[j] for _, j in PAIRS], axis=0), jnp.concatenate([v[j] for _, j in PAIRS], axis=0)],
                axis=1,
            )
            change = lax.dot_general(lhs, rhs, (((0,), (0,)), ((), ())), preferred_element_type=jnp.float32)
            for t in range(last, n // 8):
                left[t] = left[t] - change[8 * t : 8 * t + 8, :n]
                right[t] = right[t] - change[8 * t : 8 * t + 8, n:]
    upper = jnp.concatenate([jnp.where(lane >= sub + 8 * i, x, 0.0) for i, x in enumerate(left)], axis=0)
    return upper * (diagonal * inverse_row), jnp.concatenate(right, axis=0) * inverse_row


def dot3(a, b, dims):
    (ah, al), (bh, bl) = split(a, 2), split(b, 2)
    dot = functools.partial(
        lax.dot_general, dimension_numbers=(dims, ((), ())), preferred_element_type=jnp.float32
    )
    return dot(ah, bh) + (dot(ah, bl) + dot(al, bh))


def full_dot(a, b, dims):
    return lax.dot_general(
        a, b, (dims, ((), ())), precision=lax.Precision.HIGHEST, preferred_element_type=jnp.float32
    )


NN, NT, TN = ((1,), (0,)), ((1,), (1,)), ((0,), (0,))


def tail_kernel(scale, core, mine_ref, other_ref, s_ref, basis_ref, upper_ref, pack):
    half = pack.shape[0] // 2
    c = core[0]
    pack[pl.ds(pl.multiple_of(c * half, 8), half), :] = mine_ref[...] * scale
    pack[pl.ds(pl.multiple_of((1 - c) * half, 8), half), :] = other_ref[...] * scale
    row = lax.broadcasted_iota(jnp.int32, (PANEL, PANEL), 0)
    lane = lax.broadcasted_iota(jnp.int32, (PANEL, PANEL), 1)
    both, cross = pack[0:PANEL, :], pack[PANEL : 2 * PANEL, :]
    turned = both.T
    gram_one = jnp.where(lane >= row, both, turned)
    diagonal = jnp.broadcast_to(pack[2 * PANEL : 2 * PANEL + 1, :], both.shape)
    gram_two = jnp.where(lane == row, diagonal, jnp.where(lane < row, both, turned))
    upper_one, low_one = factor(gram_one)
    coupling = full_dot(low_one, cross, NN)
    basis_one = dot3(s_ref[:, 0:PANEL], low_one, NT)
    basis_ref[:, 0:PANEL] = basis_one
    remainder = s_ref[:, PANEL:] - dot3(basis_one, coupling, NN)
    upper_two, low_two = factor(gram_two - full_dot(coupling, coupling, TN))
    upper_ref[0:PANEL, 0:PANEL] = upper_one
    upper_ref[0:PANEL, PANEL:] = coupling
    upper_ref[PANEL:, 0:PANEL] = jnp.zeros_like(upper_one)
    upper_ref[PANEL:, PANEL:] = upper_two
    basis_ref[:, PANEL:] = dot3(remainder, low_two, NT)


def whole(shape):
    return pl.BlockSpec(shape, lambda *_: (0,) * len(shape))


def gather_row(value, ready):
    bits = lax.axis_size("row").bit_length() - 1
    shards = {0: value}
    for bit in reversed(range(bits)):
        for k, v in list(shards.items()):
            if bit == 0 and k:
                v, ready = lax.optimization_barrier((v, ready))
            shards[k | 1 << bit] = exchange(v, "row", 1 << bit)
    return [shards[k] for k in range(2**bits)], ready


def dense_sketch(gaussian_sketch, block_values, local_rows, local_cols, grid_rows, grid_cols):
    size_col = lax.axis_size("col")
    chips = size_col // 2
    shard_rows, width = gaussian_sketch.shape
    group = shard_rows // BS
    me = lax.axis_index("col")
    owner = local_rows // group
    peer_core = (owner + me) % 2
    near = ((owner // 2 ^ me // 2) + chips - 1) % chips
    place = ((1 - peer_core) * chips + near) * group + local_rows % group
    shard = (local_cols // group) ^ lax.axis_index("row")
    slots = place * grid_cols + shard * group + local_cols % group
    dense = scatter_blocks(slots, block_values, grid_rows * grid_cols)
    dense = dense.reshape(2 * chips, group, grid_cols, BS, BS)
    shards, dense = gather_row(gaussian_sketch, dense)
    late = [k for k in range(len(shards)) if k % 2 and k > 1]
    early = [k for k in range(len(shards)) if k not in late]

    params = pltpu.CompilerParams(vmem_limit_bytes=12 * 2**20)
    flops = 2 * shard_rows * grid_cols * BS * width
    bytes_a = 2 * shard_rows * grid_cols * BS

    def cost(n):
        return pl.CostEstimate(flops=n * flops, bytes_accessed=n * bytes_a, transcendentals=0)

    held = pl.BlockSpec(memory_space=pltpu.VMEM)
    r_block = (1, shard_rows, width)
    def block(first):
        return pl.BlockSpec(r_block, lambda i: (i + first, 0, 0))

    def product(first, count, chosen, *added):
        return pl.pallas_call(
            functools.partial(product_kernel, first, chosen),
            grid=(count,),
            in_specs=[held] * (len(chosen) + 1) + [block(first)] * len(added),
            out_specs=block(0),
            out_shape=jax.ShapeDtypeStruct((count, shard_rows, width), jnp.float32),
            compiler_params=params,
            cost_estimate=cost(count),
        )(dense, *[shards[k] for k in chosen], *added)

    first_sum = product(0, 2 * chips, early)
    parts = [(0, chips // 2), (chips // 2, chips - chips // 2)]
    peer = [exchange(product(at, n, late, first_sum), "col", 1) for at, n in parts]
    near = [product(chips + at, n, late, first_sum) for at, n in parts]
    sent = jax.ShapeDtypeStruct((shard_rows + 16, width), jnp.int16)
    kept = jax.ShapeDtypeStruct((shard_rows, width), jnp.float32)
    terms = []
    for (at, n), mine, theirs in zip(parts, near, peer):
        shapes = [kept if at + i == chips - 1 else sent for i in range(n)]
        done = pl.pallas_call(
            code_kernel,
            grid=(n,),
            in_specs=[block(0), block(0)],
            out_specs=[whole(x.shape) for x in shapes],
            out_shape=shapes,
            compiler_params=params,
        )(mine, theirs)
        for i, x in enumerate(done):
            terms.append(x if x.dtype == jnp.float32 else exchange(x, "col", 2 * (at + i + 1)))
    return terms


def tile_product(sketch_blocks, block_values, local_rows, local_cols, tile_rows):
    group_size = math.gcd(block_values.shape[0], 64)
    col_width = sketch_blocks.shape[2]

    def advance(counter, summed):
        offset = (counter * group_size).astype(jnp.int32)
        values = lax.dynamic_slice_in_dim(block_values, offset, group_size, 0)
        row_ids = lax.dynamic_slice_in_dim(local_rows, offset, group_size, 0)
        col_ids = lax.dynamic_slice_in_dim(local_cols, offset, group_size, 0)
        picked = jnp.take(sketch_blocks, col_ids, axis=0)
        product = jnp.einsum("gab,gbs->gas", values, picked, preferred_element_type=jnp.float32)
        return summed.at[row_ids].add(product)

    initial = jnp.zeros((tile_rows, block_values.shape[1], col_width), jnp.float32)
    summed = lax.fori_loop(0, block_values.shape[0] // group_size, advance, initial)
    return summed.reshape(tile_rows * block_values.shape[1], col_width)


def looped_sketch(gaussian_sketch, block_values, local_rows, local_cols, grid_rows, grid_cols):
    gathered = lax.all_gather(gaussian_sketch, "row", axis=0, tiled=True)
    sketch_blocks = gathered.reshape(grid_cols, BS, gathered.shape[1])
    partial_value = tile_product(sketch_blocks, block_values, local_rows, local_cols, grid_rows)
    return [lax.psum_scatter(partial_value, "col", scatter_dimension=0, tiled=True)]


def direct_sum(value, axis, low_bit, bits):
    t = [value] + [exchange(value, axis, mask << low_bit) for mask in range(1, 2**bits)]
    if bits == 1:
        return t[0] + t[1]
    return (t[2] + t[3]) + (t[0] + t[1])


def sum_over_axis(value, axis, low_bit):
    bits = lax.axis_size(axis).bit_length() - 1
    while low_bit < bits:
        take = min(2 if axis == "col" else 1, bits - low_bit)
        value = direct_sum(value, axis, low_bit, take)
        low_bit += take
    return value


def sum_over_mesh(mine, other, core):
    mine = mine + exchange(other, "col", 1)
    mine = sum_over_axis(mine, "col", 1)
    mine = sum_over_axis(mine, "row", 0)
    return mine, exchange(mine, "col", 1)


def on_device(gaussian_sketch, block_values, block_rows, block_columns):
    size_row = lax.axis_size("row")
    size_col = lax.axis_size("col")
    shard_rows, width = gaussian_sketch.shape
    grid_rows = shard_rows * size_col // BS
    grid_cols = shard_rows * size_row // BS
    local_rows = block_rows - lax.axis_index("row") * grid_rows
    local_cols = block_columns - lax.axis_index("col") * grid_cols
    dense = 2 * grid_rows * grid_cols * BS * BS <= DENSE_BYTES
    sketch = dense_sketch if dense else looped_sketch
    terms = sketch(
        gaussian_sketch, block_values, local_rows, local_cols, grid_rows, grid_cols
    )
    core = lax.axis_index("col") % 2
    half = jax.ShapeDtypeStruct((PACK // 2, PANEL), jnp.float32)
    sketched, mine, other = pl.pallas_call(
        reduce_kernel,
        grid_spec=pltpu.PrefetchScalarGridSpec(
            num_scalar_prefetch=1,
            grid=(1,),
            in_specs=[whole(t.shape) for t in terms],
            out_specs=[whole((shard_rows, width)), whole(half.shape), whole(half.shape)],
            scratch_shapes=[pltpu.VMEM((PACK, PANEL), jnp.float32)],
        ),
        out_shape=[jax.ShapeDtypeStruct((shard_rows, width), jnp.float32), half, half],
        compiler_params=pltpu.CompilerParams(vmem_limit_bytes=12 * 2**20),
    )(core.reshape(1), *terms)
    order_total = shard_rows * size_row * size_col
    mine, other = sum_over_mesh(mine, other, core)
    range_basis, upper_factor = pl.pallas_call(
        functools.partial(tail_kernel, 1.0 / order_total),
        grid_spec=pltpu.PrefetchScalarGridSpec(
            num_scalar_prefetch=1,
            grid=(1,),
            in_specs=[whole(half.shape), whole(half.shape), whole(sketched.shape)],
            out_specs=[whole(sketched.shape), whole((width, width))],
            scratch_shapes=[pltpu.VMEM((PACK, PANEL), jnp.float32)],
        ),
        out_shape=[
            jax.ShapeDtypeStruct(sketched.shape, jnp.float32),
            jax.ShapeDtypeStruct((width, width), jnp.float32),
        ],
        compiler_params=pltpu.CompilerParams(vmem_limit_bytes=16 * 2**20),
    )(core.reshape(1), mine, other, sketched)
    return (range_basis, upper_factor)


def solution(mesh):
    return jax.shard_map(
        on_device,
        mesh=mesh,
        in_specs=(
            P(("col", "row"), None),
            P(("row", "col"), None, None),
            P(("row", "col")),
            P(("row", "col")),
        ),
        out_specs=(P(("row", "col"), None), P()),
        check_vma=False,
    )
```

```python
import functools
import math

import jax
import jax.numpy as jnp
from jax import lax
from jax.experimental import pallas as pl
from jax.experimental.pallas import tpu as pltpu
from jax.sharding import PartitionSpec as P

PANEL = 128
BS = 128
LEVELS = 32700.0
OCTAVE = 64.0
DENSE_BYTES = 32 * 2**20
STEP = 8
PACK = 2 * PANEL + 16


def exchange(value, axis, mask):
    size = lax.axis_size(axis)
    return lax.ppermute(value, axis, [(i, i ^ mask) for i in range(size)])


def scatter_kernel(slots, values, dense, sem):
    step = math.gcd(8, math.gcd(dense.shape[0], values.shape[0]))

    @pl.loop(0, dense.shape[0] // step)
    def _(s):
        dense[pl.ds(s * step, step)] = jnp.zeros((step, *dense.shape[1:]), dense.dtype)

    @pl.loop(0, values.shape[0] // step)
    def _(b):
        for u in range(step):
            block = b * step + u
            pltpu.make_async_copy(values.at[block], dense.at[slots[block]], sem).start()

    pltpu.make_async_copy(values, values, sem).wait()


def scatter_blocks(slots, values, n_slots):
    return pl.pallas_call(
        scatter_kernel,
        out_shape=pltpu.VMEM((n_slots, BS, BS), values.dtype),
        grid_spec=pltpu.PrefetchScalarGridSpec(
            num_scalar_prefetch=1,
            grid=(),
            in_specs=[pl.BlockSpec(memory_space=pltpu.HBM)],
            out_specs=pl.BlockSpec(memory_space=pltpu.VMEM),
            scratch_shapes=[pltpu.SemaphoreType.DMA],
        ),
        compiler_params=pltpu.CompilerParams(vmem_limit_bytes=4 * 2**20),
        cost_estimate=pl.CostEstimate(flops=0, bytes_accessed=24 * 2**20, transcendentals=0),
    )(slots, pltpu.with_memory_space_constraint(values, pltpu.HBM))


def dense_dot(a_ref, x_refs, shards, chunk):
    group = a_ref.shape[1]
    total = None
    for k, x_ref in zip(shards, x_refs):
        lhs = jnp.concatenate(
            [
                jnp.concatenate([a_ref[chunk, r, k * group + c] for c in range(group)], axis=1)
                for r in range(group)
            ],
            axis=0,
        )
        part = jnp.dot(lhs, x_ref[...], preferred_element_type=jnp.float32)
        total = part if total is None else total + part
    return total


def product_kernel(first, shards, a_ref, *refs):
    *in_refs, o_ref = refs
    total = dense_dot(a_ref, in_refs, shards, pl.program_id(0) + first)
    added = in_refs[len(shards) :]
    o_ref[0] = total + added[0][0] if added else total


def quantize(total, o_ref):
    n = total.shape[0] // BS
    width = total.shape[1]
    row = lax.broadcasted_iota(jnp.int32, (16, width), 0)
    tail = jnp.zeros((16, width), jnp.float32)
    for b in range(n):
        part = total[b * BS : (b + 1) * BS]
        top = jnp.maximum(jnp.max(jnp.abs(part), axis=0, keepdims=True), 1e-30)
        step = jnp.ceil(jnp.log(top) * (OCTAVE / math.log(2.0)))
        scaled = part * (jnp.exp(step * (-math.log(2.0) / OCTAVE)) * LEVELS)
        o_ref[b * BS : (b + 1) * BS, :] = jnp.round(scaled).astype(jnp.int32).astype(jnp.int16)
        tail = jnp.where(row == b, jnp.broadcast_to(step, tail.shape), tail)
    o_ref[n * BS :, :] = tail.astype(jnp.int32).astype(jnp.int16)


def dequantize(q_ref, first, count):
    rows = q_ref.shape[0] - 16
    tail = q_ref[rows:, :].astype(jnp.int32).astype(jnp.float32)
    parts = []
    for b in range(first, first + count):
        scale = jnp.exp(tail[b : b + 1] * (math.log(2.0) / OCTAVE)) * (1.0 / LEVELS)
        parts.append(q_ref[b * BS : (b + 1) * BS, :].astype(jnp.int32).astype(jnp.float32) * scale)
    return jnp.concatenate(parts, axis=0)


def code_x_kernel(a_ref, b_ref, q_ref, keep_ref, pass_ref):
    near, diagonal = a_ref[0] + b_ref[0], a_ref[1] + b_ref[1]
    quantize(jnp.concatenate([diagonal[:, :PANEL], near[:, :PANEL]], axis=0), q_ref)
    keep_ref[...] = near[:, PANEL:]
    pass_ref[...] = diagonal[:, PANEL:]


def code_y_kernel(a_ref, b_ref, pass_ref, q_ref, keep_ref, own_ref):
    near = a_ref[0] + b_ref[0]
    quantize(jnp.concatenate([pass_ref[...], near[:, PANEL:]], axis=0), q_ref)
    keep_ref[...] = near[:, :PANEL]
    own_ref[...] = a_ref[1] + b_ref[1]


def merge_kernel(keep_ref, q_ref, o_ref):
    quantize(keep_ref[...] + dequantize(q_ref, 0, keep_ref.shape[0] // BS), o_ref)


def all_terms(own_ref, x_ref=None, y_ref=None, late_y_ref=None, late_x_ref=None):
    if x_ref is None:
        return own_ref[...]
    n = own_ref.shape[0] // BS
    first = dequantize(x_ref, n, n) + dequantize(late_y_ref, 0, n)
    second = dequantize(y_ref, n, n) + dequantize(late_x_ref, 0, n)
    return own_ref[...] + jnp.concatenate([first, second], axis=1)


def reduce_kernel(core, *refs):
    *in_refs, s_ref, mine_ref, other_ref, pack = refs
    total = all_terms(*in_refs)
    s_ref[...] = total
    gram_store(total, pack)
    half = pack.shape[0] // 2
    c = core[0]
    mine_ref[...] = pack[pl.ds(pl.multiple_of(c * half, 8), half), :]
    other_ref[...] = pack[pl.ds(pl.multiple_of((1 - c) * half, 8), half), :]


def gram_store(total, pack):
    high = total.astype(jnp.bfloat16)
    low = (total - high.astype(jnp.float32)).astype(jnp.bfloat16)
    dims = (((0,), (0,)), ((), ()))
    dot = functools.partial(lax.dot_general, dimension_numbers=dims, preferred_element_type=jnp.float32)
    cross = dot(high, low)
    gram = dot(high, high) + dot(low, low) + cross + cross.T
    row = lax.broadcasted_iota(jnp.int32, (PANEL, PANEL), 0)
    lane = lax.broadcasted_iota(jnp.int32, (PANEL, PANEL), 1)
    second = gram[PANEL:, PANEL:]
    pack[0:PANEL, :] = jnp.where(lane >= row, gram[:PANEL, :PANEL], second)
    pack[PANEL : 2 * PANEL, :] = gram[:PANEL, PANEL:]
    diagonal = jnp.sum(jnp.where(lane == row, second, 0.0), axis=0, keepdims=True)
    pack[2 * PANEL :, :] = jnp.broadcast_to(diagonal, (PACK - 2 * PANEL, PANEL))


def split(x, terms):
    out = []
    for _ in range(terms):
        part = x.astype(jnp.bfloat16)
        out.append(part)
        x = x - part.astype(jnp.float32)
    return out


PAIRS = ((0, 0), (0, 1), (1, 0), (1, 1), (0, 2), (2, 0))


def lane_copy(x, k):
    return jnp.take_along_axis(x, jnp.full(x.shape, k, jnp.int32), axis=1, mode="promise_in_bounds")


def factor(gram):
    n = gram.shape[0]
    eye = lax.broadcasted_iota(jnp.int32, (n, n), 0) == lax.broadcasted_iota(jnp.int32, (n, n), 1)
    picked = jnp.where(eye, gram, 0.0)
    diagonal = jnp.sum(picked, axis=0, keepdims=True)
    inverse_row = lax.rsqrt(diagonal)
    inverse_col = lax.rsqrt(jnp.sum(picked, axis=1, keepdims=True))
    gram = gram * inverse_row * inverse_col

    sub = lax.broadcasted_iota(jnp.int32, (8, n), 0)
    lane = lax.broadcasted_iota(jnp.int32, (8, n), 1)
    left = [gram[8 * i : 8 * i + 8] for i in range(n // 8)]
    right = [(lane == sub + 8 * i).astype(jnp.float32) for i in range(n // 8)]

    def row(x, k):
        return jnp.broadcast_to(x[k : k + 1], x.shape)

    for first in range(0, n // 8, STEP):
        last = first + STEP
        for b in range(first, last):
            cols = {
                t: [lane_copy(left[t], 8 * b + k) for k in range(8)]
                for t in range(b, last)
            }
            spread = {(i, j): row(cols[b][j], i) for j in range(8) for i in range(j, 8)}
            low, root = {}, {}
            for k in range(0, 8, 2):
                p, q, r = spread[k, k], spread[k + 1, k], spread[k + 1, k + 1]
                root[k] = lax.rsqrt(p)
                low[k + 1, k] = q * root[k]
                root[k + 1] = lax.rsqrt(p * r - q * q) * (p * root[k])
                for i in range(k + 2, 8):
                    low[i, k] = spread[i, k] * root[k]
                    low[i, k + 1] = (spread[i, k + 1] - low[i, k] * low[k + 1, k]) * root[k + 1]
                for j in range(k + 2, 8):
                    for i in range(j, 8):
                        spread[i, j] = spread[i, j] - low[i, k] * low[j, k] - low[i, k + 1] * low[j, k + 1]

            def solve(terms):
                done = []
                for k, term in enumerate(terms):
                    for j in range(k):
                        term = term - done[j] * low[k, j]
                    done.append(term * root[k])
                return done

            mult = {t: solve(cols[t]) for t in range(b + 1, last)}
            for side in (left, right):
                tops = solve([row(side[b], k) for k in range(8)])
                side[b] = tops[0]
                for k in range(1, 8):
                    side[b] = jnp.where(sub == k, tops[k], side[b])
                for t in range(b + 1, last):
                    for k in range(8):
                        side[t] = side[t] - mult[t][k] * tops[k]
        if last < n // 8:
            u = split(jnp.concatenate(left[first:last], axis=0), 3)
            v = split(jnp.concatenate(right[first:last], axis=0), 3)
            lhs = jnp.concatenate([u[i] for i, _ in PAIRS], axis=0)
            rhs = jnp.concatenate(
                [jnp.concatenate([u[j] for _, j in PAIRS], axis=0), jnp.concatenate([v[j] for _, j in PAIRS], axis=0)],
                axis=1,
            )
            change = lax.dot_general(lhs, rhs, (((0,), (0,)), ((), ())), preferred_element_type=jnp.float32)
            for t in range(last, n // 8):
                left[t] = left[t] - change[8 * t : 8 * t + 8, :n]
                right[t] = right[t] - change[8 * t : 8 * t + 8, n:]
    upper = jnp.concatenate([jnp.where(lane >= sub + 8 * i, x, 0.0) for i, x in enumerate(left)], axis=0)
    return upper * (diagonal * inverse_row), jnp.concatenate(right, axis=0) * inverse_row


def dot3(a, b, dims):
    (ah, al), (bh, bl) = split(a, 2), split(b, 2)
    dot = functools.partial(
        lax.dot_general, dimension_numbers=(dims, ((), ())), preferred_element_type=jnp.float32
    )
    return dot(ah, bh) + (dot(ah, bl) + dot(al, bh))


def full_dot(a, b, dims):
    return lax.dot_general(
        a, b, (dims, ((), ())), precision=lax.Precision.HIGHEST, preferred_element_type=jnp.float32
    )


NN, NT, TN = ((1,), (0,)), ((1,), (1,)), ((0,), (0,))


def tail_kernel(scale, core, mine_ref, other_ref, s_ref, basis_ref, upper_ref, pack):
    half = pack.shape[0] // 2
    c = core[0]
    pack[pl.ds(pl.multiple_of(c * half, 8), half), :] = mine_ref[...] * scale
    pack[pl.ds(pl.multiple_of((1 - c) * half, 8), half), :] = other_ref[...] * scale
    row = lax.broadcasted_iota(jnp.int32, (PANEL, PANEL), 0)
    lane = lax.broadcasted_iota(jnp.int32, (PANEL, PANEL), 1)
    both, cross = pack[0:PANEL, :], pack[PANEL : 2 * PANEL, :]
    turned = both.T
    gram_one = jnp.where(lane >= row, both, turned)
    diagonal = jnp.broadcast_to(pack[2 * PANEL : 2 * PANEL + 1, :], both.shape)
    gram_two = jnp.where(lane == row, diagonal, jnp.where(lane < row, both, turned))
    upper_one, low_one = factor(gram_one)
    coupling = full_dot(low_one, cross, NN)
    basis_one = dot3(s_ref[:, 0:PANEL], low_one, NT)
    basis_ref[:, 0:PANEL] = basis_one
    remainder = s_ref[:, PANEL:] - dot3(basis_one, coupling, NN)
    upper_two, low_two = factor(gram_two - full_dot(coupling, coupling, TN))
    upper_ref[0:PANEL, 0:PANEL] = upper_one
    upper_ref[0:PANEL, PANEL:] = coupling
    upper_ref[PANEL:, 0:PANEL] = jnp.zeros_like(upper_one)
    upper_ref[PANEL:, PANEL:] = upper_two
    basis_ref[:, PANEL:] = dot3(remainder, low_two, NT)


def whole(shape):
    return pl.BlockSpec(shape, lambda *_: (0,) * len(shape))


def gather_row(value, ready):
    bits = lax.axis_size("row").bit_length() - 1
    shards = {0: value}
    for bit in reversed(range(bits)):
        for k, v in list(shards.items()):
            if bit == 0 and k:
                v, ready = lax.optimization_barrier((v, ready))
            shards[k | 1 << bit] = exchange(v, "row", 1 << bit)
    return [shards[k] for k in range(2**bits)], ready


def dense_sketch(gaussian_sketch, block_values, local_rows, local_cols, grid_rows, grid_cols):
    size_col = lax.axis_size("col")
    chips = size_col // 2
    shard_rows, width = gaussian_sketch.shape
    group = shard_rows // BS
    me = lax.axis_index("col")
    owner = local_rows // group
    peer_core = (owner + me) % 2
    near = owner // 2 ^ me // 2
    near = ((near ^ near // 2) + chips - 1) % chips
    place = ((1 - peer_core) * chips + near) * group + local_rows % group
    shard = (local_cols // group) ^ lax.axis_index("row")
    slots = place * grid_cols + shard * group + local_cols % group
    dense = scatter_blocks(slots, block_values, grid_rows * grid_cols)
    dense = dense.reshape(2 * chips, group, grid_cols, BS, BS)
    shards, dense = gather_row(gaussian_sketch, dense)
    late = [k for k in range(len(shards)) if k % 2 and k > 1]
    early = [k for k in range(len(shards)) if k not in late]

    params = pltpu.CompilerParams(vmem_limit_bytes=12 * 2**20)
    flops = 2 * shard_rows * grid_cols * BS * width
    bytes_a = 2 * shard_rows * grid_cols * BS

    def cost(n):
        return pl.CostEstimate(flops=n * flops, bytes_accessed=n * bytes_a, transcendentals=0)

    held = pl.BlockSpec(memory_space=pltpu.VMEM)
    r_block = (1, shard_rows, width)
    def block(first):
        return pl.BlockSpec(r_block, lambda i: (i + first, 0, 0))

    def product(first, count, chosen, *added):
        return pl.pallas_call(
            functools.partial(product_kernel, first, chosen),
            grid=(count,),
            in_specs=[held] * (len(chosen) + 1) + [block(first)] * len(added),
            out_specs=block(0),
            out_shape=jax.ShapeDtypeStruct((count, shard_rows, width), jnp.float32),
            compiler_params=params,
            cost_estimate=cost(count),
        )(dense, *[shards[k] for k in chosen], *added)

    first_sum = product(0, 2 * chips, early)
    peer = [exchange(product(at, 2, late, first_sum), "col", 1) for at in (0, 2)]
    near = [product(chips + at, 2, late, first_sum) for at in (0, 2)]

    def call(kernel, outs, *args):
        return pl.pallas_call(
            kernel,
            grid=(1,),
            in_specs=[whole(x.shape) for x in args],
            out_specs=[whole(x.shape) for x in outs],
            out_shape=outs,
            compiler_params=params,
        )(*args)

    panel = jax.ShapeDtypeStruct((shard_rows, PANEL), jnp.float32)
    kept = jax.ShapeDtypeStruct((shard_rows, width), jnp.float32)
    two = jax.ShapeDtypeStruct((2 * shard_rows + 16, PANEL), jnp.int16)
    single = jax.ShapeDtypeStruct((shard_rows + 16, PANEL), jnp.int16)
    coded_x, keep_x, passed = call(code_x_kernel, [two, panel, panel], near[0], peer[0])
    coded_y, keep_y, own = call(code_y_kernel, [two, panel, kept], near[1], peer[1], passed)
    from_x, from_y = exchange(coded_x, "col", 2), exchange(coded_y, "col", 4)
    late_y = exchange(call(merge_kernel, [single], keep_y, from_x)[0], "col", 4)
    late_x = exchange(call(merge_kernel, [single], keep_x, from_y)[0], "col", 2)
    return [own, from_x, from_y, late_y, late_x]


def tile_product(sketch_blocks, block_values, local_rows, local_cols, tile_rows):
    group_size = math.gcd(block_values.shape[0], 64)
    col_width = sketch_blocks.shape[2]

    def advance(counter, summed):
        offset = (counter * group_size).astype(jnp.int32)
        values = lax.dynamic_slice_in_dim(block_values, offset, group_size, 0)
        row_ids = lax.dynamic_slice_in_dim(local_rows, offset, group_size, 0)
        col_ids = lax.dynamic_slice_in_dim(local_cols, offset, group_size, 0)
        picked = jnp.take(sketch_blocks, col_ids, axis=0)
        product = jnp.einsum("gab,gbs->gas", values, picked, preferred_element_type=jnp.float32)
        return summed.at[row_ids].add(product)

    initial = jnp.zeros((tile_rows, block_values.shape[1], col_width), jnp.float32)
    summed = lax.fori_loop(0, block_values.shape[0] // group_size, advance, initial)
    return summed.reshape(tile_rows * block_values.shape[1], col_width)


def looped_sketch(gaussian_sketch, block_values, local_rows, local_cols, grid_rows, grid_cols):
    gathered = lax.all_gather(gaussian_sketch, "row", axis=0, tiled=True)
    sketch_blocks = gathered.reshape(grid_cols, BS, gathered.shape[1])
    partial_value = tile_product(sketch_blocks, block_values, local_rows, local_cols, grid_rows)
    return [lax.psum_scatter(partial_value, "col", scatter_dimension=0, tiled=True)]


def direct_sum(value, axis, low_bit, bits):
    t = [value] + [exchange(value, axis, mask << low_bit) for mask in range(1, 2**bits)]
    if bits == 1:
        return t[0] + t[1]
    if axis == "col":
        return (t[2] + t[3]) + (t[0] + t[1])
    return (t[3] + t[2]) + (t[1] + t[0])


def sum_over_axis(value, axis, low_bit):
    bits = lax.axis_size(axis).bit_length() - 1
    while low_bit < bits:
        take = min(2, bits - low_bit)
        value = direct_sum(value, axis, low_bit, take)
        low_bit += take
    return value


def sum_over_mesh(mine, other, core):
    mine = mine + exchange(other, "col", 1)
    mine = sum_over_axis(mine, "col", 1)
    mine = sum_over_axis(mine, "row", 0)
    return mine, exchange(mine, "col", 1)


def on_device(gaussian_sketch, block_values, block_rows, block_columns):
    size_row = lax.axis_size("row")
    size_col = lax.axis_size("col")
    shard_rows, width = gaussian_sketch.shape
    grid_rows = shard_rows * size_col // BS
    grid_cols = shard_rows * size_row // BS
    local_rows = block_rows - lax.axis_index("row") * grid_rows
    local_cols = block_columns - lax.axis_index("col") * grid_cols
    dense = 2 * grid_rows * grid_cols * BS * BS <= DENSE_BYTES and size_col == 8 and width == 2 * PANEL
    sketch = dense_sketch if dense else looped_sketch
    terms = sketch(
        gaussian_sketch, block_values, local_rows, local_cols, grid_rows, grid_cols
    )
    core = lax.axis_index("col") % 2
    half = jax.ShapeDtypeStruct((PACK // 2, PANEL), jnp.float32)
    sketched, mine, other = pl.pallas_call(
        reduce_kernel,
        grid_spec=pltpu.PrefetchScalarGridSpec(
            num_scalar_prefetch=1,
            grid=(1,),
            in_specs=[whole(t.shape) for t in terms],
            out_specs=[whole((shard_rows, width)), whole(half.shape), whole(half.shape)],
            scratch_shapes=[pltpu.VMEM((PACK, PANEL), jnp.float32)],
        ),
        out_shape=[jax.ShapeDtypeStruct((shard_rows, width), jnp.float32), half, half],
        compiler_params=pltpu.CompilerParams(vmem_limit_bytes=12 * 2**20),
    )(core.reshape(1), *terms)
    order_total = shard_rows * size_row * size_col
    mine, other = sum_over_mesh(mine, other, core)
    range_basis, upper_factor = pl.pallas_call(
        functools.partial(tail_kernel, 1.0 / order_total),
        grid_spec=pltpu.PrefetchScalarGridSpec(
            num_scalar_prefetch=1,
            grid=(1,),
            in_specs=[whole(half.shape), whole(half.shape), whole(sketched.shape)],
            out_specs=[whole(sketched.shape), whole((width, width))],
            scratch_shapes=[pltpu.VMEM((PACK, PANEL), jnp.float32)],
        ),
        out_shape=[
            jax.ShapeDtypeStruct(sketched.shape, jnp.float32),
            jax.ShapeDtypeStruct((width, width), jnp.float32),
        ],
        compiler_params=pltpu.CompilerParams(vmem_limit_bytes=16 * 2**20),
    )(core.reshape(1), mine, other, sketched)
    return (range_basis, upper_factor)


def solution(mesh):
    return jax.shard_map(
        on_device,
        mesh=mesh,
        in_specs=(
            P(("col", "row"), None),
            P(("row", "col"), None, None),
            P(("row", "col")),
            P(("row", "col")),
        ),
        out_specs=(P(("row", "col"), None), P()),
        check_vma=False,
    )
```

```python
import functools
import math

import jax
import jax.numpy as jnp
from jax import lax
from jax.experimental import pallas as pl
from jax.experimental.pallas import tpu as pltpu
from jax.sharding import PartitionSpec as P

PANEL = 128
BS = 128
LEVELS = 32700.0
OCTAVE = 64.0
DENSE_BYTES = 32 * 2**20
STEP = 8
PACK = 2 * PANEL + 16


def exchange(value, axis, mask):
    size = lax.axis_size(axis)
    return lax.ppermute(value, axis, [(i, i ^ mask) for i in range(size)])


def scatter_kernel(slots, values, dense, sem):
    step = math.gcd(8, math.gcd(dense.shape[0], values.shape[0]))

    @pl.loop(0, dense.shape[0] // step)
    def _(s):
        dense[pl.ds(s * step, step)] = jnp.zeros((step, *dense.shape[1:]), dense.dtype)

    @pl.loop(0, values.shape[0] // step)
    def _(b):
        for u in range(step):
            block = b * step + u
            pltpu.make_async_copy(values.at[block], dense.at[slots[block]], sem).start()

    pltpu.make_async_copy(values, values, sem).wait()


def scatter_blocks(slots, values, n_slots):
    return pl.pallas_call(
        scatter_kernel,
        out_shape=pltpu.VMEM((n_slots, BS, BS), values.dtype),
        grid_spec=pltpu.PrefetchScalarGridSpec(
            num_scalar_prefetch=1,
            grid=(),
            in_specs=[pl.BlockSpec(memory_space=pltpu.HBM)],
            out_specs=pl.BlockSpec(memory_space=pltpu.VMEM),
            scratch_shapes=[pltpu.SemaphoreType.DMA],
        ),
        compiler_params=pltpu.CompilerParams(vmem_limit_bytes=4 * 2**20),
        cost_estimate=pl.CostEstimate(flops=0, bytes_accessed=24 * 2**20, transcendentals=0),
    )(slots, pltpu.with_memory_space_constraint(values, pltpu.HBM))


def dense_dot(a_ref, x_refs, shards, chunk):
    group = a_ref.shape[1]
    total = None
    for k, x_ref in zip(shards, x_refs):
        lhs = jnp.concatenate(
            [
                jnp.concatenate([a_ref[chunk, r, k * group + c] for c in range(group)], axis=1)
                for r in range(group)
            ],
            axis=0,
        )
        part = jnp.dot(lhs, x_ref[...], preferred_element_type=jnp.float32)
        total = part if total is None else total + part
    return total


def product_kernel(first, shards, a_ref, *refs):
    *in_refs, o_ref = refs
    total = dense_dot(a_ref, in_refs, shards, pl.program_id(0) + first)
    added = in_refs[len(shards) :]
    o_ref[0] = total + added[0][0] if added else total


def quantize(total, o_ref):
    n = total.shape[0] // BS
    width = total.shape[1]
    row = lax.broadcasted_iota(jnp.int32, (16, width), 0)
    tail = jnp.zeros((16, width), jnp.float32)
    for b in range(n):
        part = total[b * BS : (b + 1) * BS]
        top = jnp.maximum(jnp.max(jnp.abs(part), axis=0, keepdims=True), 1e-30)
        step = jnp.ceil(jnp.log(top) * (OCTAVE / math.log(2.0)))
        scaled = part * (jnp.exp(step * (-math.log(2.0) / OCTAVE)) * LEVELS)
        o_ref[b * BS : (b + 1) * BS, :] = jnp.round(scaled).astype(jnp.int32).astype(jnp.int16)
        tail = jnp.where(row == b, jnp.broadcast_to(step, tail.shape), tail)
    o_ref[n * BS :, :] = tail.astype(jnp.int32).astype(jnp.int16)


def dequantize(q_ref):
    n = (q_ref.shape[0] - 16) // BS
    tail = q_ref[n * BS :, :].astype(jnp.int32).astype(jnp.float32)
    parts = []
    for b in range(n):
        scale = jnp.exp(tail[b : b + 1] * (math.log(2.0) / OCTAVE)) * (1.0 / LEVELS)
        parts.append(q_ref[b * BS : (b + 1) * BS, :].astype(jnp.int32).astype(jnp.float32) * scale)
    return jnp.concatenate(parts, axis=0)


def code_kernel(a_ref, b_ref, *o_refs):
    total = a_ref[0] + b_ref[0]
    for j, o_ref in enumerate(o_refs):

        @pl.when(pl.program_id(0) == j)
        def _(o_ref=o_ref):
            if o_ref.dtype == jnp.int16:
                quantize(total, o_ref)
            else:
                o_ref[...] = total


def reduce_kernel(core, *refs):
    *in_refs, s_ref, mine_ref, other_ref, pack = refs
    total = None
    for ref in in_refs:
        term = dequantize(ref) if ref.dtype == jnp.int16 else ref[...]
        total = term if total is None else total + term
    s_ref[...] = total
    gram_store(total, pack)
    half = pack.shape[0] // 2
    c = core[0]
    mine_ref[...] = pack[pl.ds(pl.multiple_of(c * half, 8), half), :]
    other_ref[...] = pack[pl.ds(pl.multiple_of((1 - c) * half, 8), half), :]


def gram_store(total, pack):
    high = total.astype(jnp.bfloat16)
    low = (total - high.astype(jnp.float32)).astype(jnp.bfloat16)
    dims = (((0,), (0,)), ((), ()))
    dot = functools.partial(lax.dot_general, dimension_numbers=dims, preferred_element_type=jnp.float32)
    cross = dot(high, low)
    gram = dot(high, high) + dot(low, low) + cross + cross.T
    row = lax.broadcasted_iota(jnp.int32, (PANEL, PANEL), 0)
    lane = lax.broadcasted_iota(jnp.int32, (PANEL, PANEL), 1)
    second = gram[PANEL:, PANEL:]
    pack[0:PANEL, :] = jnp.where(lane >= row, gram[:PANEL, :PANEL], second)
    pack[PANEL : 2 * PANEL, :] = gram[:PANEL, PANEL:]
    diagonal = jnp.sum(jnp.where(lane == row, second, 0.0), axis=0, keepdims=True)
    pack[2 * PANEL :, :] = jnp.broadcast_to(diagonal, (PACK - 2 * PANEL, PANEL))


def split(x, terms):
    out = []
    for _ in range(terms):
        part = x.astype(jnp.bfloat16)
        out.append(part)
        x = x - part.astype(jnp.float32)
    return out


PAIRS = ((0, 0), (0, 1), (1, 0), (1, 1), (0, 2), (2, 0))


def lane_copy(x, k):
    return jnp.take_along_axis(x, jnp.full(x.shape, k, jnp.int32), axis=1, mode="promise_in_bounds")


def factor(gram):
    n = gram.shape[0]
    eye = lax.broadcasted_iota(jnp.int32, (n, n), 0) == lax.broadcasted_iota(jnp.int32, (n, n), 1)
    picked = jnp.where(eye, gram, 0.0)
    diagonal = jnp.sum(picked, axis=0, keepdims=True)
    inverse_row = lax.rsqrt(diagonal)
    inverse_col = lax.rsqrt(jnp.sum(picked, axis=1, keepdims=True))
    gram = gram * inverse_row * inverse_col

    sub = lax.broadcasted_iota(jnp.int32, (8, n), 0)
    lane = lax.broadcasted_iota(jnp.int32, (8, n), 1)
    left = [gram[8 * i : 8 * i + 8] for i in range(n // 8)]
    right = [(lane == sub + 8 * i).astype(jnp.float32) for i in range(n // 8)]

    def row(x, k):
        return jnp.broadcast_to(x[k : k + 1], x.shape)

    for first in range(0, n // 8, STEP):
        last = first + STEP
        for b in range(first, last):
            cols = {
                t: [lane_copy(left[t], 8 * b + k) for k in range(8)]
                for t in range(b, last)
            }
            spread = {(i, j): row(cols[b][j], i) for j in range(8) for i in range(j, 8)}
            low, root = {}, {}
            for k in range(0, 8, 2):
                p, q, r = spread[k, k], spread[k + 1, k], spread[k + 1, k + 1]
                root[k] = lax.rsqrt(p)
                low[k + 1, k] = q * root[k]
                root[k + 1] = lax.rsqrt(p * r - q * q) * (p * root[k])
                for i in range(k + 2, 8):
                    low[i, k] = spread[i, k] * root[k]
                    low[i, k + 1] = (spread[i, k + 1] - low[i, k] * low[k + 1, k]) * root[k + 1]
                for j in range(k + 2, 8):
                    for i in range(j, 8):
                        spread[i, j] = spread[i, j] - low[i, k] * low[j, k] - low[i, k + 1] * low[j, k + 1]

            def solve(terms):
                done = []
                for k, term in enumerate(terms):
                    for j in range(k):
                        term = term - done[j] * low[k, j]
                    done.append(term * root[k])
                return done

            mult = {t: solve(cols[t]) for t in range(b + 1, last)}
            for side in (left, right):
                tops = solve([row(side[b], k) for k in range(8)])
                side[b] = tops[0]
                for k in range(1, 8):
                    side[b] = jnp.where(sub == k, tops[k], side[b])
                for t in range(b + 1, last):
                    for k in range(8):
                        side[t] = side[t] - mult[t][k] * tops[k]
        if last < n // 8:
            u = split(jnp.concatenate(left[first:last], axis=0), 3)
            v = split(jnp.concatenate(right[first:last], axis=0), 3)
            lhs = jnp.concatenate([u[i] for i, _ in PAIRS], axis=0)
            rhs = jnp.concatenate(
                [jnp.concatenate([u[j] for _, j in PAIRS], axis=0), jnp.concatenate([v[j] for _, j in PAIRS], axis=0)],
                axis=1,
            )
            change = lax.dot_general(lhs, rhs, (((0,), (0,)), ((), ())), preferred_element_type=jnp.float32)
            for t in range(last, n // 8):
                left[t] = left[t] - change[8 * t : 8 * t + 8, :n]
                right[t] = right[t] - change[8 * t : 8 * t + 8, n:]
    upper = jnp.concatenate([jnp.where(lane >= sub + 8 * i, x, 0.0) for i, x in enumerate(left)], axis=0)
    return upper * (diagonal * inverse_row), jnp.concatenate(right, axis=0) * inverse_row


def dot3(a, b, dims):
    (ah, al), (bh, bl) = split(a, 2), split(b, 2)
    dot = functools.partial(
        lax.dot_general, dimension_numbers=(dims, ((), ())), preferred_element_type=jnp.float32
    )
    return dot(ah, bh) + (dot(ah, bl) + dot(al, bh))


def full_dot(a, b, dims):
    return lax.dot_general(
        a, b, (dims, ((), ())), precision=lax.Precision.HIGHEST, preferred_element_type=jnp.float32
    )


NN, NT, TN = ((1,), (0,)), ((1,), (1,)), ((0,), (0,))


def tail_kernel(scale, core, mine_ref, other_ref, s_ref, basis_ref, upper_ref, pack):
    half = pack.shape[0] // 2
    c = core[0]
    pack[pl.ds(pl.multiple_of(c * half, 8), half), :] = mine_ref[...] * scale
    pack[pl.ds(pl.multiple_of((1 - c) * half, 8), half), :] = other_ref[...] * scale
    row = lax.broadcasted_iota(jnp.int32, (PANEL, PANEL), 0)
    lane = lax.broadcasted_iota(jnp.int32, (PANEL, PANEL), 1)
    both, cross = pack[0:PANEL, :], pack[PANEL : 2 * PANEL, :]
    turned = both.T
    gram_one = jnp.where(lane >= row, both, turned)
    diagonal = jnp.broadcast_to(pack[2 * PANEL : 2 * PANEL + 1, :], both.shape)
    gram_two = jnp.where(lane == row, diagonal, jnp.where(lane < row, both, turned))
    upper_one, low_one = factor(gram_one)
    coupling = full_dot(low_one, cross, NN)
    basis_one = dot3(s_ref[:, 0:PANEL], low_one, NT)
    basis_ref[:, 0:PANEL] = basis_one
    remainder = s_ref[:, PANEL:] - dot3(basis_one, coupling, NN)
    upper_two, low_two = factor(gram_two - full_dot(coupling, coupling, TN))
    upper_ref[0:PANEL, 0:PANEL] = upper_one
    upper_ref[0:PANEL, PANEL:] = coupling
    upper_ref[PANEL:, 0:PANEL] = jnp.zeros_like(upper_one)
    upper_ref[PANEL:, PANEL:] = upper_two
    basis_ref[:, PANEL:] = dot3(remainder, low_two, NT)


def whole(shape):
    return pl.BlockSpec(shape, lambda *_: (0,) * len(shape))


def gather_row(value, ready):
    bits = lax.axis_size("row").bit_length() - 1
    shards = {0: value}
    for bit in reversed(range(bits)):
        for k, v in list(shards.items()):
            if bit == 0 and k:
                v, ready = lax.optimization_barrier((v, ready))
            shards[k | 1 << bit] = exchange(v, "row", 1 << bit)
    return [shards[k] for k in range(2**bits)], ready


def dense_sketch(gaussian_sketch, block_values, local_rows, local_cols, grid_rows, grid_cols):
    size_col = lax.axis_size("col")
    chips = size_col // 2
    shard_rows, width = gaussian_sketch.shape
    group = shard_rows // BS
    me = lax.axis_index("col")
    owner = local_rows // group
    peer_core = (owner + me) % 2
    near = ((owner // 2 ^ me // 2) + chips - 1) % chips
    place = ((1 - peer_core) * chips + near) * group + local_rows % group
    shard = (local_cols // group) ^ lax.axis_index("row")
    slots = place * grid_cols + shard * group + local_cols % group
    dense = scatter_blocks(slots, block_values, grid_rows * grid_cols)
    dense = dense.reshape(2 * chips, group, grid_cols, BS, BS)
    shards, dense = gather_row(gaussian_sketch, dense)
    late = [k for k in range(len(shards)) if k % 2 and k > 1]
    early = [k for k in range(len(shards)) if k not in late]

    params = pltpu.CompilerParams(vmem_limit_bytes=12 * 2**20)
    flops = 2 * shard_rows * grid_cols * BS * width
    bytes_a = 2 * shard_rows * grid_cols * BS

    def cost(n):
        return pl.CostEstimate(flops=n * flops, bytes_accessed=n * bytes_a, transcendentals=0)

    held = pl.BlockSpec(memory_space=pltpu.VMEM)
    r_block = (1, shard_rows, width)
    def block(first):
        return pl.BlockSpec(r_block, lambda i: (i + first, 0, 0))

    def product(first, count, chosen, *added):
        return pl.pallas_call(
            functools.partial(product_kernel, first, chosen),
            grid=(count,),
            in_specs=[held] * (len(chosen) + 1) + [block(first)] * len(added),
            out_specs=block(0),
            out_shape=jax.ShapeDtypeStruct((count, shard_rows, width), jnp.float32),
            compiler_params=params,
            cost_estimate=cost(count),
        )(dense, *[shards[k] for k in chosen], *added)

    first_sum = product(0, 2 * chips, early)
    parts = [(0, chips // 2), (chips // 2, chips - chips // 2)]
    peer = [exchange(product(at, n, late, first_sum), "col", 1) for at, n in parts]
    near = [product(chips + at, n, late, first_sum) for at, n in parts]
    sent = jax.ShapeDtypeStruct((shard_rows + 16, width), jnp.int16)
    kept = jax.ShapeDtypeStruct((shard_rows, width), jnp.float32)
    terms = []
    for (at, n), mine, theirs in zip(parts, near, peer):
        shapes = [kept if at + i == chips - 1 else sent for i in range(n)]
        done = pl.pallas_call(
            code_kernel,
            grid=(n,),
            in_specs=[block(0), block(0)],
            out_specs=[whole(x.shape) for x in shapes],
            out_shape=shapes,
            compiler_params=params,
        )(mine, theirs)
        for i, x in enumerate(done):
            terms.append(x if x.dtype == jnp.float32 else exchange(x, "col", 2 * (at + i + 1)))
    return terms


def tile_product(sketch_blocks, block_values, local_rows, local_cols, tile_rows):
    group_size = math.gcd(block_values.shape[0], 64)
    col_width = sketch_blocks.shape[2]

    def advance(counter, summed):
        offset = (counter * group_size).astype(jnp.int32)
        values = lax.dynamic_slice_in_dim(block_values, offset, group_size, 0)
        row_ids = lax.dynamic_slice_in_dim(local_rows, offset, group_size, 0)
        col_ids = lax.dynamic_slice_in_dim(local_cols, offset, group_size, 0)
        picked = jnp.take(sketch_blocks, col_ids, axis=0)
        product = jnp.einsum("gab,gbs->gas", values, picked, preferred_element_type=jnp.float32)
        return summed.at[row_ids].add(product)

    initial = jnp.zeros((tile_rows, block_values.shape[1], col_width), jnp.float32)
    summed = lax.fori_loop(0, block_values.shape[0] // group_size, advance, initial)
    return summed.reshape(tile_rows * block_values.shape[1], col_width)


def looped_sketch(gaussian_sketch, block_values, local_rows, local_cols, grid_rows, grid_cols):
    gathered = lax.all_gather(gaussian_sketch, "row", axis=0, tiled=True)
    sketch_blocks = gathered.reshape(grid_cols, BS, gathered.shape[1])
    partial_value = tile_product(sketch_blocks, block_values, local_rows, local_cols, grid_rows)
    return [lax.psum_scatter(partial_value, "col", scatter_dimension=0, tiled=True)]


def direct_sum(value, axis, low_bit, bits):
    t = [value] + [exchange(value, axis, mask << low_bit) for mask in range(1, 2**bits)]
    if bits == 1:
        return t[0] + t[1]
    if axis == "col":
        return (t[0] + t[1]) + (t[3] + t[2])
    return (t[3] + t[2]) + (t[1] + t[0])


def sum_over_axis(value, axis, low_bit):
    bits = lax.axis_size(axis).bit_length() - 1
    while low_bit < bits:
        take = min(2, bits - low_bit)
        value = direct_sum(value, axis, low_bit, take)
        low_bit += take
    return value


def sum_over_mesh(mine, other, core):
    mine = mine + exchange(other, "col", 1)
    mine = sum_over_axis(mine, "col", 1)
    mine = sum_over_axis(mine, "row", 0)
    return mine, exchange(mine, "col", 1)


def on_device(gaussian_sketch, block_values, block_rows, block_columns):
    size_row = lax.axis_size("row")
    size_col = lax.axis_size("col")
    shard_rows, width = gaussian_sketch.shape
    grid_rows = shard_rows * size_col // BS
    grid_cols = shard_rows * size_row // BS
    local_rows = block_rows - lax.axis_index("row") * grid_rows
    local_cols = block_columns - lax.axis_index("col") * grid_cols
    dense = 2 * grid_rows * grid_cols * BS * BS <= DENSE_BYTES
    sketch = dense_sketch if dense else looped_sketch
    terms = sketch(
        gaussian_sketch, block_values, local_rows, local_cols, grid_rows, grid_cols
    )
    core = lax.axis_index("col") % 2
    half = jax.ShapeDtypeStruct((PACK // 2, PANEL), jnp.float32)
    sketched, mine, other = pl.pallas_call(
        reduce_kernel,
        grid_spec=pltpu.PrefetchScalarGridSpec(
            num_scalar_prefetch=1,
            grid=(1,),
            in_specs=[whole(t.shape) for t in terms],
            out_specs=[whole((shard_rows, width)), whole(half.shape), whole(half.shape)],
            scratch_shapes=[pltpu.VMEM((PACK, PANEL), jnp.float32)],
        ),
        out_shape=[jax.ShapeDtypeStruct((shard_rows, width), jnp.float32), half, half],
        compiler_params=pltpu.CompilerParams(vmem_limit_bytes=12 * 2**20),
    )(core.reshape(1), *terms)
    order_total = shard_rows * size_row * size_col
    mine, other = sum_over_mesh(mine, other, core)
    range_basis, upper_factor = pl.pallas_call(
        functools.partial(tail_kernel, 1.0 / order_total),
        grid_spec=pltpu.PrefetchScalarGridSpec(
            num_scalar_prefetch=1,
            grid=(1,),
            in_specs=[whole(half.shape), whole(half.shape), whole(sketched.shape)],
            out_specs=[whole(sketched.shape), whole((width, width))],
            scratch_shapes=[pltpu.VMEM((PACK, PANEL), jnp.float32)],
        ),
        out_shape=[
            jax.ShapeDtypeStruct(sketched.shape, jnp.float32),
            jax.ShapeDtypeStruct((width, width), jnp.float32),
        ],
        compiler_params=pltpu.CompilerParams(vmem_limit_bytes=16 * 2**20),
    )(core.reshape(1), mine, other, sketched)
    return (range_basis, upper_factor)


def solution(mesh):
    return jax.shard_map(
        on_device,
        mesh=mesh,
        in_specs=(
            P(("col", "row"), None),
            P(("row", "col"), None, None),
            P(("row", "col")),
            P(("row", "col")),
        ),
        out_specs=(P(("row", "col"), None), P()),
        check_vma=False,
    )
```

```python
import functools
import math

import jax
import jax.numpy as jnp
from jax import lax
from jax.experimental import pallas as pl
from jax.experimental.pallas import tpu as pltpu
from jax.sharding import PartitionSpec as P

PANEL = 128
BS = 128
LEVELS = 32700.0
OCTAVE = 64.0
DENSE_BYTES = 32 * 2**20
STEP = 8
PACK = 2 * PANEL + 16


def exchange(value, axis, mask):
    size = lax.axis_size(axis)
    return lax.ppermute(value, axis, [(i, i ^ mask) for i in range(size)])


def scatter_kernel(slots, values, dense, sem):
    step = math.gcd(8, math.gcd(dense.shape[0], values.shape[0]))

    @pl.loop(0, dense.shape[0] // step)
    def _(s):
        dense[pl.ds(s * step, step)] = jnp.zeros((step, *dense.shape[1:]), dense.dtype)

    @pl.loop(0, values.shape[0] // step)
    def _(b):
        for u in range(step):
            block = b * step + u
            pltpu.make_async_copy(values.at[block], dense.at[slots[block]], sem).start()

    pltpu.make_async_copy(values, values, sem).wait()


def scatter_blocks(slots, values, n_slots):
    return pl.pallas_call(
        scatter_kernel,
        out_shape=pltpu.VMEM((n_slots, BS, BS), values.dtype),
        grid_spec=pltpu.PrefetchScalarGridSpec(
            num_scalar_prefetch=1,
            grid=(),
            in_specs=[pl.BlockSpec(memory_space=pltpu.HBM)],
            out_specs=pl.BlockSpec(memory_space=pltpu.VMEM),
            scratch_shapes=[pltpu.SemaphoreType.DMA],
        ),
        compiler_params=pltpu.CompilerParams(vmem_limit_bytes=4 * 2**20),
        cost_estimate=pl.CostEstimate(flops=0, bytes_accessed=24 * 2**20, transcendentals=0),
    )(slots, pltpu.with_memory_space_constraint(values, pltpu.HBM))


def dense_dot(a_ref, x_refs, shards, chunk):
    group = a_ref.shape[1]
    total = None
    for k, x_ref in zip(shards, x_refs):
        lhs = jnp.concatenate(
            [
                jnp.concatenate([a_ref[chunk, r, k * group + c] for c in range(group)], axis=1)
                for r in range(group)
            ],
            axis=0,
        )
        part = jnp.dot(lhs, x_ref[...], preferred_element_type=jnp.float32)
        total = part if total is None else total + part
    return total


def product_kernel(first, shards, a_ref, *refs):
    *in_refs, o_ref = refs
    total = dense_dot(a_ref, in_refs, shards, pl.program_id(0) + first)
    added = in_refs[len(shards) :]
    o_ref[0] = total + added[0][0] if added else total


def quantize(total, o_ref):
    n = total.shape[0] // BS
    width = total.shape[1]
    row = lax.broadcasted_iota(jnp.int32, (8, width), 0)
    tail = jnp.zeros((8, width), jnp.float32)
    for b in range(n):
        part = total[b * BS : (b + 1) * BS]
        top = jnp.maximum(jnp.max(jnp.abs(part), axis=0, keepdims=True), 1e-30)
        step = jnp.ceil(jnp.log(top) * (OCTAVE / math.log(2.0)))
        scaled = part * (jnp.exp(step * (-math.log(2.0) / OCTAVE)) * LEVELS)
        o_ref[b * BS : (b + 1) * BS, :] = jnp.round(scaled).astype(jnp.int32).astype(jnp.int16)
        tail = jnp.where(row == b, jnp.broadcast_to(step, tail.shape), tail)
    o_ref[n * BS :, :] = tail.astype(jnp.int32).astype(jnp.int16)


def dequantize(q_ref):
    n = (q_ref.shape[0] - 8) // BS
    tail = q_ref[n * BS :, :].astype(jnp.int32).astype(jnp.float32)
    parts = []
    for b in range(n):
        scale = jnp.exp(tail[b : b + 1] * (math.log(2.0) / OCTAVE)) * (1.0 / LEVELS)
        parts.append(q_ref[b * BS : (b + 1) * BS, :].astype(jnp.int32).astype(jnp.float32) * scale)
    return jnp.concatenate(parts, axis=0)


def code_kernel(a_ref, b_ref, *o_refs):
    total = a_ref[0] + b_ref[0]
    for j, o_ref in enumerate(o_refs):

        @pl.when(pl.program_id(0) == j)
        def _(o_ref=o_ref):
            if o_ref.dtype == jnp.int16:
                quantize(total, o_ref)
            else:
                o_ref[...] = total


def reduce_kernel(core, *refs):
    *in_refs, s_ref, mine_ref, other_ref, pack = refs
    total = None
    for ref in in_refs:
        term = dequantize(ref) if ref.dtype == jnp.int16 else ref[...]
        total = term if total is None else total + term
    s_ref[...] = total
    gram_store(total, pack)
    half = pack.shape[0] // 2
    c = core[0]
    mine_ref[...] = pack[pl.ds(pl.multiple_of(c * half, 8), half), :]
    other_ref[...] = pack[pl.ds(pl.multiple_of((1 - c) * half, 8), half), :]


def gram_store(total, pack):
    high = total.astype(jnp.bfloat16)
    low = (total - high.astype(jnp.float32)).astype(jnp.bfloat16)
    dims = (((0,), (0,)), ((), ()))
    dot = functools.partial(lax.dot_general, dimension_numbers=dims, preferred_element_type=jnp.float32)
    cross = dot(high, low)
    gram = dot(high, high) + dot(low, low) + cross + cross.T
    row = lax.broadcasted_iota(jnp.int32, (PANEL, PANEL), 0)
    lane = lax.broadcasted_iota(jnp.int32, (PANEL, PANEL), 1)
    second = gram[PANEL:, PANEL:]
    pack[0:PANEL, :] = jnp.where(lane >= row, gram[:PANEL, :PANEL], second)
    pack[PANEL : 2 * PANEL, :] = gram[:PANEL, PANEL:]
    diagonal = jnp.sum(jnp.where(lane == row, second, 0.0), axis=0, keepdims=True)
    pack[2 * PANEL :, :] = jnp.broadcast_to(diagonal, (PACK - 2 * PANEL, PANEL))


def split(x, terms):
    out = []
    for _ in range(terms):
        part = x.astype(jnp.bfloat16)
        out.append(part)
        x = x - part.astype(jnp.float32)
    return out


PAIRS = ((0, 0), (0, 1), (1, 0), (1, 1), (0, 2), (2, 0))


def lane_copy(x, k):
    return jnp.take_along_axis(x, jnp.full(x.shape, k, jnp.int32), axis=1, mode="promise_in_bounds")


def factor(gram):
    n = gram.shape[0]
    eye = lax.broadcasted_iota(jnp.int32, (n, n), 0) == lax.broadcasted_iota(jnp.int32, (n, n), 1)
    picked = jnp.where(eye, gram, 0.0)
    diagonal = jnp.sum(picked, axis=0, keepdims=True)
    inverse_row = lax.rsqrt(diagonal)
    inverse_col = lax.rsqrt(jnp.sum(picked, axis=1, keepdims=True))
    gram = gram * inverse_row * inverse_col

    sub = lax.broadcasted_iota(jnp.int32, (8, n), 0)
    lane = lax.broadcasted_iota(jnp.int32, (8, n), 1)
    left = [gram[8 * i : 8 * i + 8] for i in range(n // 8)]
    right = [(lane == sub + 8 * i).astype(jnp.float32) for i in range(n // 8)]

    def row(x, k):
        return jnp.broadcast_to(x[k : k + 1], x.shape)

    for first in range(0, n // 8, STEP):
        last = first + STEP
        for b in range(first, last):
            cols = {
                t: [lane_copy(left[t], 8 * b + k) for k in range(8)]
                for t in range(b, last)
            }
            spread = {(i, j): row(cols[b][j], i) for j in range(8) for i in range(j, 8)}
            low, root = {}, {}
            for k in range(0, 8, 2):
                p, q, r = spread[k, k], spread[k + 1, k], spread[k + 1, k + 1]
                root[k] = lax.rsqrt(p)
                low[k + 1, k] = q * root[k]
                root[k + 1] = lax.rsqrt(p * r - q * q) * (p * root[k])
                for i in range(k + 2, 8):
                    low[i, k] = spread[i, k] * root[k]
                    low[i, k + 1] = (spread[i, k + 1] - low[i, k] * low[k + 1, k]) * root[k + 1]
                for j in range(k + 2, 8):
                    for i in range(j, 8):
                        spread[i, j] = spread[i, j] - low[i, k] * low[j, k] - low[i, k + 1] * low[j, k + 1]

            def solve(terms):
                done = []
                for k, term in enumerate(terms):
                    for j in range(k):
                        term = term - done[j] * low[k, j]
                    done.append(term * root[k])
                return done

            mult = {t: solve(cols[t]) for t in range(b + 1, last)}
            for side in (left, right):
                tops = solve([row(side[b], k) for k in range(8)])
                side[b] = tops[0]
                for k in range(1, 8):
                    side[b] = jnp.where(sub == k, tops[k], side[b])
                for t in range(b + 1, last):
                    for k in range(8):
                        side[t] = side[t] - mult[t][k] * tops[k]
        if last < n // 8:
            u = split(jnp.concatenate(left[first:last], axis=0), 3)
            v = split(jnp.concatenate(right[first:last], axis=0), 3)
            lhs = jnp.concatenate([u[i] for i, _ in PAIRS], axis=0)
            rhs = jnp.concatenate(
                [jnp.concatenate([u[j] for _, j in PAIRS], axis=0), jnp.concatenate([v[j] for _, j in PAIRS], axis=0)],
                axis=1,
            )
            change = lax.dot_general(lhs, rhs, (((0,), (0,)), ((), ())), preferred_element_type=jnp.float32)
            for t in range(last, n // 8):
                left[t] = left[t] - change[8 * t : 8 * t + 8, :n]
                right[t] = right[t] - change[8 * t : 8 * t + 8, n:]
    upper = jnp.concatenate([jnp.where(lane >= sub + 8 * i, x, 0.0) for i, x in enumerate(left)], axis=0)
    return upper * (diagonal * inverse_row), jnp.concatenate(right, axis=0) * inverse_row


def dot3(a, b, dims):
    (ah, al), (bh, bl) = split(a, 2), split(b, 2)
    dot = functools.partial(
        lax.dot_general, dimension_numbers=(dims, ((), ())), preferred_element_type=jnp.float32
    )
    return dot(ah, bh) + (dot(ah, bl) + dot(al, bh))


def full_dot(a, b, dims):
    (da,), (db,) = dims
    sa, sb = split(a, 3), split(b, 3)
    lhs = jnp.concatenate([sa[i] for i, _ in PAIRS], axis=da)
    rhs = jnp.concatenate([sb[j] for _, j in PAIRS], axis=db)
    return lax.dot_general(lhs, rhs, (dims, ((), ())), preferred_element_type=jnp.float32)


NN, NT, TN = ((1,), (0,)), ((1,), (1,)), ((0,), (0,))


def tail_kernel(scale, core, mine_ref, other_ref, s_ref, basis_ref, upper_ref, pack):
    half = pack.shape[0] // 2
    c = core[0]
    pack[pl.ds(pl.multiple_of(c * half, 8), half), :] = mine_ref[...] * scale
    pack[pl.ds(pl.multiple_of((1 - c) * half, 8), half), :] = other_ref[...] * scale
    row = lax.broadcasted_iota(jnp.int32, (PANEL, PANEL), 0)
    lane = lax.broadcasted_iota(jnp.int32, (PANEL, PANEL), 1)
    both, cross = pack[0:PANEL, :], pack[PANEL : 2 * PANEL, :]
    turned = both.T
    gram_one = jnp.where(lane >= row, both, turned)
    diagonal = jnp.broadcast_to(pack[2 * PANEL : 2 * PANEL + 1, :], both.shape)
    gram_two = jnp.where(lane == row, diagonal, jnp.where(lane < row, both, turned))
    upper_one, low_one = factor(gram_one)
    coupling = full_dot(low_one, cross, NN)
    basis_one = dot3(s_ref[:, 0:PANEL], low_one, NT)
    basis_ref[:, 0:PANEL] = basis_one
    remainder = s_ref[:, PANEL:] - dot3(basis_one, coupling, NN)
    upper_two, low_two = factor(gram_two - full_dot(coupling, coupling, TN))
    upper_ref[0:PANEL, 0:PANEL] = upper_one
    upper_ref[0:PANEL, PANEL:] = coupling
    upper_ref[PANEL:, 0:PANEL] = jnp.zeros_like(upper_one)
    upper_ref[PANEL:, PANEL:] = upper_two
    basis_ref[:, PANEL:] = dot3(remainder, low_two, NT)


def whole(shape):
    return pl.BlockSpec(shape, lambda *_: (0,) * len(shape))


def gather_row(value, ready):
    bits = lax.axis_size("row").bit_length() - 1
    shards = {0: value}
    for bit in reversed(range(bits)):
        for k, v in list(shards.items()):
            if bit == 0 and k:
                v, ready = lax.optimization_barrier((v, ready))
            shards[k | 1 << bit] = exchange(v, "row", 1 << bit)
    return [shards[k] for k in range(2**bits)], ready


def dense_sketch(gaussian_sketch, block_values, local_rows, local_cols, grid_rows, grid_cols):
    size_col = lax.axis_size("col")
    chips = size_col // 2
    shard_rows, width = gaussian_sketch.shape
    group = shard_rows // BS
    me = lax.axis_index("col")
    owner = local_rows // group
    peer_core = (owner + me) % 2
    near = ((owner // 2 ^ me // 2) + chips - 1) % chips
    place = ((1 - peer_core) * chips + near) * group + local_rows % group
    shard = (local_cols // group) ^ lax.axis_index("row")
    slots = place * grid_cols + shard * group + local_cols % group
    dense = scatter_blocks(slots, block_values, grid_rows * grid_cols)
    dense = dense.reshape(2 * chips, group, grid_cols, BS, BS)
    shards, dense = gather_row(gaussian_sketch, dense)
    late = [k for k in range(len(shards)) if k % 2 and k > 1]
    early = [k for k in range(len(shards)) if k not in late]

    params = pltpu.CompilerParams(vmem_limit_bytes=12 * 2**20)
    flops = 2 * shard_rows * grid_cols * BS * width
    bytes_a = 2 * shard_rows * grid_cols * BS

    def cost(n):
        return pl.CostEstimate(flops=n * flops, bytes_accessed=n * bytes_a, transcendentals=0)

    held = pl.BlockSpec(memory_space=pltpu.VMEM)
    r_block = (1, shard_rows, width)
    def block(first):
        return pl.BlockSpec(r_block, lambda i: (i + first, 0, 0))

    def product(first, count, chosen, *added):
        return pl.pallas_call(
            functools.partial(product_kernel, first, chosen),
            grid=(count,),
            in_specs=[held] * (len(chosen) + 1) + [block(first)] * len(added),
            out_specs=block(0),
            out_shape=jax.ShapeDtypeStruct((count, shard_rows, width), jnp.float32),
            compiler_params=params,
            cost_estimate=cost(count),
        )(dense, *[shards[k] for k in chosen], *added)

    first_sum = product(0, 2 * chips, early)
    parts = [(0, chips // 2), (chips // 2, chips - chips // 2)]
    peer = [exchange(product(at, n, late, first_sum), "col", 1) for at, n in parts]
    near = [product(chips + at, n, late, first_sum) for at, n in parts]
    sent = jax.ShapeDtypeStruct((shard_rows + 8, width), jnp.int16)
    kept = jax.ShapeDtypeStruct((shard_rows, width), jnp.float32)
    terms = []
    for (at, n), mine, theirs in zip(parts, near, peer):
        shapes = [kept if at + i == chips - 1 else sent for i in range(n)]
        done = pl.pallas_call(
            code_kernel,
            grid=(n,),
            in_specs=[block(0), block(0)],
            out_specs=[whole(x.shape) for x in shapes],
            out_shape=shapes,
            compiler_params=params,
        )(mine, theirs)
        for i, x in enumerate(done):
            terms.append(x if x.dtype == jnp.float32 else exchange(x, "col", 2 * (at + i + 1)))
    return terms


def tile_product(sketch_blocks, block_values, local_rows, local_cols, tile_rows):
    group_size = math.gcd(block_values.shape[0], 64)
    col_width = sketch_blocks.shape[2]

    def advance(counter, summed):
        offset = (counter * group_size).astype(jnp.int32)
        values = lax.dynamic_slice_in_dim(block_values, offset, group_size, 0)
        row_ids = lax.dynamic_slice_in_dim(local_rows, offset, group_size, 0)
        col_ids = lax.dynamic_slice_in_dim(local_cols, offset, group_size, 0)
        picked = jnp.take(sketch_blocks, col_ids, axis=0)
        product = jnp.einsum("gab,gbs->gas", values, picked, preferred_element_type=jnp.float32)
        return summed.at[row_ids].add(product)

    initial = jnp.zeros((tile_rows, block_values.shape[1], col_width), jnp.float32)
    summed = lax.fori_loop(0, block_values.shape[0] // group_size, advance, initial)
    return summed.reshape(tile_rows * block_values.shape[1], col_width)


def looped_sketch(gaussian_sketch, block_values, local_rows, local_cols, grid_rows, grid_cols):
    gathered = lax.all_gather(gaussian_sketch, "row", axis=0, tiled=True)
    sketch_blocks = gathered.reshape(grid_cols, BS, gathered.shape[1])
    partial_value = tile_product(sketch_blocks, block_values, local_rows, local_cols, grid_rows)
    return [lax.psum_scatter(partial_value, "col", scatter_dimension=0, tiled=True)]


def direct_sum(value, axis, low_bit, bits):
    t = [value] + [exchange(value, axis, mask << low_bit) for mask in range(1, 2**bits)]
    if bits == 1:
        return t[0] + t[1]
    if axis == "col":
        return (t[2] + t[3]) + (t[0] + t[1])
    return (t[3] + t[2]) + (t[1] + t[0])


def sum_over_axis(value, axis, low_bit):
    bits = lax.axis_size(axis).bit_length() - 1
    while low_bit < bits:
        take = min(2, bits - low_bit)
        value = direct_sum(value, axis, low_bit, take)
        low_bit += take
    return value


def sum_over_mesh(mine, other, core):
    mine = mine + exchange(other, "col", 1)
    mine = sum_over_axis(mine, "col", 1)
    mine = sum_over_axis(mine, "row", 0)
    return mine, exchange(mine, "col", 1)


def on_device(gaussian_sketch, block_values, block_rows, block_columns):
    size_row = lax.axis_size("row")
    size_col = lax.axis_size("col")
    shard_rows, width = gaussian_sketch.shape
    grid_rows = shard_rows * size_col // BS
    grid_cols = shard_rows * size_row // BS
    local_rows = block_rows - lax.axis_index("row") * grid_rows
    local_cols = block_columns - lax.axis_index("col") * grid_cols
    dense = 2 * grid_rows * grid_cols * BS * BS <= DENSE_BYTES
    sketch = dense_sketch if dense else looped_sketch
    terms = sketch(
        gaussian_sketch, block_values, local_rows, local_cols, grid_rows, grid_cols
    )
    core = lax.axis_index("col") % 2
    half = jax.ShapeDtypeStruct((PACK // 2, PANEL), jnp.float32)
    sketched, mine, other = pl.pallas_call(
        reduce_kernel,
        grid_spec=pltpu.PrefetchScalarGridSpec(
            num_scalar_prefetch=1,
            grid=(1,),
            in_specs=[whole(t.shape) for t in terms],
            out_specs=[whole((shard_rows, width)), whole(half.shape), whole(half.shape)],
            scratch_shapes=[pltpu.VMEM((PACK, PANEL), jnp.float32)],
        ),
        out_shape=[jax.ShapeDtypeStruct((shard_rows, width), jnp.float32), half, half],
        compiler_params=pltpu.CompilerParams(vmem_limit_bytes=12 * 2**20),
    )(core.reshape(1), *terms)
    order_total = shard_rows * size_row * size_col
    mine, other = sum_over_mesh(mine, other, core)
    range_basis, upper_factor = pl.pallas_call(
        functools.partial(tail_kernel, 1.0 / order_total),
        grid_spec=pltpu.PrefetchScalarGridSpec(
            num_scalar_prefetch=1,
            grid=(1,),
            in_specs=[whole(half.shape), whole(half.shape), whole(sketched.shape)],
            out_specs=[whole(sketched.shape), whole((width, width))],
            scratch_shapes=[pltpu.VMEM((PACK, PANEL), jnp.float32)],
        ),
        out_shape=[
            jax.ShapeDtypeStruct(sketched.shape, jnp.float32),
            jax.ShapeDtypeStruct((width, width), jnp.float32),
        ],
        compiler_params=pltpu.CompilerParams(vmem_limit_bytes=16 * 2**20),
    )(core.reshape(1), mine, other, sketched)
    return (range_basis, upper_factor)


def solution(mesh):
    return jax.shard_map(
        on_device,
        mesh=mesh,
        in_specs=(
            P(("col", "row"), None),
            P(("row", "col"), None, None),
            P(("row", "col")),
            P(("row", "col")),
        ),
        out_specs=(P(("row", "col"), None), P()),
        check_vma=False,
    )
```

```python
import functools
import math

import jax
import jax.numpy as jnp
from jax import lax
from jax.experimental import pallas as pl
from jax.experimental.pallas import tpu as pltpu
from jax.sharding import PartitionSpec as P

PANEL = 128
BS = 128
LEVELS = 32700.0
OCTAVE = 64.0
DENSE_BYTES = 32 * 2**20
STEP = 8
PACK = 2 * PANEL + 16


def exchange(value, axis, mask):
    size = lax.axis_size(axis)
    return lax.ppermute(value, axis, [(i, i ^ mask) for i in range(size)])


def scatter_kernel(slots, values, dense, sem):
    step = math.gcd(8, math.gcd(dense.shape[0], values.shape[0]))

    @pl.loop(0, dense.shape[0] // step)
    def _(s):
        dense[pl.ds(s * step, step)] = jnp.zeros((step, *dense.shape[1:]), dense.dtype)

    @pl.loop(0, values.shape[0] // step)
    def _(b):
        for u in range(step):
            block = b * step + u
            pltpu.make_async_copy(values.at[block], dense.at[slots[block]], sem).start()

    pltpu.make_async_copy(values, values, sem).wait()


def scatter_blocks(slots, values, n_slots):
    return pl.pallas_call(
        scatter_kernel,
        out_shape=pltpu.VMEM((n_slots, BS, BS), values.dtype),
        grid_spec=pltpu.PrefetchScalarGridSpec(
            num_scalar_prefetch=1,
            grid=(),
            in_specs=[pl.BlockSpec(memory_space=pltpu.HBM)],
            out_specs=pl.BlockSpec(memory_space=pltpu.VMEM),
            scratch_shapes=[pltpu.SemaphoreType.DMA],
        ),
        compiler_params=pltpu.CompilerParams(vmem_limit_bytes=4 * 2**20),
        cost_estimate=pl.CostEstimate(flops=0, bytes_accessed=24 * 2**20, transcendentals=0),
    )(slots, pltpu.with_memory_space_constraint(values, pltpu.HBM))


def dense_dot(a_ref, x_refs, shards, chunk):
    group = a_ref.shape[1]
    total = None
    for k, x_ref in zip(shards, x_refs):
        lhs = jnp.concatenate(
            [
                jnp.concatenate([a_ref[chunk, r, k * group + c] for c in range(group)], axis=1)
                for r in range(group)
            ],
            axis=0,
        )
        part = jnp.dot(lhs, x_ref[...], preferred_element_type=jnp.float32)
        total = part if total is None else total + part
    return total


def product_kernel(first, shards, a_ref, *refs):
    *in_refs, o_ref = refs
    total = dense_dot(a_ref, in_refs, shards, pl.program_id(0) + first)
    added = in_refs[len(shards) :]
    o_ref[0] = total + added[0][0] if added else total


def quantize(total, o_ref):
    n = total.shape[0] // BS
    width = total.shape[1]
    row = lax.broadcasted_iota(jnp.int32, (8, width), 0)
    tail = jnp.zeros((8, width), jnp.float32)
    for b in range(n):
        part = total[b * BS : (b + 1) * BS]
        top = jnp.maximum(jnp.max(jnp.abs(part), axis=0, keepdims=True), 1e-30)
        step = jnp.ceil(jnp.log(top) * (OCTAVE / math.log(2.0)))
        scaled = part * (jnp.exp(step * (-math.log(2.0) / OCTAVE)) * LEVELS)
        o_ref[b * BS : (b + 1) * BS, :] = jnp.round(scaled).astype(jnp.int32).astype(jnp.int16)
        tail = jnp.where(row == b, jnp.broadcast_to(step, tail.shape), tail)
    o_ref[n * BS :, :] = tail.astype(jnp.int32).astype(jnp.int16)


def dequantize(q_ref):
    n = (q_ref.shape[0] - 8) // BS
    tail = q_ref[n * BS :, :].astype(jnp.int32).astype(jnp.float32)
    parts = []
    for b in range(n):
        scale = jnp.exp(tail[b : b + 1] * (math.log(2.0) / OCTAVE)) * (1.0 / LEVELS)
        parts.append(q_ref[b * BS : (b + 1) * BS, :].astype(jnp.int32).astype(jnp.float32) * scale)
    return jnp.concatenate(parts, axis=0)


def code_kernel(a_ref, b_ref, *o_refs):
    total = a_ref[0] + b_ref[0]
    for j, o_ref in enumerate(o_refs):

        @pl.when(pl.program_id(0) == j)
        def _(o_ref=o_ref):
            if o_ref.dtype == jnp.int16:
                quantize(total, o_ref)
            else:
                o_ref[...] = total


def reduce_kernel(core, *refs):
    *in_refs, s_ref, mine_ref, other_ref, pack = refs
    total = None
    for ref in in_refs:
        term = dequantize(ref) if ref.dtype == jnp.int16 else ref[...]
        total = term if total is None else total + term
    s_ref[...] = total
    gram_store(total, pack)
    half = pack.shape[0] // 2
    c = core[0]
    mine_ref[...] = pack[pl.ds(pl.multiple_of(c * half, 8), half), :]
    other_ref[...] = pack[pl.ds(pl.multiple_of((1 - c) * half, 8), half), :]


def gram_store(total, pack):
    high = total.astype(jnp.bfloat16)
    low = (total - high.astype(jnp.float32)).astype(jnp.bfloat16)
    dims = (((0,), (0,)), ((), ()))
    dot = functools.partial(lax.dot_general, dimension_numbers=dims, preferred_element_type=jnp.float32)
    cross = dot(high, low)
    gram = dot(high, high) + dot(low, low) + cross + cross.T
    row = lax.broadcasted_iota(jnp.int32, (PANEL, PANEL), 0)
    lane = lax.broadcasted_iota(jnp.int32, (PANEL, PANEL), 1)
    second = gram[PANEL:, PANEL:]
    pack[0:PANEL, :] = jnp.where(lane >= row, gram[:PANEL, :PANEL], second)
    pack[PANEL : 2 * PANEL, :] = gram[:PANEL, PANEL:]
    diagonal = jnp.sum(jnp.where(lane == row, second, 0.0), axis=0, keepdims=True)
    pack[2 * PANEL :, :] = jnp.broadcast_to(diagonal, (PACK - 2 * PANEL, PANEL))


def split(x, terms):
    out = []
    for _ in range(terms):
        part = x.astype(jnp.bfloat16)
        out.append(part)
        x = x - part.astype(jnp.float32)
    return out


PAIRS = ((0, 0), (0, 1), (1, 0), (1, 1), (0, 2), (2, 0))


def lane_copy(x, k):
    return jnp.take_along_axis(x, jnp.full(x.shape, k, jnp.int32), axis=1, mode="promise_in_bounds")


def factor(gram):
    n = gram.shape[0]
    eye = lax.broadcasted_iota(jnp.int32, (n, n), 0) == lax.broadcasted_iota(jnp.int32, (n, n), 1)
    picked = jnp.where(eye, gram, 0.0)
    diagonal = jnp.sum(picked, axis=0, keepdims=True)
    inverse_row = lax.rsqrt(diagonal)
    inverse_col = lax.rsqrt(jnp.sum(picked, axis=1, keepdims=True))
    gram = gram * inverse_row * inverse_col

    sub = lax.broadcasted_iota(jnp.int32, (8, n), 0)
    lane = lax.broadcasted_iota(jnp.int32, (8, n), 1)
    left = [gram[8 * i : 8 * i + 8] for i in range(n // 8)]
    right = [(lane == sub + 8 * i).astype(jnp.float32) for i in range(n // 8)]

    def row(x, k):
        return jnp.broadcast_to(x[k : k + 1], x.shape)

    for first in range(0, n // 8, STEP):
        last = first + STEP
        for b in range(first, last):
            cols = {
                t: [lane_copy(left[t], 8 * b + k) for k in range(8)]
                for t in range(b, last)
            }
            spread = {(i, j): row(cols[b][j], i) for j in range(8) for i in range(j, 8)}
            low, root = {}, {}
            for k in range(0, 8, 2):
                p, q, r = spread[k, k], spread[k + 1, k], spread[k + 1, k + 1]
                root[k] = lax.rsqrt(p)
                low[k + 1, k] = q * root[k]
                root[k + 1] = lax.rsqrt(p * r - q * q) * (p * root[k])
                for i in range(k + 2, 8):
                    low[i, k] = spread[i, k] * root[k]
                    low[i, k + 1] = (spread[i, k + 1] - low[i, k] * low[k + 1, k]) * root[k + 1]
                for j in range(k + 2, 8):
                    for i in range(j, 8):
                        spread[i, j] = spread[i, j] - low[i, k] * low[j, k] - low[i, k + 1] * low[j, k + 1]

            def solve(terms):
                done = []
                for k, term in enumerate(terms):
                    for j in range(k):
                        term = term - done[j] * low[k, j]
                    done.append(term * root[k])
                return done

            mult = {t: solve(cols[t]) for t in range(b + 1, last)}
            for side in (left, right):
                tops = solve([row(side[b], k) for k in range(8)])
                side[b] = tops[0]
                for k in range(1, 8):
                    side[b] = jnp.where(sub == k, tops[k], side[b])
                for t in range(b + 1, last):
                    for k in range(8):
                        side[t] = side[t] - mult[t][k] * tops[k]
        if last < n // 8:
            u = split(jnp.concatenate(left[first:last], axis=0), 3)
            v = split(jnp.concatenate(right[first:last], axis=0), 3)
            lhs = jnp.concatenate([u[i] for i, _ in PAIRS], axis=0)
            rhs = jnp.concatenate(
                [jnp.concatenate([u[j] for _, j in PAIRS], axis=0), jnp.concatenate([v[j] for _, j in PAIRS], axis=0)],
                axis=1,
            )
            change = lax.dot_general(lhs, rhs, (((0,), (0,)), ((), ())), preferred_element_type=jnp.float32)
            for t in range(last, n // 8):
                left[t] = left[t] - change[8 * t : 8 * t + 8, :n]
                right[t] = right[t] - change[8 * t : 8 * t + 8, n:]
    upper = jnp.concatenate([jnp.where(lane >= sub + 8 * i, x, 0.0) for i, x in enumerate(left)], axis=0)
    return upper * (diagonal * inverse_row), jnp.concatenate(right, axis=0) * inverse_row


def dot3(a, b, dims):
    (ah, al), (bh, bl) = split(a, 2), split(b, 2)
    dot = functools.partial(
        lax.dot_general, dimension_numbers=(dims, ((), ())), preferred_element_type=jnp.float32
    )
    return dot(ah, bh) + (dot(ah, bl) + dot(al, bh))


def full_dot(a, b, dims):
    (da,), (db,) = dims
    sa, sb = split(a, 3), split(b, 3)
    lhs = jnp.concatenate([sa[i] for i, _ in PAIRS], axis=da)
    rhs = jnp.concatenate([sb[j] for _, j in PAIRS], axis=db)
    return lax.dot_general(lhs, rhs, (dims, ((), ())), preferred_element_type=jnp.float32)


NN, NT, TN = ((1,), (0,)), ((1,), (1,)), ((0,), (0,))


def tail_kernel(scale, core, mine_ref, other_ref, s_ref, basis_ref, upper_ref, pack):
    half = pack.shape[0] // 2
    c = core[0]
    pack[pl.ds(pl.multiple_of(c * half, 8), half), :] = mine_ref[...] * scale
    pack[pl.ds(pl.multiple_of((1 - c) * half, 8), half), :] = other_ref[...] * scale
    row = lax.broadcasted_iota(jnp.int32, (PANEL, PANEL), 0)
    lane = lax.broadcasted_iota(jnp.int32, (PANEL, PANEL), 1)
    both, cross = pack[0:PANEL, :], pack[PANEL : 2 * PANEL, :]
    turned = both.T
    gram_one = jnp.where(lane >= row, both, turned)
    diagonal = jnp.broadcast_to(pack[2 * PANEL : 2 * PANEL + 1, :], both.shape)
    gram_two = jnp.where(lane == row, diagonal, jnp.where(lane < row, both, turned))
    upper_one, low_one = factor(gram_one)
    coupling = full_dot(low_one, cross, NN)
    basis_one = dot3(s_ref[:, 0:PANEL], low_one, NT)
    basis_ref[:, 0:PANEL] = basis_one
    remainder = s_ref[:, PANEL:] - dot3(basis_one, coupling, NN)
    upper_two, low_two = factor(gram_two - full_dot(coupling, coupling, TN))
    upper_ref[0:PANEL, 0:PANEL] = upper_one
    upper_ref[0:PANEL, PANEL:] = coupling
    upper_ref[PANEL:, 0:PANEL] = jnp.zeros_like(upper_one)
    upper_ref[PANEL:, PANEL:] = upper_two
    basis_ref[:, PANEL:] = dot3(remainder, low_two, NT)


def whole(shape):
    return pl.BlockSpec(shape, lambda *_: (0,) * len(shape))


def gather_row(value, ready):
    bits = lax.axis_size("row").bit_length() - 1
    shards = {0: value}
    for bit in reversed(range(bits)):
        for k, v in list(shards.items()):
            if bit == 0 and k:
                v, ready = lax.optimization_barrier((v, ready))
            shards[k | 1 << bit] = exchange(v, "row", 1 << bit)
    return [shards[k] for k in range(2**bits)], ready


def dense_sketch(gaussian_sketch, block_values, local_rows, local_cols, grid_rows, grid_cols):
    size_col = lax.axis_size("col")
    chips = size_col // 2
    shard_rows, width = gaussian_sketch.shape
    group = shard_rows // BS
    me = lax.axis_index("col")
    owner = local_rows // group
    peer_core = (owner + me) % 2
    near = ((owner // 2 ^ me // 2) + chips - 1) % chips
    place = ((1 - peer_core) * chips + near) * group + local_rows % group
    shard = (local_cols // group) ^ lax.axis_index("row")
    slots = place * grid_cols + shard * group + local_cols % group
    dense = scatter_blocks(slots, block_values, grid_rows * grid_cols)
    dense = dense.reshape(2 * chips, group, grid_cols, BS, BS)
    shards, dense = gather_row(gaussian_sketch, dense)
    late = [k for k in range(len(shards)) if k % 2 and k > 1]
    early = [k for k in range(len(shards)) if k not in late]

    params = pltpu.CompilerParams(vmem_limit_bytes=12 * 2**20)
    flops = 2 * shard_rows * grid_cols * BS * width
    bytes_a = 2 * shard_rows * grid_cols * BS

    def cost(n):
        return pl.CostEstimate(flops=n * flops, bytes_accessed=n * bytes_a, transcendentals=0)

    held = pl.BlockSpec(memory_space=pltpu.VMEM)
    r_block = (1, shard_rows, width)
    def block(first):
        return pl.BlockSpec(r_block, lambda i: (i + first, 0, 0))

    def product(first, count, chosen, *added):
        return pl.pallas_call(
            functools.partial(product_kernel, first, chosen),
            grid=(count,),
            in_specs=[held] * (len(chosen) + 1) + [block(first)] * len(added),
            out_specs=block(0),
            out_shape=jax.ShapeDtypeStruct((count, shard_rows, width), jnp.float32),
            compiler_params=params,
            cost_estimate=cost(count),
        )(dense, *[shards[k] for k in chosen], *added)

    first_sum = product(0, 2 * chips, early)
    parts = [(0, chips // 2), (chips // 2, chips - chips // 2)]
    peer = [exchange(product(at, n, late, first_sum), "col", 1) for at, n in parts]
    near = product(chips, chips, late, first_sum)
    sent = jax.ShapeDtypeStruct((shard_rows + 8, width), jnp.int16)
    kept = jax.ShapeDtypeStruct((shard_rows, width), jnp.float32)
    terms = []
    for (at, n), theirs in zip(parts, peer):
        shapes = [kept if at + i == chips - 1 else sent for i in range(n)]
        done = pl.pallas_call(
            code_kernel,
            grid=(n,),
            in_specs=[block(at), block(0)],
            out_specs=[whole(x.shape) for x in shapes],
            out_shape=shapes,
            compiler_params=params,
        )(near, theirs)
        for i, x in enumerate(done):
            terms.append(x if x.dtype == jnp.float32 else exchange(x, "col", 2 * (at + i + 1)))
    return terms


def tile_product(sketch_blocks, block_values, local_rows, local_cols, tile_rows):
    group_size = math.gcd(block_values.shape[0], 64)
    col_width = sketch_blocks.shape[2]

    def advance(counter, summed):
        offset = (counter * group_size).astype(jnp.int32)
        values = lax.dynamic_slice_in_dim(block_values, offset, group_size, 0)
        row_ids = lax.dynamic_slice_in_dim(local_rows, offset, group_size, 0)
        col_ids = lax.dynamic_slice_in_dim(local_cols, offset, group_size, 0)
        picked = jnp.take(sketch_blocks, col_ids, axis=0)
        product = jnp.einsum("gab,gbs->gas", values, picked, preferred_element_type=jnp.float32)
        return summed.at[row_ids].add(product)

    initial = jnp.zeros((tile_rows, block_values.shape[1], col_width), jnp.float32)
    summed = lax.fori_loop(0, block_values.shape[0] // group_size, advance, initial)
    return summed.reshape(tile_rows * block_values.shape[1], col_width)


def looped_sketch(gaussian_sketch, block_values, local_rows, local_cols, grid_rows, grid_cols):
    gathered = lax.all_gather(gaussian_sketch, "row", axis=0, tiled=True)
    sketch_blocks = gathered.reshape(grid_cols, BS, gathered.shape[1])
    partial_value = tile_product(sketch_blocks, block_values, local_rows, local_cols, grid_rows)
    return [lax.psum_scatter(partial_value, "col", scatter_dimension=0, tiled=True)]


def direct_sum(value, axis, low_bit, bits):
    t = [value] + [exchange(value, axis, mask << low_bit) for mask in range(1, 2**bits)]
    if bits == 1:
        return t[0] + t[1]
    if axis == "col":
        return (t[2] + t[3]) + (t[0] + t[1])
    return (t[3] + t[2]) + (t[1] + t[0])


def sum_over_axis(value, axis, low_bit):
    bits = lax.axis_size(axis).bit_length() - 1
    while low_bit < bits:
        take = min(2, bits - low_bit)
        value = direct_sum(value, axis, low_bit, take)
        low_bit += take
    return value


def sum_over_mesh(mine, other, core):
    mine = mine + exchange(other, "col", 1)
    mine = sum_over_axis(mine, "col", 1)
    mine = sum_over_axis(mine, "row", 0)
    return mine, exchange(mine, "col", 1)


def on_device(gaussian_sketch, block_values, block_rows, block_columns):
    size_row = lax.axis_size("row")
    size_col = lax.axis_size("col")
    shard_rows, width = gaussian_sketch.shape
    grid_rows = shard_rows * size_col // BS
    grid_cols = shard_rows * size_row // BS
    local_rows = block_rows - lax.axis_index("row") * grid_rows
    local_cols = block_columns - lax.axis_index("col") * grid_cols
    dense = 2 * grid_rows * grid_cols * BS * BS <= DENSE_BYTES
    sketch = dense_sketch if dense else looped_sketch
    terms = sketch(
        gaussian_sketch, block_values, local_rows, local_cols, grid_rows, grid_cols
    )
    core = lax.axis_index("col") % 2
    half = jax.ShapeDtypeStruct((PACK // 2, PANEL), jnp.float32)
    sketched, mine, other = pl.pallas_call(
        reduce_kernel,
        grid_spec=pltpu.PrefetchScalarGridSpec(
            num_scalar_prefetch=1,
            grid=(1,),
            in_specs=[whole(t.shape) for t in terms],
            out_specs=[whole((shard_rows, width)), whole(half.shape), whole(half.shape)],
            scratch_shapes=[pltpu.VMEM((PACK, PANEL), jnp.float32)],
        ),
        out_shape=[jax.ShapeDtypeStruct((shard_rows, width), jnp.float32), half, half],
        compiler_params=pltpu.CompilerParams(vmem_limit_bytes=12 * 2**20),
    )(core.reshape(1), *terms)
    order_total = shard_rows * size_row * size_col
    mine, other = sum_over_mesh(mine, other, core)
    range_basis, upper_factor = pl.pallas_call(
        functools.partial(tail_kernel, 1.0 / order_total),
        grid_spec=pltpu.PrefetchScalarGridSpec(
            num_scalar_prefetch=1,
            grid=(1,),
            in_specs=[whole(half.shape), whole(half.shape), whole(sketched.shape)],
            out_specs=[whole(sketched.shape), whole((width, width))],
            scratch_shapes=[pltpu.VMEM((PACK, PANEL), jnp.float32)],
        ),
        out_shape=[
            jax.ShapeDtypeStruct(sketched.shape, jnp.float32),
            jax.ShapeDtypeStruct((width, width), jnp.float32),
        ],
        compiler_params=pltpu.CompilerParams(vmem_limit_bytes=16 * 2**20),
    )(core.reshape(1), mine, other, sketched)
    return (range_basis, upper_factor)


def solution(mesh):
    return jax.shard_map(
        on_device,
        mesh=mesh,
        in_specs=(
            P(("col", "row"), None),
            P(("row", "col"), None, None),
            P(("row", "col")),
            P(("row", "col")),
        ),
        out_specs=(P(("row", "col"), None), P()),
        check_vma=False,
    )
```
